256 devices in a mesh: seq: 16 (over y, x), head: 8 (over z), dp: 2 (over core).
Axes of the slice: x: 4, y: 4, z: 8, core: 2. Of those that a mesh axis runs over, the one named last changes fastest.
Arguments:
- query_heads: bfloat16 [2, 4096, 4096], P('dp', 'seq', 'head'), may hold values from -100 to 100
- key_heads: bfloat16 [2, 4096, 4096], P('dp', 'seq', 'head'), may hold values from -100 to 100
- value_heads: bfloat16 [2, 4096, 4096], P('dp', 'seq', 'head'), may hold values from -6 to 6
- query_gain: float32 [4096], P('head'), may hold values from 0.5 to 1.5
- key_gain: float32 [4096], P('head'), may hold values from 0.5 to 1.5
- key_squeeze: bfloat16 [32, 512, 128], P('head'), may hold values from -0.25 to 0.25
- value_squeeze: bfloat16 [32, 512, 128], P('head'), may hold values from -0.25 to 0.25
- grad_out: bfloat16 [2, 4096, 4096], P('dp', 'seq', 'head'), may hold values from -6 to 6
Outputs:
- grad_query: bfloat16 [2, 4096, 4096], P('dp', 'seq', 'head')
- grad_key: bfloat16 [2, 4096, 4096], P('dp', 'seq', 'head')
- grad_value: bfloat16 [2, 4096, 4096], P('dp', 'seq', 'head')
- grad_query_gain: float32 [4096], P('head')
- grad_key_gain: float32 [4096], P('head')
- grad_key_squeeze: float32 [32, 512, 128], P('head')
- grad_value_squeeze: float32 [32, 512, 128], P('head')
The draws below stay inside these ranges and needn't reach their ends.
All inputs are finite; a program needn't handle non-finite values.
Results may differ from the reference program's by a relative error of at most 0.025.
Values may be sent and summed in bfloat16 or wider, within the bound.
A program may use at most 64 MiB of HBM per device.

```python
import jax
import jax.numpy as jnp
from jax import lax

H = 32
HD = 128
KS = 4
S_DEV = 256
HH = 4096
L = 4096
BATCH = 2
SLOTS = 64
NMEM = 1024
N_SEQ = 16


def drawn_pair(key):
    base = jax.random.fold_in(key, 811)
    streams = jax.random.split(base, 12)
    columns = jnp.arange(HH)
    rise = 3.0
    tilt = rise ** (columns / (HH - 1.0)) / jnp.sqrt(rise)

    def scaled(first, second, third):
        noise = jax.random.truncated_normal(streams[first], -3.0, 3.0, (BATCH, L, HH), jnp.float32)
        row_scale = jnp.exp(jax.random.uniform(streams[second], (BATCH, L, 1), jnp.float32, jnp.log(0.3), jnp.log(3.0)))
        col_scale = jnp.exp(jax.random.uniform(streams[third], (HH,), jnp.float32, jnp.log(0.3), jnp.log(3.0)))
        return (noise, noise * row_scale * col_scale * tilt)
    noise_q, queries = scaled(0, 1, 2)
    noise_k, keyset = scaled(3, 4, 5)
    return (queries, keyset)


def draw_query_heads(key, part):
    return drawn_pair(key)[0].astype(jnp.bfloat16)


def draw_key_heads(key, part):
    return drawn_pair(key)[1].astype(jnp.bfloat16)


def shard_levels(rng, shape, cuts, low, largest):
    level = 1.0
    for dim, shards_of in cuts:
        heights = jax.random.uniform(jax.random.fold_in(jax.random.fold_in(rng, 6), dim), (shards_of,), jnp.float32, low / len(cuts), largest / len(cuts))
        level = level * jnp.repeat(jnp.exp(heights), shape[dim] // shards_of).reshape((-1,) + (1,) * (len(shape) - 1 - dim))
    return level


def scatter_about(own_key, dims, spread, limit, cuts=(), kind=jnp.bfloat16):
    result = jax.random.normal(own_key, dims, jnp.float32) * spread
    if len(cuts) > 0:
        result = shard_levels(own_key, dims, cuts, -0.22, 0.18) * result
    return jnp.clip(result, min=-limit, max=limit).astype(kind)


def setup_inputs(seed: int = 0) -> dict:
    key_list = jax.random.split(jax.random.key(seed), 9)
    return {
        "query_heads": draw_query_heads(jax.random.fold_in(key_list[8], 71), 0),
        "key_heads": draw_key_heads(jax.random.fold_in(key_list[8], 71), 0),
        "value_heads": scatter_about(key_list[2], (BATCH, L, HH), 1.0, 6.0, ((0, 2), (1, 16), (2, 8))),
        "query_gain": jnp.clip(1.0 + 0.1 * jax.random.normal(key_list[3], (HH,), jnp.float32), 0.5, 1.5),
        "key_gain": jnp.clip(1.0 + 0.1 * jax.random.normal(key_list[4], (HH,), jnp.float32), 0.5, 1.5),
        "key_squeeze": scatter_about(key_list[5], (H, KS * HD, HD), (KS * HD) ** -0.5, 0.25, ((0, 8),)),
        "value_squeeze": scatter_about(key_list[6], (H, KS * HD, HD), (KS * HD) ** -0.5, 0.25, ((0, 8),)),
        "grad_out": scatter_about(key_list[7], (BATCH, L, HH), 1.0, 6.0, ((0, 2), (1, 16), (2, 8))),
    }


EPSILON = 1e-06

def to_half(source):
    return lax.optimization_barrier(source.astype(jnp.bfloat16)).astype(jnp.float32)

def normalize(source, gain):
    full = source.astype(jnp.float32)
    inverse = lax.rsqrt(lax.optimization_barrier(jnp.sum(full * full, -1, keepdims=True)) / HH + EPSILON)
    return (full, inverse, (full * inverse * gain).astype(jnp.bfloat16))

def unfold_slots(source):
    return source.reshape(BATCH, NMEM, KS, H, HD).transpose(0, 1, 3, 2, 4).reshape(BATCH, NMEM, H, KS * HD)

def fold_slots(source):
    return source.reshape(BATCH, NMEM, H, KS, HD).transpose(0, 1, 3, 2, 4).reshape(BATCH, L, HH)

def compress(unfolded, weight):
    return jnp.einsum('bmhc,hcd->bmhd', unfolded.astype(jnp.float32), weight.astype(jnp.float32)).astype(jnp.bfloat16)

def sequence_grads(queries, key_rows, value_rows, cotangent, mem_keys, mem_values):
    score_scale = HD ** (-0.5)
    positions = jnp.arange(S_DEV, dtype=jnp.int32)
    causal = positions[:, None] >= positions[None, :]
    slot_ids = jnp.arange(NMEM, dtype=jnp.int32)
    keys_mem = mem_keys.astype(jnp.float32)
    values_mem = mem_values.astype(jnp.float32)

    def shard_step(carry, index):
        first_row = index * S_DEV
        query_blk = lax.dynamic_slice_in_dim(queries, first_row, S_DEV, 0).astype(jnp.float32)
        key_blk = lax.dynamic_slice_in_dim(key_rows, first_row, S_DEV, 0).astype(jnp.float32)
        value_blk = lax.dynamic_slice_in_dim(value_rows, first_row, S_DEV, 0).astype(jnp.float32)
        grad_blk = lax.dynamic_slice_in_dim(cotangent, first_row, S_DEV, 0).astype(jnp.float32)
        keys_all = jnp.concatenate([key_blk, keys_mem], 0)
        values_all = jnp.concatenate([value_blk, values_mem], 0)
        scores = jnp.einsum('thd,uhd->htu', query_blk, keys_all) * score_scale
        earlier = jnp.broadcast_to(slot_ids[None, :] < index * SLOTS, (S_DEV, NMEM))
        allowed = jnp.concatenate([causal, earlier], 1)
        scores = jnp.where(allowed[None], scores, -jnp.inf)
        peak = lax.optimization_barrier(jnp.max(scores, -1, keepdims=True))
        log_mass = peak + jnp.log(lax.optimization_barrier(jnp.sum(jnp.exp(scores - peak), -1, keepdims=True)))
        attend = jnp.exp(scores - log_mass)
        grads = jnp.einsum('thd,uhd->htu', grad_blk, values_all)
        row_delta = lax.optimization_barrier(jnp.sum(attend * grads, -1, keepdims=True))
        d_scores = to_half(attend * (grads - row_delta))
        grad_q = score_scale * jnp.einsum('htu,uhd->thd', d_scores, keys_all)
        grad_keys = score_scale * jnp.einsum('htu,thd->uhd', d_scores, query_blk)
        grad_values = jnp.einsum('htu,thd->uhd', to_half(attend), grad_blk)
        sum_k, sum_v = carry
        carry = (sum_k + to_half(grad_keys[S_DEV:]), sum_v + to_half(grad_values[S_DEV:]))
        return (carry, (grad_q, grad_keys[:S_DEV], grad_values[:S_DEV]))
    zeros = jnp.zeros((NMEM, H, HD), jnp.float32)
    sums, per_shard = lax.scan(shard_step, (zeros, zeros), jnp.arange(N_SEQ, dtype=jnp.int32))
    flat = tuple((stacked.reshape(L, HH) for stacked in per_shard))
    return (sums, flat)

def reference(query_heads, key_heads, value_heads, query_gain, key_gain, key_squeeze, value_squeeze, grad_out):
    q_full, inv_q, q_norm = normalize(query_heads, query_gain)
    k_full, inv_k, k_norm = normalize(key_heads, key_gain)
    k_unf = unfold_slots(k_norm)
    v_unf = unfold_slots(value_heads)
    mem_k = compress(k_unf, key_squeeze)
    mem_v = compress(v_unf, value_squeeze)
    results = []
    for member in range(BATCH):
        results.append(sequence_grads(q_norm[member].reshape(L, H, HD), k_norm[member].reshape(L, H, HD), value_heads[member].reshape(L, H, HD), grad_out[member].reshape(L, H, HD), mem_k[member], mem_v[member]))
    grad_mem_k = jnp.stack([item[0][0] for item in results]).astype(jnp.bfloat16)
    grad_mem_v = jnp.stack([item[0][1] for item in results]).astype(jnp.bfloat16)
    grad_qn = jnp.stack([item[1][0] for item in results])
    grad_kn_local = jnp.stack([item[1][1] for item in results])
    grad_v_local = jnp.stack([item[1][2] for item in results])
    grad_key_squeeze = jnp.einsum('bmhc,bmhd->hcd', k_unf.astype(jnp.float32), grad_mem_k.astype(jnp.float32))
    grad_value_squeeze = jnp.einsum('bmhc,bmhd->hcd', v_unf.astype(jnp.float32), grad_mem_v.astype(jnp.float32))
    back_k = fold_slots(jnp.einsum('bmhd,hcd->bmhc', grad_mem_k.astype(jnp.float32), key_squeeze.astype(jnp.float32)))
    back_v = fold_slots(jnp.einsum('bmhd,hcd->bmhc', grad_mem_v.astype(jnp.float32), value_squeeze.astype(jnp.float32)))
    grad_kn = grad_kn_local + back_k
    grad_value = (grad_v_local + back_v).astype(jnp.bfloat16)
    grad_query_gain = lax.optimization_barrier(jnp.sum(grad_qn * q_full * inv_q, (0, 1)))
    grad_key_gain = lax.optimization_barrier(jnp.sum(grad_kn * k_full * inv_k, (0, 1)))
    dot_q = lax.optimization_barrier(jnp.sum(query_gain * grad_qn * q_full, -1, keepdims=True))
    dot_k = lax.optimization_barrier(jnp.sum(key_gain * grad_kn * k_full, -1, keepdims=True))
    grad_query = (inv_q * query_gain * grad_qn - q_full * inv_q ** 3 * dot_q / HH).astype(jnp.bfloat16)
    grad_key = (inv_k * key_gain * grad_kn - k_full * inv_k ** 3 * dot_k / HH).astype(jnp.bfloat16)
    return (grad_query, grad_key, grad_value, grad_query_gain, grad_key_gain, grad_key_squeeze, grad_value_squeeze)
```

```python
import functools

import jax
import jax.numpy as jnp
from jax import lax
from jax.experimental import pallas as pl
from jax.experimental.pallas import tpu as pltpu
from jax.sharding import PartitionSpec as P

HD = 128
KS = 4
N = 4
T = 256
M = 64
EPS = 1e-06
NEG = -1e30
MESH = pl.DeviceIdType.MESH
F32 = jnp.float32
BF16 = jnp.bfloat16
PIECE = 144

A2A = 0
Z1 = A2A + 12
Y1 = Z1 + 7
MEM = Y1 + 3
DMEM = MEM + 6
DQ = DMEM + 24
DK = DQ + 3
DV = DK + 3
PD = DV + 3
Z2 = PD + 3
C1 = Z2 + 7
RS = C1 + 1
AGX = RS + 3
AGY = AGX + 3
C2 = AGY + 3
N_SEM = C2 + 4


def dot_nt(a, b):
    return lax.dot_general(a, b, (((1,), (1,)), ((), ())), preferred_element_type=F32)


def dot_tn(a, b):
    return lax.dot_general(a, b, (((0,), (0,)), ((), ())), preferred_element_type=F32)


def dot_nn(a, b):
    return lax.dot_general(a, b, (((1,), (0,)), ((), ())), preferred_element_type=F32)


def as_column(row):
    return jnp.transpose(jnp.broadcast_to(row, (HD, row.shape[1])))


def row_sum(block):
    return jnp.sum(jnp.transpose(block), 0, keepdims=True)


def fold8(block):
    return block.reshape(block.shape[0] // 8, 8, block.shape[1])


def kernel(
    nz,
    q_ref, k_ref, v_ref, o_ref, gq_ref, gk_ref, wk_ref, wv_ref,
    dq_out, dk_out, dv_out, qg_out, kg_out, sk_out, sv_out,
    hq, hk, hv, ho, qn, kn, icq, ick, fs, ku, vu, zs, ys, mk, mv,
    s_all, g_all, d_buf, p_buf, dmk, dmv, sbk, sbv, rbk, rbv,
    dkl, dvl, aq, ak, av, pd, aqh, akh, avh, pdh, zs2,
    pay, pin, rsb, rsi, full,
    ss, rs, loc,
):
    seq = lax.axis_index("seq")
    x = lax.rem(seq, N)
    y = lax.div(seq, N)
    z = lax.axis_index("head")
    c = lax.axis_index("dp")
    hh = nz * N * HD
    scale = HD ** (-0.5)

    def ydev(r):
        return {"seq": lax.rem(y + r, N) * N + x}

    def xdev(r):
        return {"seq": y * N + lax.rem(x + r, N)}

    def zdev(r):
        return {"head": lax.rem(z + r, nz)}

    cdev = {"dp": 1 - c}

    def remote(src, dst, index, device):
        return pltpu.make_async_remote_copy(
            src_ref=src,
            dst_ref=dst,
            send_sem=ss.at[index],
            recv_sem=rs.at[index],
            device_id=device,
            device_id_type=MESH,
        )

    sent = []

    def start(copy):
        copy.start()
        sent.append(copy)
        return copy

    barrier = pltpu.get_barrier_semaphore()
    peers = [ydev(r) for r in (1, 2, 3)] + [xdev(r) for r in (1, 2, 3)]
    peers += [zdev(r) for r in range(1, nz)] + [cdev]
    for peer in peers:
        pl.semaphore_signal(barrier, inc=1, device_id=peer, device_id_type=MESH)

    for row, ref in ((0, q_ref), (1, k_ref)):
        full_rows = ref[...].astype(F32)
        squares = full_rows * full_rows
        folded = squares[:, :HD]
        for h in range(1, N):
            folded = folded + squares[:, h * HD : (h + 1) * HD]
        zs[z, row : row + 1, :] = row_sum(folded)

    pl.semaphore_wait(barrier, len(peers))

    z1 = [start(remote(zs.at[z], zs.at[z], Z1 + r - 1, zdev(r))) for r in range(1, nz)]
    rows_mine = pl.ds(pl.multiple_of(y * T, T), T)
    a2a = []
    own = []
    for i, (src, dst) in enumerate(((v_ref, hv), (k_ref, hk), (q_ref, hq), (o_ref, ho))):
        group = []
        for r in (1, 3, 2):
            cols = pl.ds(pl.multiple_of(lax.rem(y + r, N) * HD, HD), HD)
            group.append(
                start(remote(src.at[:, cols], dst.at[rows_mine, :], A2A + 3 * i + r - 1, ydev(r)))
            )
        a2a.append(group)
        cols = pl.ds(pl.multiple_of(y * HD, HD), HD)
        copy = pltpu.make_async_copy(src.at[:, cols], dst.at[rows_mine, :], loc.at[i])
        copy.start()
        own.append(copy)

    def arrived(i):
        for copy in a2a[i]:
            copy.wait_recv()
        own[i].wait()

    for copy in z1:
        copy.wait_recv()
    total = zs[0]
    for r in range(1, nz):
        total = total + zs[r]
    ys[y] = total
    y1 = [start(remote(ys.at[y], ys.at[y], Y1 + r - 1, ydev(r))) for r in (1, 3, 2)]

    def unfold(dst):
        for j in range(KS):
            dst[:, j * HD : (j + 1) * HD] = fs[pl.ds(j, N * M, stride=KS), :].astype(BF16)

    def spread(mem, value, index):
        rounded = value.astype(BF16)
        for b in range(N):
            mem[b, x] = rounded[b * M : (b + 1) * M]
        return [
            start(remote(mem.at[:, x], mem.at[:, x], MEM + 3 * index + r - 1, xdev(r)))
            for r in (1, 3, 2)
        ]

    arrived(0)
    fs[...] = hv[...].astype(F32)
    unfold(vu)
    mem_copies = spread(mv, dot_nn(vu[...], wv_ref[y]), 1)

    for copy in y1:
        copy.wait_recv()
    gain_q = gq_ref[y]
    gain_k = gk_ref[y]
    arrived(1)
    for a in range(N):
        rows = slice(a * T, (a + 1) * T)
        inverse = lax.rsqrt(ys[a] * (1.0 / hh) + EPS)
        icq[rows, :] = as_column(inverse[0:1])
        ick[rows, :] = as_column(inverse[1:2])
        normed = (hk[rows, :].astype(F32) * ick[rows, :] * gain_k).astype(BF16)
        kn[rows, :] = normed
        fs[rows, :] = normed.astype(F32)
    unfold(ku)
    mem_copies += spread(mk, dot_nn(ku[...], wk_ref[y]), 0)

    arrived(2)
    arrived(3)
    key_at = lax.broadcasted_iota(jnp.int32, (T, T), 0)
    query_at = lax.broadcasted_iota(jnp.int32, (T, T), 1)
    peaks = []
    for a in range(N):
        rows = slice(a * T, (a + 1) * T)
        normed = (hq[rows, :].astype(F32) * icq[rows, :] * gain_q).astype(BF16)
        qn[rows, :] = normed
        scores = jnp.where(key_at <= query_at, dot_nt(kn[rows, :], normed), NEG)
        s_all[a, 0:T, :] = scores
        g_all[a, 0:T, :] = dot_nt(hv[rows, :], ho[rows, :])
        peaks.append(jnp.max(fold8(scores), 0))

    for copy in mem_copies:
        copy.wait_recv()

    gain_q_sum = jnp.zeros((8, HD), F32)
    dmem_copies = []
    for a in range(N - 1, -1, -1):
        rows = slice(a * T, (a + 1) * T)
        width = T * (a + 2)
        q_rows = qn[rows, :]
        o_rows = ho[rows, :]
        peak8 = peaks[a]
        for b in range(a + 1):
            scores = dot_nt(mk[b].reshape(T, HD), q_rows)
            if b == a:
                scores = jnp.where(key_at < x * M, scores, NEG)
            at = slice(T * (b + 1), T * (b + 2))
            s_all[a, at, :] = scores
            peak8 = jnp.maximum(peak8, jnp.max(fold8(scores), 0))
            g_all[a, at, :] = dot_nt(mv[b].reshape(T, HD), o_rows)
        peak = jnp.max(peak8, 0, keepdims=True)

        def lift(i, state, a=a, peak=peak):
            mass8, weighted8 = state
            at = pl.ds(pl.multiple_of(i * 64, 64), 64)
            lifted = jnp.exp((s_all[a, at, :] - peak) * scale)
            s_all[a, at, :] = lifted
            mass8 = mass8 + jnp.sum(fold8(lifted), 0)
            weighted8 = weighted8 + jnp.sum(fold8(lifted * g_all[a, at, :]), 0)
            return mass8, weighted8

        none = jnp.zeros((8, T), F32)
        mass8, weighted8 = lax.fori_loop(0, width // 64, lift, (none, none))
        inverse_mass = 1.0 / jnp.sum(mass8, 0, keepdims=True)
        row_delta = jnp.sum(weighted8, 0, keepdims=True) * inverse_mass

        def settle(i, state, a=a, inverse_mass=inverse_mass, row_delta=row_delta):
            at = pl.ds(pl.multiple_of(i * 64, 64), 64)
            attend = s_all[a, at, :] * inverse_mass
            p_buf[at, :] = attend.astype(BF16)
            d_buf[at, :] = (attend * (g_all[a, at, :] - row_delta)).astype(BF16)
            return state

        lax.fori_loop(0, width // 64, settle, 0)

        for b in range(a, -1, -1):
            at = slice(T * (b + 1), T * (b + 2))
            add_k = dot_nn(d_buf[at, :], q_rows)
            add_v = dot_nn(p_buf[at, :], o_rows)
            if a < N - 1:
                add_k = add_k + dmk[b * T : (b + 1) * T, :]
                add_v = add_v + dmv[b * T : (b + 1) * T, :]
            if b == a:
                sbk[a] = (add_k * scale).astype(BF16).reshape(N, M, HD)
                sbv[a] = add_v.astype(BF16).reshape(N, M, HD)
                for i, (sb, rb) in enumerate(((sbk, rbk), (sbv, rbv))):
                    for r in (1, 3, 2):
                        to = lax.rem(x + r, N)
                        index = DMEM + 12 * i + 3 * a + r - 1
                        dmem_copies.append(
                            start(remote(sb.at[a, to], rb.at[x, a], index, xdev(r)))
                        )
            else:
                dmk[b * T : (b + 1) * T, :] = add_k
                dmv[b * T : (b + 1) * T, :] = add_v
        grad_q = dot_tn(d_buf[0:T, :], kn[rows, :])
        for b in range(a + 1):
            at = slice(T * (b + 1), T * (b + 2))
            grad_q = grad_q + dot_tn(d_buf[at, :], mk[b].reshape(T, HD))
        grad_q = grad_q * scale
        dkl[rows, :] = dot_nn(d_buf[0:T, :], q_rows) * scale
        dvl[rows, :] = dot_nn(p_buf[0:T, :], o_rows)
        q_full = hq[rows, :].astype(F32)
        inv = icq[rows, :]
        gain_q_sum = gain_q_sum + jnp.sum(fold8(grad_q * q_full * inv), 0)
        gained = grad_q * gain_q
        aq[a] = (gained * inv).astype(BF16)
        pd[a, 0:1, :] = row_sum(gained * q_full)

    def homeward(src, dst, base):
        dst[y] = src[y]
        return [
            start(remote(src.at[lax.rem(y + r, N)], dst.at[y], base + r - 1, ydev(r)))
            for r in (1, 3, 2)
        ]

    home = homeward(aq, aqh, DQ)

    for copy in dmem_copies:
        copy.wait_recv()
    grad_mem_k = []
    grad_mem_v = []
    for out, sb, rb in ((grad_mem_k, sbk, rbk), (grad_mem_v, sbv, rbv)):
        for b in range(N):
            total = sb[b, x].astype(F32)
            for r in (1, 2, 3):
                total = total + rb[lax.rem(x + r, N), b].astype(F32)
            out.append(total.astype(BF16))
    grad_mem_k = jnp.concatenate(grad_mem_k, 0)
    grad_mem_v = jnp.concatenate(grad_mem_v, 0)

    square_k = dot_tn(ku[...], grad_mem_k)
    square_v = dot_tn(vu[...], grad_mem_v)
    for p in range(N):
        pay[0, p, 0:HD, :] = square_k[p * HD : (p + 1) * HD].astype(BF16)
        pay[1, p, 0:HD, :] = square_v[p * HD : (p + 1) * HD].astype(BF16)
    for j in range(KS):
        at = pl.ds(j, N * M, stride=KS)
        cols = slice(j * HD, (j + 1) * HD)
        dkl[at, :] = dkl[at, :] + dot_nt(grad_mem_k, wk_ref[y, cols, :])
        dvl[at, :] = dvl[at, :] + dot_nt(grad_mem_v, wv_ref[y, cols, :])
    gain_k_sum = jnp.zeros((8, HD), F32)
    for a in range(N):
        rows = slice(a * T, (a + 1) * T)
        av[a] = dvl[rows, :].astype(BF16)
        grad_k = dkl[rows, :]
        k_full = hk[rows, :].astype(F32)
        inv = ick[rows, :]
        gain_k_sum = gain_k_sum + jnp.sum(fold8(grad_k * k_full * inv), 0)
        gained = grad_k * gain_k
        ak[a] = (gained * inv).astype(BF16)
        pd[a, 1:2, :] = row_sum(gained * k_full)
    tail = PIECE - HD
    tail_k = jnp.broadcast_to(jnp.sum(gain_k_sum, 0, keepdims=True), (tail, HD)).astype(BF16)
    tail_q = jnp.broadcast_to(jnp.sum(gain_q_sum, 0, keepdims=True), (tail, HD)).astype(BF16)
    for p in range(N):
        pay[0, p, HD:PIECE, :] = tail_k
        pay[1, p, HD:PIECE, :] = tail_q

    c1 = start(remote(pay.at[1 - c], pin, C1, cdev))
    home_pd = homeward(pd, pdh, PD)
    home += homeward(ak, akh, DK)
    home += homeward(av, avh, DV)

    c1.wait_recv()
    for p in range(N):
        rsb[p] = (pay[c, p].astype(F32) + pin[p].astype(F32)).astype(BF16)
    rs_copies = [
        start(remote(rsb.at[lax.rem(x + r, N)], rsi.at[x], RS + r - 1, xdev(r)))
        for r in (1, 3, 2)
    ]

    for copy in home_pd:
        copy.wait_recv()
    total = pdh[0]
    for h in range(1, N):
        total = total + pdh[h]
    zs2[z] = total
    z2 = [start(remote(zs2.at[z], zs2.at[z], Z2 + r - 1, zdev(r))) for r in range(1, nz)]

    for copy in rs_copies:
        copy.wait_recv()
    total = rsb[x].astype(F32)
    for r in (1, 2, 3):
        total = total + rsi[lax.rem(x + r, N)].astype(F32)
    full[c, y, x] = total.astype(BF16)
    agx = [
        start(remote(full.at[c, y, x], full.at[c, y, x], AGX + r - 1, xdev(r))) for r in (1, 3, 2)
    ]
    for copy in agx:
        copy.wait_recv()
    agy = [start(remote(full.at[c, y], full.at[c, y], AGY + r - 1, ydev(r))) for r in (1, 3, 2)]
    c2 = [start(remote(full.at[c, y], full.at[c, y], C2, cdev))]

    for copy in z2:
        copy.wait_recv()
    total = zs2[0]
    for r in range(1, nz):
        total = total + zs2[r]
    inverse = lax.rsqrt(ys[y] * (1.0 / hh) + EPS)
    shift = inverse * inverse * inverse * total * (1.0 / hh)
    shift_q = as_column(shift[0:1])
    shift_k = as_column(shift[1:2])
    for copy in home:
        copy.wait_recv()
    for h in range(N):
        cols = slice(h * HD, (h + 1) * HD)
        dq_out[:, cols] = (aqh[h].astype(F32) - q_ref[:, cols].astype(F32) * shift_q).astype(BF16)
        dk_out[:, cols] = (akh[h].astype(F32) - k_ref[:, cols].astype(F32) * shift_k).astype(BF16)
        dv_out[:, cols] = avh[h]

    for i, r in enumerate((1, 3, 2)):
        agy[i].wait_recv()
        at = full.at[c, lax.rem(y + N - r, N)]
        c2.append(start(remote(at, at, C2 + i + 1, cdev)))
    for copy in c2:
        copy.wait_recv()
    for h in range(N):
        for p in range(N):
            rows = slice(p * HD, (p + 1) * HD)
            sk_out[h, rows, :] = full[0, h, p, 0:HD, :].astype(F32)
            sv_out[h, rows, :] = full[1, h, p, 0:HD, :].astype(F32)
        kg_out[h] = full[0, h, 0, HD:PIECE, :].astype(F32)[0:1]
        qg_out[h] = full[1, h, 0, HD:PIECE, :].astype(F32)[0:1]

    for copy in sent:
        copy.wait_send()


def on_device(nz, q, k, v, query_gain, key_gain, key_squeeze, value_squeeze, o):
    width = N * HD
    bf = functools.partial(pltpu.VMEM, dtype=BF16)
    ff = functools.partial(pltpu.VMEM, dtype=F32)
    rows = N * T
    scratch = [bf((rows, HD))] * 4 + [bf((rows, HD))] * 2 + [ff((rows, HD))] * 2
    scratch += [ff((rows, HD)), bf((N * M, KS * HD)), bf((N * M, KS * HD))]
    scratch += [ff((nz, 2, T)), ff((N, 2, T)), bf((N, N, M, HD)), bf((N, N, M, HD))]
    deep = (N + 1) * T
    scratch += [ff((N, deep, T)), ff((N, deep, T)), bf((deep, T)), bf((deep, T))]
    scratch += [ff((N * T, HD))] * 2 + [bf((N, N, M, HD))] * 4
    scratch += [ff((rows, HD))] * 2 + [bf((N, T, HD))] * 3 + [ff((N, 2, T))]
    scratch += [bf((N, T, HD))] * 3 + [ff((N, 2, T)), ff((nz, 2, T))]
    scratch += [bf((2, N, PIECE, HD)), bf((N, PIECE, HD)), bf((N, PIECE, HD))]
    scratch += [bf((N, PIECE, HD)), bf((2, N, N, PIECE, HD))]
    scratch += [
        pltpu.SemaphoreType.DMA((N_SEM,)),
        pltpu.SemaphoreType.DMA((N_SEM,)),
        pltpu.SemaphoreType.DMA((4,)),
    ]
    vmem = pl.BlockSpec(memory_space=pltpu.VMEM)
    outs = pl.pallas_call(
        functools.partial(kernel, nz),
        out_shape=[jax.ShapeDtypeStruct((T, width), BF16)] * 3
        + [jax.ShapeDtypeStruct((N, 1, HD), F32)] * 2
        + [jax.ShapeDtypeStruct((N, KS * HD, HD), F32)] * 2,
        in_specs=[vmem] * 8,
        out_specs=[vmem] * 7,
        scratch_shapes=scratch,
        compiler_params=pltpu.CompilerParams(
            collective_id=0, has_side_effects=True, vmem_limit_bytes=60 * 2**20
        ),
    )(
        q[0], k[0], v[0], o[0],
        query_gain.reshape(N, 1, HD), key_gain.reshape(N, 1, HD),
        key_squeeze, value_squeeze,
    )
    dq, dk, dv, qg, kg, sk, sv = outs
    return dq[None], dk[None], dv[None], qg.reshape(width), kg.reshape(width), sk, sv


def solution(mesh):
    by_token = P("dp", "seq", "head")
    by_head = P("head", None, None)
    return jax.shard_map(
        functools.partial(on_device, mesh.shape["head"]),
        mesh=mesh,
        in_specs=(by_token,) * 3 + (P("head"), P("head"), by_head, by_head, by_token),
        out_specs=(by_token,) * 3 + (P("head"), P("head"), by_head, by_head),
        check_vma=False,
    )
```

```python
import functools

import jax
import jax.numpy as jnp
from jax import lax
from jax.experimental import pallas as pl
from jax.experimental.pallas import tpu as pltpu
from jax.sharding import PartitionSpec as P

HD = 128
KS = 4
N = 4
T = 256
M = 64
EPS = 1e-06
NEG = -1e30
MESH = pl.DeviceIdType.MESH
F32 = jnp.float32
BF16 = jnp.bfloat16
PIECE = 144

A2A = 0
Z1 = A2A + 12
G1 = Z1 + 7
MEM = G1 + 3
DMEM = MEM + 6
DMEM1 = DMEM + 24
DQ = DMEM1 + 8
DK = DQ + 3
DV = DK + 3
PD = DV + 3
Z2 = PD + 3
RS = Z2 + 7
RSX = RS + 3
AGG = RSX + 4
AGO = AGG + 3
C2 = AGO + 3
N_SEM = C2 + 4


def dot_nt(a, b):
    return lax.dot_general(a, b, (((1,), (1,)), ((), ())), preferred_element_type=F32)


def dot_tn(a, b):
    return lax.dot_general(a, b, (((0,), (0,)), ((), ())), preferred_element_type=F32)


def dot_nn(a, b):
    return lax.dot_general(a, b, (((1,), (0,)), ((), ())), preferred_element_type=F32)


def as_column(row):
    return jnp.transpose(jnp.broadcast_to(row, (HD, row.shape[1])))


def row_sum(block):
    return jnp.sum(jnp.transpose(block), 0, keepdims=True)


def fold8(block):
    return block.reshape(block.shape[0] // 8, 8, block.shape[1])


def kernel(
    nz,
    q_hbm, k_hbm, v_hbm, o_hbm, gq_ref, gk_ref, wk_hbm, wv_hbm,
    dq_out, dk_out, dv_out, full_out,
    q_ref, k_ref, v_ref, o_ref, wk_ref, wv_ref,
    hq, hk, hv, ho, qn, kn, icq, ick, fs, ku, vu, zs, gs, mkg, mvg, mkc, mvc,
    s_all, g_all, d_all, p_all, acc_k, acc_v, sbk, sbv, rbk, rbv,
    dkl, dvl, aq, ak, av, pd, aqh, akh, avh, pdh, zs2,
    pay, rsi, full,
    ss, rs, loc,
):
    seq = lax.axis_index("seq")
    x = lax.rem(seq, N)
    y = lax.div(seq, N)
    z = lax.axis_index("head")
    c = lax.axis_index("dp")
    i = y + c * (x - y)
    j = x + c * (y - x)
    hh = nz * N * HD
    scale = HD ** (-0.5)
    first_core = c == 0

    def place(core, along, across):
        return along * (N - (N - 1) * core) + across * (1 + (N - 1) * core)

    def gdev(r):
        return {"seq": place(c, lax.rem(i + r, N), j)}

    def odev(r):
        return {"seq": place(c, i, lax.rem(j + r, N))}

    def cross(p):
        return {"seq": place(1 - c, i, p), "dp": 1 - c}

    def zdev(r):
        return {"head": lax.rem(z + r, nz)}

    cdev = {"dp": 1 - c}

    def remote(src, dst, index, device, landing=None):
        return pltpu.make_async_remote_copy(
            src_ref=src,
            dst_ref=dst,
            send_sem=ss.at[index],
            recv_sem=rs.at[index if landing is None else landing],
            device_id=device,
            device_id_type=MESH,
        )

    sent = []

    def start(copy):
        copy.start()
        sent.append((None, copy))
        return copy

    def start_if(cond, copy):
        pl.when(cond)(copy.start)
        sent.append((cond, copy))
        return copy

    barrier = pltpu.get_barrier_semaphore()
    peers = [gdev(r) for r in (1, 2, 3)] + [odev(r) for r in (1, 2, 3)]
    peers += [zdev(r) for r in range(1, nz)] + [cross(p) for p in range(N)] + [cdev]
    for peer in peers:
        pl.semaphore_signal(barrier, inc=1, device_id=peer, device_id_type=MESH)

    loads = [
        pltpu.make_async_copy(src, dst, loc.at[4 + n])
        for n, (src, dst) in enumerate(
            (
                (q_hbm, q_ref), (k_hbm, k_ref), (v_hbm, v_ref), (o_hbm, o_ref),
                (wv_hbm.at[i], wv_ref), (wk_hbm.at[i], wk_ref),
            )
        )
    ]
    for copy in loads:
        copy.start()

    for row, ref in ((0, q_ref), (1, k_ref)):
        loads[row].wait()
        full_rows = ref[...].astype(F32)
        squares = full_rows * full_rows
        folded = squares[:, :HD]
        for h in range(1, N):
            folded = folded + squares[:, h * HD : (h + 1) * HD]
        zs[z, row : row + 1, :] = row_sum(folded)
    for copy in loads[2:]:
        copy.wait()

    pl.semaphore_wait(barrier, len(peers))

    z1 = [start(remote(zs.at[z], zs.at[z], Z1 + r - 1, zdev(r))) for r in range(1, nz)]
    rows_mine = pl.ds(pl.multiple_of(i * T, T), T)
    a2a = {}

    def exchange(n, src, dst):
        group = []
        for r in (1, 3, 2):
            cols = pl.ds(pl.multiple_of(lax.rem(i + r, N) * HD, HD), HD)
            group.append(
                start(remote(src.at[:, cols], dst.at[rows_mine, :], A2A + 3 * n + r - 1, gdev(r)))
            )
        cols = pl.ds(pl.multiple_of(i * HD, HD), HD)
        copy = pltpu.make_async_copy(src.at[:, cols], dst.at[rows_mine, :], loc.at[n])
        copy.start()
        a2a[n] = (group, copy)

    def arrived(n):
        group, copy = a2a[n]
        for item in group:
            item.wait_recv()
        copy.wait()

    exchange(0, v_ref, hv)
    exchange(1, k_ref, hk)
    exchange(2, q_ref, hq)

    for copy in z1:
        copy.wait_recv()
    total = zs[0]
    for r in range(1, nz):
        total = total + zs[r]
    gs[i] = total
    g1 = [start(remote(gs.at[i], gs.at[i], G1 + r - 1, gdev(r))) for r in (1, 3, 2)]
    exchange(3, o_ref, ho)

    def unfold(dst):
        for n in range(KS):
            dst[:, n * HD : (n + 1) * HD] = fs[pl.ds(n, N * M, stride=KS), :].astype(BF16)

    mem_copies = []

    def spread(mem, value, index):
        mem[j] = value.astype(BF16).reshape(N, M, HD)
        for r in (1, 3, 2):
            wanted = first_core | (lax.rem(j + r, N) > j)
            copy = remote(mem.at[j], mem.at[j], MEM + 3 * index + r - 1, odev(r))
            start_if(wanted, copy)
            mem_copies.append((first_core | (lax.rem(j + N - r, N) < j), copy))

    arrived(0)
    fs[...] = hv[...].astype(F32)
    unfold(vu)
    spread(mvg, dot_nn(vu[...], wv_ref[...]), 1)

    for copy in g1:
        copy.wait_recv()
    gain_q = gq_ref[i]
    gain_k = gk_ref[i]
    arrived(1)
    for a in range(N):
        rows = slice(a * T, (a + 1) * T)
        inverse = lax.rsqrt(gs[a] * (1.0 / hh) + EPS)
        icq[rows, :] = as_column(inverse[0:1])
        ick[rows, :] = as_column(inverse[1:2])
        normed = (hk[rows, :].astype(F32) * ick[rows, :] * gain_k).astype(BF16)
        kn[rows, :] = normed
        fs[rows, :] = normed.astype(F32)
    unfold(ku)
    spread(mkg, dot_nn(ku[...], wk_ref[...]), 0)

    arrived(2)
    arrived(3)
    key_at = lax.broadcasted_iota(jnp.int32, (T, T), 0)
    query_at = lax.broadcasted_iota(jnp.int32, (T, T), 1)
    peaks = []
    for a in range(N):
        rows = slice(a * T, (a + 1) * T)
        normed = (hq[rows, :].astype(F32) * icq[rows, :] * gain_q).astype(BF16)
        qn[rows, :] = normed
        scores = jnp.where(key_at <= query_at, dot_nt(kn[rows, :], normed), NEG)
        s_all[a, 0:T, :] = scores
        g_all[a, 0:T, :] = dot_nt(hv[rows, :], ho[rows, :])
        peaks.append(jnp.max(fold8(scores), 0))

    for wanted, copy in mem_copies:
        pl.when(wanted)(copy.wait_recv)
    for b in range(N):
        for t in range(N):
            at = slice(t * M, (t + 1) * M)
            source = t + c * (b - t)
            member = b + c * (t - b)
            mkc[b, at, :] = mkg[source, member]
            mvc[b, at, :] = mvg[source, member]

    blocks = [a + c * (j - a) + 1 for a in range(N)]
    cuts = [M * (j + c * (a - j)) for a in range(N)]

    for a in range(N):
        rows = slice(a * T, (a + 1) * T)
        q_rows = qn[rows, :]
        o_rows = ho[rows, :]

        def score(b, peak8, a=a, q_rows=q_rows, o_rows=o_rows):
            limit = jnp.where(b == blocks[a] - 1, cuts[a], T)
            scores = jnp.where(key_at < limit, dot_nt(mkc[b], q_rows), NEG)
            at = pl.ds(pl.multiple_of(T * (b + 1), T), T)
            s_all[a, at, :] = scores
            g_all[a, at, :] = dot_nt(mvc[b], o_rows)
            return jnp.maximum(peak8, jnp.max(fold8(scores), 0))

        peak = jnp.max(lax.fori_loop(0, blocks[a], score, peaks[a]), 0, keepdims=True)

        def lift(n, state, a=a, peak=peak):
            mass8, weighted8 = state
            at = pl.ds(pl.multiple_of(n * 64, 64), 64)
            lifted = jnp.exp((s_all[a, at, :] - peak) * scale)
            s_all[a, at, :] = lifted
            mass8 = mass8 + jnp.sum(fold8(lifted), 0)
            weighted8 = weighted8 + jnp.sum(fold8(lifted * g_all[a, at, :]), 0)
            return mass8, weighted8

        none = jnp.zeros((8, T), F32)
        steps = (blocks[a] + 1) * (T // 64)
        mass8, weighted8 = lax.fori_loop(0, steps, lift, (none, none))
        inverse_mass = 1.0 / jnp.sum(mass8, 0, keepdims=True)
        row_delta = jnp.sum(weighted8, 0, keepdims=True) * inverse_mass

        def settle(n, state, a=a, inverse_mass=inverse_mass, row_delta=row_delta):
            at = pl.ds(pl.multiple_of(n * 64, 64), 64)
            attend = s_all[a, at, :] * inverse_mass
            p_all[a, at, :] = attend.astype(BF16)
            d_all[a, at, :] = (attend * (g_all[a, at, :] - row_delta)).astype(BF16)
            return state

        lax.fori_loop(0, steps, settle, 0)

    dmem_parts = []
    dmem_whole = []
    for b in range(N - 1, -1, -1):
        at = slice(T * (b + 1), T * (b + 2))
        for a in range(N - 1, -1, -1):
            rows = slice(a * T, (a + 1) * T)

            @pl.when(b < blocks[a])
            def _(a=a, rows=rows, at=at):
                add_k = dot_nn(d_all[a, at, :], qn[rows, :])
                add_v = dot_nn(p_all[a, at, :], ho[rows, :])
                if a < N - 1:
                    add_k = add_k + acc_k[...]
                    add_v = add_v + acc_v[...]
                acc_k[...] = add_k
                acc_v[...] = add_v

        @pl.when(b < blocks[N - 1])
        def _(b=b):
            sbk[b] = (acc_k[...] * scale).astype(BF16).reshape(N, M, HD)
            sbv[b] = acc_v[...].astype(BF16).reshape(N, M, HD)

        for n, (sb, rb) in enumerate(((sbk, rbk), (sbv, rbv))):
            for r in (1, 3, 2):
                to = lax.rem(j + r, N)
                copy = remote(
                    sb.at[b, to], rb.at[j, b], DMEM + 12 * n + 3 * b + r - 1, odev(r)
                )
                start_if(first_core, copy)
                dmem_parts.append((n, r, copy))
            whole = remote(
                sb.at[b], rb.at[j], DMEM1 + 4 * n + b, {"seq": place(c, i, b)}, DMEM1 + 4 * n + j
            )
            start_if((c == 1) & (b < j), whole)

    gain_q_sum = jnp.zeros((8, HD), F32)
    for a in range(N):
        rows = slice(a * T, (a + 1) * T)
        q_rows = qn[rows, :]

        def gather_q(b, total, a=a):
            at = pl.ds(pl.multiple_of(T * (b + 1), T), T)
            return total + dot_tn(d_all[a, at, :], mkc[b])

        grad_q = lax.fori_loop(0, blocks[a], gather_q, dot_tn(d_all[a, 0:T, :], kn[rows, :]))
        grad_q = grad_q * scale
        dkl[rows, :] = dot_nn(d_all[a, 0:T, :], q_rows) * scale
        dvl[rows, :] = dot_nn(p_all[a, 0:T, :], ho[rows, :])
        q_full = hq[rows, :].astype(F32)
        inv = icq[rows, :]
        gain_q_sum = gain_q_sum + jnp.sum(fold8(grad_q * q_full * inv), 0)
        gained = grad_q * gain_q
        aq[a] = (gained * inv).astype(BF16)
        pd[a, 0:1, :] = row_sum(gained * q_full)

    def homeward(src, dst, base):
        dst[i] = src[i]
        return [
            start(remote(src.at[lax.rem(i + r, N)], dst.at[i], base + r - 1, gdev(r)))
            for r in (1, 3, 2)
        ]

    home = homeward(aq, aqh, DQ)

    for m in range(N):
        at = slice(m * M, (m + 1) * M)
        block = m + c * (j - m)
        part = j + c * (m - j)
        acc_k[at, :] = sbk[block, part].astype(F32)
        acc_v[at, :] = sbv[block, part].astype(F32)
    for r in (1, 3, 2):
        source = lax.rem(j + N - r, N)

        @pl.when(first_core)
        def _(r=r):
            for _, q, copy in dmem_parts:
                if q == r:
                    copy.wait_recv()

        later = (c == 1) & (source > j)

        @pl.when(later)
        def _(source=source):
            for n, rb in ((0, rbk), (1, rbv)):
                remote(
                    rb.at[source], rb.at[source], DMEM1, odev(1), DMEM1 + 4 * n + source
                ).wait_recv()

        @pl.when(first_core | later)
        def _(source=source):
            acc_k[...] = acc_k[...] + rbk[source].reshape(N * M, HD).astype(F32)
            acc_v[...] = acc_v[...] + rbv[source].reshape(N * M, HD).astype(F32)

    grad_mem_k = acc_k[...].astype(BF16)
    grad_mem_v = acc_v[...].astype(BF16)

    square_k = dot_tn(ku[...], grad_mem_k)
    square_v = dot_tn(vu[...], grad_mem_v)
    for p in range(N):
        pay[0, p, 0:HD, :] = square_k[p * HD : (p + 1) * HD].astype(BF16)
        pay[1, p, 0:HD, :] = square_v[p * HD : (p + 1) * HD].astype(BF16)
    for n in range(KS):
        at = pl.ds(n, N * M, stride=KS)
        cols = slice(n * HD, (n + 1) * HD)
        dkl[at, :] = dkl[at, :] + dot_nt(grad_mem_k, wk_ref[cols, :])
        dvl[at, :] = dvl[at, :] + dot_nt(grad_mem_v, wv_ref[cols, :])
    gain_k_sum = jnp.zeros((8, HD), F32)
    for a in range(N):
        rows = slice(a * T, (a + 1) * T)
        av[a] = dvl[rows, :].astype(BF16)
        grad_k = dkl[rows, :]
        k_full = hk[rows, :].astype(F32)
        inv = ick[rows, :]
        gain_k_sum = gain_k_sum + jnp.sum(fold8(grad_k * k_full * inv), 0)
        gained = grad_k * gain_k
        ak[a] = (gained * inv).astype(BF16)
        pd[a, 1:2, :] = row_sum(gained * k_full)
    tail = PIECE - HD
    tail_k = jnp.broadcast_to(jnp.sum(gain_k_sum, 0, keepdims=True), (tail, HD)).astype(BF16)
    tail_q = jnp.broadcast_to(jnp.sum(gain_q_sum, 0, keepdims=True), (tail, HD)).astype(BF16)
    for p in range(N):
        pay[0, p, HD:PIECE, :] = tail_k
        pay[1, p, HD:PIECE, :] = tail_q

    scatter = [
        start(remote(pay.at[1 - c, p], rsi.at[1, j], RSX + p, cross(p), RSX + j))
        for p in range(N)
    ]
    scatter += [
        start(remote(pay.at[c, lax.rem(j + r, N)], rsi.at[0, j], RS + r - 1, odev(r)))
        for r in (1, 3, 2)
    ]
    home_pd = homeward(pd, pdh, PD)
    home += homeward(av, avh, DV)
    home += homeward(ak, akh, DK)

    for p in range(N):
        remote(pay.at[0, p], rsi.at[1, p], RSX + p, cross(p), RSX + p).wait_recv()
    for copy in scatter[N:]:
        copy.wait_recv()
    total = pay[c, j].astype(F32)
    for r in (1, 2, 3):
        total = total + rsi[0, lax.rem(j + r, N)].astype(F32)
    for p in range(N):
        total = total + rsi[1, p].astype(F32)
    full[c, j, i] = total.astype(BF16)
    agg = [
        start(remote(full.at[c, j, i], full.at[c, j, i], AGG + r - 1, gdev(r))) for r in (1, 3, 2)
    ]

    for copy in home_pd:
        copy.wait_recv()
    total = pdh[0]
    for h in range(1, N):
        total = total + pdh[h]
    zs2[z] = total
    z2 = [start(remote(zs2.at[z], zs2.at[z], Z2 + r - 1, zdev(r))) for r in range(1, nz)]

    for copy in agg:
        copy.wait_recv()
    ago = [start(remote(full.at[c, j], full.at[c, j], AGO + r - 1, odev(r))) for r in (1, 3, 2)]
    c2 = [start(remote(full.at[c, j], full.at[c, j], C2, cdev))]

    for copy in z2:
        copy.wait_recv()
    total = zs2[0]
    for r in range(1, nz):
        total = total + zs2[r]
    inverse = lax.rsqrt(gs[i] * (1.0 / hh) + EPS)
    shift = inverse * inverse * inverse * total * (1.0 / hh)
    shift_q = as_column(shift[0:1])
    shift_k = as_column(shift[1:2])
    for copy in home:
        copy.wait_recv()
    for h in range(N):
        cols = slice(h * HD, (h + 1) * HD)
        dq_out[:, cols] = (aqh[h].astype(F32) - q_ref[:, cols].astype(F32) * shift_q).astype(BF16)
        dk_out[:, cols] = (akh[h].astype(F32) - k_ref[:, cols].astype(F32) * shift_k).astype(BF16)
        dv_out[:, cols] = avh[h]

    for n, r in enumerate((1, 3, 2)):
        ago[n].wait_recv()
        at = full.at[c, lax.rem(j + N - r, N)]
        c2.append(start(remote(at, at, C2 + n + 1, cdev)))
    for copy in c2:
        copy.wait_recv()
    full_out[...] = full[...]

    for cond, copy in sent:
        if cond is None:
            copy.wait_send()
        else:
            pl.when(cond)(copy.wait_send)


def finish(
    dq_ref, dk_ref, dv_ref, full_ref,
    dq_out, dk_out, dv_out, qg_out, kg_out, sk_out, sv_out,
    sk_buf, sv_buf, sems,
):
    copies = [
        pltpu.make_async_copy(src, dst, sems.at[n])
        for n, (src, dst) in enumerate(((dq_ref, dq_out), (dk_ref, dk_out), (dv_ref, dv_out)))
    ]
    for copy in copies:
        copy.start()
    for n, (core, buf, out) in enumerate(((0, sk_buf, sk_out), (1, sv_buf, sv_out))):
        for h in range(N):
            for p in range(N):
                buf[h, p * HD : (p + 1) * HD, :] = full_ref[core, p, h, 0:HD, :].astype(F32)
            copy = pltpu.make_async_copy(buf.at[h], out.at[h], sems.at[3 + N * n + h])
            copy.start()
            copies.append(copy)
    for h in range(N):
        kg_out[h] = full_ref[0, 0, h, HD:PIECE, :].astype(F32)[0:1]
        qg_out[h] = full_ref[1, 0, h, HD:PIECE, :].astype(F32)[0:1]
    for copy in copies:
        copy.wait()


def on_device(nz, q, k, v, query_gain, key_gain, key_squeeze, value_squeeze, o):
    width = N * HD
    bf = functools.partial(pltpu.VMEM, dtype=BF16)
    ff = functools.partial(pltpu.VMEM, dtype=F32)
    rows = N * T
    deep = (N + 1) * T
    scratch = [bf((T, width))] * 4 + [bf((KS * HD, HD))] * 2
    scratch += [bf((rows, HD))] * 4 + [bf((rows, HD))] * 2 + [ff((rows, HD))] * 2
    scratch += [ff((rows, HD)), bf((N * M, KS * HD)), bf((N * M, KS * HD))]
    scratch += [ff((nz, 2, T)), ff((N, 2, T))]
    scratch += [bf((N, N, M, HD))] * 2 + [bf((N, N * M, HD))] * 2
    scratch += [ff((N, deep, T))] * 2 + [bf((N, deep, T))] * 2
    scratch += [ff((N * M, HD))] * 2 + [bf((N, N, M, HD))] * 4
    scratch += [ff((rows, HD))] * 2 + [bf((N, T, HD))] * 3 + [ff((N, 2, T))]
    scratch += [bf((N, T, HD))] * 3 + [ff((N, 2, T)), ff((nz, 2, T))]
    scratch += [bf((2, N, PIECE, HD))] * 2 + [bf((2, N, N, PIECE, HD))]
    scratch += [
        pltpu.SemaphoreType.DMA((N_SEM,)),
        pltpu.SemaphoreType.DMA((N_SEM,)),
        pltpu.SemaphoreType.DMA((10,)),
    ]
    vmem = pl.BlockSpec(memory_space=pltpu.VMEM)
    hbm = pl.BlockSpec(memory_space=pltpu.MemorySpace.HBM)
    stay = functools.partial(
        pltpu.with_memory_space_constraint, memory_space=pltpu.MemorySpace.HBM
    )
    grads = [jax.ShapeDtypeStruct((T, width), BF16)] * 3
    outs = pl.pallas_call(
        functools.partial(kernel, nz),
        out_shape=grads + [jax.ShapeDtypeStruct((2, N, N, PIECE, HD), BF16)],
        in_specs=[hbm] * 4 + [vmem] * 2 + [hbm] * 2,
        out_specs=[vmem] * 4,
        scratch_shapes=scratch,
        compiler_params=pltpu.CompilerParams(
            collective_id=0, has_side_effects=True, vmem_limit_bytes=40 * 2**20
        ),
    )(
        stay(q[0]), stay(k[0]), stay(v[0]), stay(o[0]),
        stay(query_gain.reshape(N, 1, HD)), stay(key_gain.reshape(N, 1, HD)),
        stay(key_squeeze), stay(value_squeeze),
    )
    kernels = jax.ShapeDtypeStruct((N, KS * HD, HD), F32)
    gains = jax.ShapeDtypeStruct((N, 1, HD), F32)
    dq, dk, dv, qg, kg, sk, sv = pl.pallas_call(
        finish,
        out_shape=grads + [gains] * 2 + [kernels] * 2,
        in_specs=[vmem] * 4,
        out_specs=[hbm] * 3 + [vmem] * 2 + [hbm] * 2,
        scratch_shapes=[
            ff((N, KS * HD, HD)), ff((N, KS * HD, HD)), pltpu.SemaphoreType.DMA((3 + 2 * N,)),
        ],
        compiler_params=pltpu.CompilerParams(vmem_limit_bytes=16 * 2**20),
    )(*outs)
    return dq[None], dk[None], dv[None], qg.reshape(width), kg.reshape(width), sk, sv


def solution(mesh):
    by_token = P("dp", "seq", "head")
    by_head = P("head", None, None)
    return jax.shard_map(
        functools.partial(on_device, mesh.shape["head"]),
        mesh=mesh,
        in_specs=(by_token,) * 3 + (P("head"), P("head"), by_head, by_head, by_token),
        out_specs=(by_token,) * 3 + (P("head"), P("head"), by_head, by_head),
        check_vma=False,
    )
```

```python
import functools

import jax
import jax.numpy as jnp
from jax import lax
from jax.experimental import pallas as pl
from jax.experimental.pallas import tpu as pltpu
from jax.sharding import PartitionSpec as P

HD = 128
KS = 4
N = 4
T = 256
M = 64
EPS = 1e-06
NEG = -1e30
LOG2E = 1.4426950408889634
MESH = pl.DeviceIdType.MESH
F32 = jnp.float32
BF16 = jnp.bfloat16

A2A = 0
Z1 = A2A + 12
G1 = Z1 + 7
MEM = G1 + 3
DMEM = MEM + 6
DMEM1 = DMEM + 24
DQ = DMEM1 + 8
DK = DQ + 3
DV = DK + 3
PD = DV + 3
Z2 = PD + 3
RS = Z2 + 7
RSX = RS + 3
AGG = RSX + 4
AGO = AGG + 3
C2 = AGO + 12
GM = C2 + 16
GR = GM + 6
GRX = GR + 3
GG = GRX + 4
N_SEM = GG + 3


def dot_nt(a, b):
    return lax.dot_general(a, b, (((1,), (1,)), ((), ())), preferred_element_type=F32)


def dot_tn(a, b):
    return lax.dot_general(a, b, (((0,), (0,)), ((), ())), preferred_element_type=F32)


def dot_nn(a, b):
    return lax.dot_general(a, b, (((1,), (0,)), ((), ())), preferred_element_type=F32)


def as_column(row):
    return jnp.transpose(jnp.broadcast_to(row, (HD, row.shape[1])))


def row_sum(block):
    return jnp.sum(jnp.transpose(block), 0, keepdims=True)


def fold8(block):
    return block.reshape(block.shape[0] // 8, 8, block.shape[1])


def kernel(
    nz,
    q_hbm, k_hbm, v_hbm, o_hbm, gq_ref, gk_ref, wk_hbm, wv_hbm,
    dq_out, dk_out, dv_out, full_out, gain_out,
    q_ref, k_ref, v_ref, o_ref, wk_ref, wv_ref,
    hq, hk, hv, ho, qn, kn, icq, ick, fs, ku, vu, zs, gs, mkg, mvg, mkc, mvc,
    p_all, g_all, m_all, fin, mkt, knt, dqt, acc_k, acc_v, sbk, sbv, rbk, rbv,
    aq, ak, av, pd, aqh, akh, avh, pdh, zs2,
    gmk, gmv, gmkh, gmvh, bkf, bvf, gmine, gsame, gother, gall,
    pay, rsi, full,
    ss, rs, loc,
):
    seq = lax.axis_index("seq")
    x = lax.rem(seq, N)
    y = lax.div(seq, N)
    z = lax.axis_index("head")
    c = lax.axis_index("dp")
    i = y + c * (x - y)
    j = x + c * (y - x)
    hh = nz * N * HD
    scale = HD ** (-0.5)
    first_core = c == 0

    def place(core, along, across):
        return along * (N - (N - 1) * core) + across * (1 + (N - 1) * core)

    def gdev(r):
        return {"seq": place(c, lax.rem(i + r, N), j)}

    def odev(r):
        return {"seq": place(c, i, lax.rem(j + r, N))}

    def cross(p):
        return {"seq": place(1 - c, i, p), "dp": 1 - c}

    def zdev(r):
        return {"head": lax.rem(z + r, nz)}

    cdev = {"dp": 1 - c}

    def remote(src, dst, index, device, landing=None):
        return pltpu.make_async_remote_copy(
            src_ref=src,
            dst_ref=dst,
            send_sem=ss.at[index],
            recv_sem=rs.at[index if landing is None else landing],
            device_id=device,
            device_id_type=MESH,
        )

    sent = []

    def start(copy):
        copy.start()
        sent.append((None, copy))
        return copy

    def start_if(cond, copy):
        pl.when(cond)(copy.start)
        sent.append((cond, copy))
        return copy

    barrier = pltpu.get_barrier_semaphore()
    peers = [gdev(r) for r in (1, 2, 3)] + [odev(r) for r in (1, 2, 3)]
    peers += [zdev(r) for r in range(1, nz)] + [cross(p) for p in range(N)] + [cdev]
    for peer in peers:
        pl.semaphore_signal(barrier, inc=1, device_id=peer, device_id_type=MESH)

    loads = [
        pltpu.make_async_copy(src, dst, loc.at[4 + n])
        for n, (src, dst) in enumerate(
            (
                (q_hbm, q_ref), (k_hbm, k_ref), (v_hbm, v_ref), (o_hbm, o_ref),
                (wv_hbm, wv_ref), (wk_hbm, wk_ref),
            )
        )
    ]
    for copy in loads:
        copy.start()

    for row, ref in ((0, q_ref), (1, k_ref)):
        loads[row].wait()
        full_rows = ref[...].astype(F32)
        squares = full_rows * full_rows
        folded = squares[:, :HD]
        for h in range(1, N):
            folded = folded + squares[:, h * HD : (h + 1) * HD]
        zs[z, row : row + 1, :] = row_sum(folded)
    for copy in loads[2:4]:
        copy.wait()

    pl.semaphore_wait(barrier, len(peers))

    z1 = [start(remote(zs.at[z], zs.at[z], Z1 + r - 1, zdev(r))) for r in range(1, nz)]
    rows_mine = pl.ds(pl.multiple_of(i * T, T), T)
    a2a = {}

    def exchange(n, src, dst):
        group = []
        for r in (1, 3, 2):
            cols = pl.ds(pl.multiple_of(lax.rem(i + r, N) * HD, HD), HD)
            group.append(
                start(remote(src.at[:, cols], dst.at[rows_mine, :], A2A + 3 * n + r - 1, gdev(r)))
            )
        cols = pl.ds(pl.multiple_of(i * HD, HD), HD)
        copy = pltpu.make_async_copy(src.at[:, cols], dst.at[rows_mine, :], loc.at[n])
        copy.start()
        a2a[n] = (group, copy)

    def arrived(n):
        group, copy = a2a[n]
        for item in group:
            item.wait_recv()
        copy.wait()

    exchange(0, v_ref, hv)
    exchange(1, k_ref, hk)
    exchange(2, q_ref, hq)

    for copy in z1:
        copy.wait_recv()
    total = zs[0]
    for r in range(1, nz):
        total = total + zs[r]
    gs[i] = total
    g1 = [start(remote(gs.at[i], gs.at[i], G1 + r - 1, gdev(r))) for r in (1, 3, 2)]
    exchange(3, o_ref, ho)
    for copy in loads[4:]:
        copy.wait()

    def unfold(dst):
        for n in range(KS):
            dst[:, n * HD : (n + 1) * HD] = fs[pl.ds(n, N * M, stride=KS), :].astype(BF16)

    mem_copies = []

    def spread(mem, value, index):
        mem[j] = value.astype(BF16).reshape(N, M, HD)
        for r in (1, 3, 2):
            wanted = first_core | (lax.rem(j + r, N) > j)
            copy = remote(mem.at[j], mem.at[j], MEM + 3 * index + r - 1, odev(r))
            start_if(wanted, copy)
            mem_copies.append((first_core | (lax.rem(j + N - r, N) < j), copy))

    arrived(0)
    fs[...] = hv[...].astype(F32)
    unfold(vu)
    spread(mvg, dot_nn(vu[...], wv_ref[i]), 1)

    for copy in g1:
        copy.wait_recv()
    gain_q = gq_ref[i]
    gain_k = gk_ref[i]
    arrived(1)
    for a in range(N):
        rows = slice(a * T, (a + 1) * T)
        inverse = lax.rsqrt(gs[a] * (1.0 / hh) + EPS)
        icq[rows, :] = as_column(inverse[0:1])
        ick[rows, :] = as_column(inverse[1:2])
        normed = (hk[rows, :].astype(F32) * ick[rows, :] * gain_k).astype(BF16)
        kn[rows, :] = normed
        fs[rows, :] = normed.astype(F32)
    unfold(ku)
    spread(mkg, dot_nn(ku[...], wk_ref[i]), 0)

    arrived(2)
    arrived(3)
    key_at = lax.broadcasted_iota(jnp.int32, (T, T), 0)
    query_at = lax.broadcasted_iota(jnp.int32, (T, T), 1)
    rate = scale * LOG2E

    def score(a, block, mask, keys, values):
        at = pl.ds(pl.multiple_of(block * T, T), T)
        rows = slice(a * T, (a + 1) * T)
        scores = jnp.where(mask, dot_nt(keys, qn[rows, :]), NEG)
        grads = dot_nt(values, ho[rows, :])
        peak = jnp.max(jnp.max(fold8(scores), 0), 0, keepdims=True)
        lifted = jnp.exp2((scores - peak) * rate)
        p_all[a, at, :] = lifted
        g_all[a, at, :] = grads
        m_all[a, block] = peak
        mass = jnp.sum(jnp.sum(fold8(lifted), 0), 0, keepdims=True)
        weighted = jnp.sum(jnp.sum(fold8(lifted * grads), 0), 0, keepdims=True)
        return peak, mass, weighted

    state = []
    for a in range(N):
        rows = slice(a * T, (a + 1) * T)
        qn[rows, :] = (hq[rows, :].astype(F32) * icq[rows, :] * gain_q).astype(BF16)
        state.append(score(a, 0, key_at <= query_at, kn[rows, :], hv[rows, :]))
        knt[a] = jnp.transpose(kn[rows, :])

    for wanted, copy in mem_copies:
        pl.when(wanted)(copy.wait_recv)
    for b in range(N):
        for t in range(N):
            at = slice(t * M, (t + 1) * M)
            source = t + c * (b - t)
            member = b + c * (t - b)
            mkc[b, at, :] = mkg[source, member]
            mvc[b, at, :] = mvg[source, member]
        mkt[b] = jnp.transpose(mkc[b])

    edges = [a + c * (j - a) for a in range(N)]
    cuts = [M * (j + c * (a - j)) for a in range(N)]
    blocks = [edges[a] + jnp.where(cuts[a] > 0, 1, 0) for a in range(N)]

    for a in range(N):

        def absorb(b, current, a=a):
            old_peak, old_mass, old_weighted = current
            limit = jnp.where(b == edges[a], cuts[a], T)
            peak, mass, weighted = score(a, b + 1, key_at < limit, mkc[b], mvc[b])
            top = jnp.maximum(old_peak, peak)
            old_factor = jnp.exp2((old_peak - top) * rate)
            factor = jnp.exp2((peak - top) * rate)
            return (
                top,
                old_mass * old_factor + mass * factor,
                old_weighted * old_factor + weighted * factor,
            )

        peak, mass, weighted = lax.fori_loop(0, blocks[a], absorb, state[a])
        inverse_mass = 1.0 / mass
        fin[a, 0] = peak
        fin[a, 1] = inverse_mass
        fin[a, 2] = weighted * inverse_mass

    def settle(a, block):
        at = pl.ds(pl.multiple_of(block * T, T), T)
        factor = jnp.exp2((m_all[a, block] - fin[a, 0]) * rate) * fin[a, 1]
        attend = p_all[a, at, :] * factor
        d_scores = attend * (g_all[a, at, :] - fin[a, 2])
        return attend.astype(BF16), d_scores.astype(BF16)

    def homeward(src, dst, base):
        dst[i] = src[i]
        return [
            start(remote(src.at[lax.rem(i + r, N)], dst.at[i], base + r - 1, gdev(r)))
            for r in (1, 3, 2)
        ]

    def norm_side(grad, raw, inv, gain):
        raw_full = raw.astype(F32)
        gained = grad * gain
        total = jnp.sum(fold8(grad * raw_full * inv), 0)
        return total, (gained * inv).astype(BF16), row_sum(gained * raw_full)

    gain_k_sum = jnp.zeros((8, HD), F32)
    for a in range(N):
        rows = slice(a * T, (a + 1) * T)
        attend, d_scores = settle(a, 0)
        dqt[a] = dot_nn(knt[a], d_scores)
        grad_k = dot_nn(d_scores, qn[rows, :]) * scale
        av[a] = dot_nn(attend, ho[rows, :]).astype(BF16)
        total, ak[a], pd[a, 1:2, :] = norm_side(grad_k, hk[rows, :], ick[rows, :], gain_k)
        gain_k_sum = gain_k_sum + total
    home = homeward(av, avh, DV)
    home += homeward(ak, akh, DK)

    dmem_parts = []
    dmem_whole = []
    for b in range(N):
        acc_k[...] = jnp.zeros((T, HD), F32)
        acc_v[...] = jnp.zeros((T, HD), F32)

        def add_up(a, nothing, b=b):
            rows = pl.ds(pl.multiple_of(a * T, T), T)
            attend, d_scores = settle(a, b + 1)
            acc_k[...] = acc_k[...] + dot_nn(d_scores, qn[rows, :])
            acc_v[...] = acc_v[...] + dot_nn(attend, ho[rows, :])
            dqt[a] = dqt[a] + dot_nn(mkt[b], d_scores)
            return nothing

        past = jnp.where(j > 0, 0, 1)
        within = jnp.where(b == j, 1, 0)
        lowest = (1 - c) * (b + past) + c * jnp.where(b <= j, within, N)
        lax.fori_loop(lowest, N, add_up, 0)

        @pl.when(first_core | (b <= j))
        def _(b=b):
            sbk[b] = (acc_k[...] * scale).astype(BF16).reshape(N, M, HD)
            sbv[b] = acc_v[...].astype(BF16).reshape(N, M, HD)

        for n, (sb, rb) in enumerate(((sbk, rbk), (sbv, rbv))):
            for r in (1, 3, 2):
                to = lax.rem(j + r, N)
                copy = remote(
                    sb.at[b, to], rb.at[j, b], DMEM + 12 * n + 3 * b + r - 1, odev(r)
                )
                start_if(first_core, copy)
                dmem_parts.append((n, r, copy))
            whole = remote(
                sb.at[b], rb.at[j], DMEM1 + 4 * n + b, {"seq": place(c, i, b)}, DMEM1 + 4 * n + j
            )
            start_if((c == 1) & (b < j), whole)

    gain_q_sum = jnp.zeros((8, HD), F32)
    for a in range(N):
        rows = slice(a * T, (a + 1) * T)
        grad_q = jnp.transpose(dqt[a]) * scale
        total, aq[a], pd[a, 0:1, :] = norm_side(grad_q, hq[rows, :], icq[rows, :], gain_q)
        gain_q_sum = gain_q_sum + total

    home_pd = homeward(pd, pdh, PD)

    for m in range(N):
        at = slice(m * M, (m + 1) * M)
        block = m + c * (j - m)
        part = j + c * (m - j)
        acc_k[at, :] = sbk[block, part].astype(F32)
        acc_v[at, :] = sbv[block, part].astype(F32)
    for r in (1, 3, 2):
        source = lax.rem(j + N - r, N)

        @pl.when(first_core)
        def _(r=r):
            for _, q, copy in dmem_parts:
                if q == r:
                    copy.wait_recv()

        later = (c == 1) & (source > j)

        @pl.when(later)
        def _(source=source):
            for n, rb in ((0, rbk), (1, rbv)):
                remote(
                    rb.at[source], rb.at[source], DMEM1, odev(1), DMEM1 + 4 * n + source
                ).wait_recv()

        @pl.when(first_core | later)
        def _(source=source):
            acc_k[...] = acc_k[...] + rbk[source].reshape(N * M, HD).astype(F32)
            acc_v[...] = acc_v[...] + rbv[source].reshape(N * M, HD).astype(F32)

    grad_mem_k = acc_k[...].astype(BF16)
    grad_mem_v = acc_v[...].astype(BF16)

    square_k = dot_tn(ku[...], grad_mem_k)
    square_v = dot_tn(vu[...], grad_mem_v)
    for p in range(N):
        pay[0, p] = square_k[p * HD : (p + 1) * HD].astype(BF16)
        pay[1, p] = square_v[p * HD : (p + 1) * HD].astype(BF16)
    gmk[...] = grad_mem_k.reshape(N, M, HD)
    gmv[...] = grad_mem_v.reshape(N, M, HD)

    scatter = [
        start(remote(pay.at[1 - c, p], rsi.at[1, j], RSX + p, cross(p), RSX + j))
        for p in range(N)
    ]
    scatter += [
        start(remote(pay.at[c, lax.rem(j + r, N)], rsi.at[0, j], RS + r - 1, odev(r)))
        for r in (1, 3, 2)
    ]
    slots = homeward(gmk, gmkh, GM) + homeward(gmv, gmvh, GM + 3)

    crossed = square_k[0:HD] * wk_ref[i, 0:HD, :].astype(F32)
    for p in range(1, N):
        at = slice(p * HD, (p + 1) * HD)
        crossed = crossed + square_k[at] * wk_ref[i, at, :].astype(F32)
    gmine[0:1, :] = jnp.sum(gain_q_sum, 0, keepdims=True)
    gmine[1:2, :] = jnp.sum(gain_k_sum, 0, keepdims=True) + row_sum(crossed) / gain_k
    gains = [start(remote(gmine, gsame.at[j], GR + r - 1, odev(r))) for r in (1, 3, 2)]
    for p in range(N):
        start(remote(gmine, gother.at[j], GRX + p, cross(p), GRX + j))

    home += homeward(aq, aqh, DQ)

    for copy in slots:
        copy.wait_recv()
    product = jnp.zeros((T, HD), F32)
    for h in range(N):
        spread_k = dot_nt(gmkh[h], wk_ref[h])
        spread_v = dot_nt(gmvh[h], wv_ref[h])
        for n in range(KS):
            at = pl.ds(n, M, stride=KS)
            cols = slice(n * HD, (n + 1) * HD)
            bkf[h, at, :] = spread_k[:, cols]
            bvf[h, at, :] = spread_v[:, cols]
        gained = bkf[h] * gk_ref[h]
        bkf[h] = gained
        product = product + gained * k_ref[:, h * HD : (h + 1) * HD].astype(F32)

    for copy in home_pd:
        copy.wait_recv()
    total = pdh[0]
    for h in range(1, N):
        total = total + pdh[h]
    zs2[z, 0:1, :] = total[0:1]
    zs2[z, 1:2, :] = total[1:2] + row_sum(product)
    z2 = [start(remote(zs2.at[z], zs2.at[z], Z2 + r - 1, zdev(r))) for r in range(1, nz)]

    for p in range(N):
        remote(pay.at[0, p], rsi.at[1, p], RSX + p, cross(p), RSX + p).wait_recv()
    for copy in scatter[N:]:
        copy.wait_recv()
    total = pay[c, j].astype(F32)
    for r in (1, 2, 3):
        total = total + rsi[0, lax.rem(j + r, N)].astype(F32)
    for p in range(N):
        total = total + rsi[1, p].astype(F32)
    full[c, j, i] = total.astype(BF16)
    agg = [
        start(remote(full.at[c, j, i], full.at[c, j, i], AGG + r - 1, gdev(r))) for r in (1, 3, 2)
    ]
    ago = {}
    c2 = []

    def pass_on(slot, member):
        piece = full.at[c, j, member]
        for r in (1, 3, 2):
            ago[r, slot] = start(remote(piece, piece, AGO + 4 * (r - 1) + slot, odev(r)))
        c2.append(start(remote(piece, piece, C2 + slot, cdev)))

    pass_on(0, i)

    for copy in gains:
        copy.wait_recv()
    for p in range(N):
        remote(gmine, gother.at[p], GRX + p, cross(p), GRX + p).wait_recv()
    total = gmine[...]
    for r in (1, 2, 3):
        total = total + gsame[lax.rem(j + r, N)]
    for p in range(N):
        total = total + gother[p]
    gall[i] = total
    gg = [start(remote(gall.at[i], gall.at[i], GG + r - 1, gdev(r))) for r in (1, 3, 2)]

    for n, r in enumerate((1, 3, 2)):
        agg[n].wait_recv()
        pass_on(n + 1, lax.rem(i + N - r, N))

    for copy in z2:
        copy.wait_recv()
    total = zs2[0]
    for r in range(1, nz):
        total = total + zs2[r]
    inverse = lax.rsqrt(gs[i] * (1.0 / hh) + EPS)
    shift = inverse * inverse * inverse * total * (1.0 / hh)
    shift_q = as_column(shift[0:1])
    shift_k = as_column(shift[1:2])
    for copy in home:
        copy.wait_recv()
    inverse_k = as_column(inverse[1:2])
    for h in range(N):
        cols = slice(h * HD, (h + 1) * HD)
        dq_out[:, cols] = (aqh[h].astype(F32) - q_ref[:, cols].astype(F32) * shift_q).astype(BF16)
        grad_k = akh[h].astype(F32) + bkf[h] * inverse_k
        dk_out[:, cols] = (grad_k - k_ref[:, cols].astype(F32) * shift_k).astype(BF16)
        dv_out[:, cols] = (avh[h].astype(F32) + bvf[h]).astype(BF16)
    for copy in gg:
        copy.wait_recv()
    gain_out[...] = gall[...]

    for slot, back in enumerate((0, 1, 3, 2)):
        for n, r in enumerate((1, 3, 2)):
            ago[r, slot].wait_recv()
            at = full.at[c, lax.rem(j + N - r, N), lax.rem(i + N - back, N)]
            c2.append(start(remote(at, at, C2 + 4 + 3 * slot + n, cdev)))
    for copy in c2:
        copy.wait_recv()
    full_out[...] = full[...]

    for cond, copy in sent:
        if cond is None:
            copy.wait_send()
        else:
            pl.when(cond)(copy.wait_send)


def finish(
    dq_ref, dk_ref, dv_ref, full_ref, gain_ref,
    dq_out, dk_out, dv_out, qg_out, kg_out, sk_out, sv_out,
    sk_buf, sv_buf, sems,
):
    copies = [
        pltpu.make_async_copy(src, dst, sems.at[n])
        for n, (src, dst) in enumerate(((dq_ref, dq_out), (dk_ref, dk_out), (dv_ref, dv_out)))
    ]
    for copy in copies:
        copy.start()
    for n, (core, buf, out) in enumerate(((0, sk_buf, sk_out), (1, sv_buf, sv_out))):
        for h in range(N):
            for p in range(N):
                buf[h, p * HD : (p + 1) * HD, :] = full_ref[core, p, h, 0:HD, :].astype(F32)
            copy = pltpu.make_async_copy(buf.at[h], out.at[h], sems.at[3 + N * n + h])
            copy.start()
            copies.append(copy)
    for h in range(N):
        qg_out[h] = gain_ref[h, 0:1, :]
        kg_out[h] = gain_ref[h, 1:2, :]
    for copy in copies:
        copy.wait()


def on_device(nz, q, k, v, query_gain, key_gain, key_squeeze, value_squeeze, o):
    width = N * HD
    bf = functools.partial(pltpu.VMEM, dtype=BF16)
    ff = functools.partial(pltpu.VMEM, dtype=F32)
    rows = N * T
    deep = (N + 1) * T
    scratch = [bf((T, width))] * 4 + [bf((N, KS * HD, HD))] * 2
    scratch += [bf((rows, HD))] * 4 + [bf((rows, HD))] * 2 + [ff((rows, HD))] * 2
    scratch += [ff((rows, HD)), bf((N * M, KS * HD)), bf((N * M, KS * HD))]
    scratch += [ff((nz, 2, T)), ff((N, 2, T))]
    scratch += [bf((N, N, M, HD))] * 2 + [bf((N, N * M, HD))] * 2
    scratch += [ff((N, deep, T))] * 2 + [ff((N, N + 1, 1, T)), ff((N, 3, 1, T))]
    scratch += [bf((N, HD, T))] * 2 + [ff((N, HD, T))]
    scratch += [ff((N * M, HD))] * 2 + [bf((N, N, M, HD))] * 4
    scratch += [bf((N, T, HD))] * 3 + [ff((N, 2, T))]
    scratch += [bf((N, T, HD))] * 3 + [ff((N, 2, T)), ff((nz, 2, T))]
    scratch += [bf((N, M, HD))] * 4 + [ff((N, T, HD))] * 2
    scratch += [ff((2, HD))] + [ff((N, 2, HD))] * 3
    scratch += [bf((2, N, HD, HD))] * 2 + [bf((2, N, N, HD, HD))]
    scratch += [
        pltpu.SemaphoreType.DMA((N_SEM,)),
        pltpu.SemaphoreType.DMA((N_SEM,)),
        pltpu.SemaphoreType.DMA((10,)),
    ]
    vmem = pl.BlockSpec(memory_space=pltpu.VMEM)
    hbm = pl.BlockSpec(memory_space=pltpu.MemorySpace.HBM)
    stay = functools.partial(
        pltpu.with_memory_space_constraint, memory_space=pltpu.MemorySpace.HBM
    )
    grads = [jax.ShapeDtypeStruct((T, width), BF16)] * 3
    outs = pl.pallas_call(
        functools.partial(kernel, nz),
        out_shape=grads
        + [jax.ShapeDtypeStruct((2, N, N, HD, HD), BF16), jax.ShapeDtypeStruct((N, 2, HD), F32)],
        in_specs=[hbm] * 4 + [vmem] * 2 + [hbm] * 2,
        out_specs=[vmem] * 5,
        scratch_shapes=scratch,
        compiler_params=pltpu.CompilerParams(
            collective_id=0, has_side_effects=True, vmem_limit_bytes=40 * 2**20
        ),
    )(
        stay(q[0]), stay(k[0]), stay(v[0]), stay(o[0]),
        stay(query_gain.reshape(N, 1, HD)), stay(key_gain.reshape(N, 1, HD)),
        stay(key_squeeze), stay(value_squeeze),
    )
    kernels = jax.ShapeDtypeStruct((N, KS * HD, HD), F32)
    gains = jax.ShapeDtypeStruct((N, 1, HD), F32)
    dq, dk, dv, qg, kg, sk, sv = pl.pallas_call(
        finish,
        out_shape=grads + [gains] * 2 + [kernels] * 2,
        in_specs=[vmem] * 5,
        out_specs=[hbm] * 3 + [vmem] * 2 + [hbm] * 2,
        scratch_shapes=[
            ff((N, KS * HD, HD)), ff((N, KS * HD, HD)), pltpu.SemaphoreType.DMA((3 + 2 * N,)),
        ],
        compiler_params=pltpu.CompilerParams(vmem_limit_bytes=16 * 2**20),
    )(*outs)
    return dq[None], dk[None], dv[None], qg.reshape(width), kg.reshape(width), sk, sv


def solution(mesh):
    by_token = P("dp", "seq", "head")
    by_head = P("head", None, None)
    return jax.shard_map(
        functools.partial(on_device, mesh.shape["head"]),
        mesh=mesh,
        in_specs=(by_token,) * 3 + (P("head"), P("head"), by_head, by_head, by_token),
        out_specs=(by_token,) * 3 + (P("head"), P("head"), by_head, by_head),
        check_vma=False,
    )
```

```python
import functools

import jax
import jax.numpy as jnp
from jax import lax
from jax.experimental import pallas as pl
from jax.experimental.pallas import tpu as pltpu
from jax.sharding import PartitionSpec as P

HD = 128
KS = 4
N = 4
T = 256
M = 64
EPS = 1e-06
NEG = -1e30
LOG2E = 1.4426950408889634
MESH = pl.DeviceIdType.MESH
F32 = jnp.float32
BF16 = jnp.bfloat16

A2A = 0
Z1 = A2A + 4
G1 = Z1 + 1
MEM = G1 + 1
DMEM = MEM + 2
DMEM3 = DMEM + 2
DQ = DMEM3 + 6
DK = DQ + 1
DV = DK + 1
PD = DV + 1
Z2 = PD + 1
RS = Z2 + 1
RSX = RS + 1
AGG = RSX + 1
AGO = AGG + 3
C2 = AGO + 4
GM = C2 + 8
GR = GM + 2
GRX = GR + 1
GG = GRX + 1
N_RECV = GG + 1
N_SEND = 4 + 6


def dot_nt(a, b):
    return lax.dot_general(a, b, (((1,), (1,)), ((), ())), preferred_element_type=F32)


def dot_tn(a, b):
    return lax.dot_general(a, b, (((0,), (0,)), ((), ())), preferred_element_type=F32)


def dot_nn(a, b):
    return lax.dot_general(a, b, (((1,), (0,)), ((), ())), preferred_element_type=F32)


def as_column(row):
    return jnp.transpose(jnp.broadcast_to(row, (HD, row.shape[1])))


def row_sum(block):
    return jnp.sum(jnp.transpose(block), 0, keepdims=True)


def fold8(block):
    return block.reshape(block.shape[0] // 8, 8, block.shape[1])


def kernel(
    nz,
    q_hbm, k_hbm, v_hbm, o_hbm, gq_hbm, gk_hbm, wk_hbm, wv_hbm,
    dq_out, dk_out, dv_out, kern_out, gain_out,
    gq_ref, gk_ref, dq_buf, dk_buf, dv_buf, kern, gain_buf, q_ref, k_ref, v_ref, o_ref, wk_ref, wv_ref,
    hq, hk, hv, ho, qn, kn, icq, ick, fs, ku, vu, gsp, zs, gs, mkg, mvg, mkc, mvc,
    p_all, g_all, m_all, fin, mkt, knt, dqt, acc_k, acc_v, sbk, sbv, rbk, rbv,
    aq, ak, av, pd, aqh, akh, avh, pdh, zs2,
    gmk, gmv, gmkh, gmvh, bkf, bvf, gmine, gsame, gother, gall,
    pay, rsi, full, tally,
    ss, rs, loc, out_sem,
):
    seq = lax.axis_index("seq")
    x = lax.rem(seq, N)
    y = lax.div(seq, N)
    z = lax.axis_index("head")
    c = lax.axis_index("dp")
    i = y
    j = x
    near = i + c * (j - i)
    far = j + c * (i - j)
    hh = nz * N * HD
    scale = HD ** (-0.5)

    def gdev(r):
        return {"seq": lax.rem(i + r, N) * N + j}

    def odev(r):
        return {"seq": i * N + lax.rem(j + r, N)}

    def ndev(r):
        to = lax.rem(near + r, N)
        return {"seq": to * (N - (N - 1) * c) + far * (1 + (N - 1) * c)}

    def fdev(r):
        to = lax.rem(far + r, N)
        return {"seq": near * (N - (N - 1) * c) + to * (1 + (N - 1) * c)}

    def cross(p):
        return {"seq": i * N + p, "dp": 1 - c}

    def zdev(r):
        return {"head": lax.rem(z + r, nz)}

    cdev = {"dp": 1 - c}

    def remote(src, dst, index, device, group):
        return pltpu.make_async_remote_copy(
            src_ref=src,
            dst_ref=dst,
            send_sem=ss.at[group],
            recv_sem=rs.at[index],
            device_id=device,
            device_id_type=MESH,
        )

    sent = [0, 0, 0, 0]

    def send(src, dst, index, device, group):
        remote(src, dst, index, device, group).start()
        size = 1
        for length in src.shape:
            size = size * length
        sent[group] += size * src.dtype.itemsize

    def landed(index, space):
        remote(space, space, index, cdev, 0).wait_recv()

    written = []

    def write(src, dst, index):
        copy = pltpu.make_async_copy(src, dst, out_sem.at[index])
        copy.start()
        written.append(copy)

    def emit(core, across, along):
        head = along + core * (across - along)
        rows = pl.ds(pl.multiple_of((across + core * (along - across)) * HD, HD), HD)
        kern[core, head, rows, :] = full[core, across, along].astype(F32)
        copy = pltpu.make_async_copy(
            kern.at[core, head, rows, :], kern_out.at[core, head, rows, :], out_sem.at[0]
        )
        copy.start()


    barrier = pltpu.get_barrier_semaphore()
    peers = [gdev(r) for r in (1, 2, 3)] + [odev(r) for r in (1, 2, 3)]
    peers += [zdev(r) for r in range(1, nz)] + [cross(p) for p in range(N)] + [cdev]
    for peer in peers:
        pl.semaphore_signal(barrier, inc=1, device_id=peer, device_id_type=MESH)

    loads = [
        pltpu.make_async_copy(src, dst, loc.at[4 + n])
        for n, (src, dst) in enumerate(
            (
                (q_hbm, q_ref), (k_hbm, k_ref), (v_hbm, v_ref), (o_hbm, o_ref),
                (wv_hbm, wv_ref), (wk_hbm, wk_ref),
                (gq_hbm, gq_ref), (gk_hbm, gk_ref),
            )
        )
    ]
    for copy in loads:
        copy.start()

    for row, ref in ((0, q_ref), (1, k_ref)):
        loads[row].wait()
        full_rows = ref[...].astype(F32)
        squares = full_rows * full_rows
        folded = squares[:, :HD]
        for h in range(1, N):
            folded = folded + squares[:, h * HD : (h + 1) * HD]
        gsp[i, row : row + 1, :] = row_sum(folded)
    for copy in loads[2:4]:
        copy.wait()

    pl.semaphore_wait(barrier, len(peers))

    for r in (2, 1, 3):
        send(gsp.at[i], gsp.at[i], G1, gdev(r), 3)
    rows_mine = pl.ds(pl.multiple_of(i * T, T), T)
    own = {}

    def exchange(n, src, dst):
        for r in (1, 3, 2):
            cols = pl.ds(pl.multiple_of(lax.rem(i + r, N) * HD, HD), HD)
            send(src.at[:, cols], dst.at[rows_mine, :], A2A + n, gdev(r), 0)
        cols = pl.ds(pl.multiple_of(i * HD, HD), HD)
        own[n] = pltpu.make_async_copy(src.at[:, cols], dst.at[rows_mine, :], loc.at[n])
        own[n].start()

    def arrived(n):
        landed(A2A + n, hv.at[0 : 3 * T, :])
        own[n].wait()

    exchange(0, v_ref, hv)
    exchange(1, k_ref, hk)

    exchange(2, q_ref, hq)
    exchange(3, o_ref, ho)

    landed(G1, gsp.at[0:3])
    for r in range(1, nz):
        send(gsp, zs.at[z], Z1, zdev(r), 0)
    for copy in loads[4:]:
        copy.wait()

    def unfold(dst):
        for n in range(KS):
            dst[:, n * HD : (n + 1) * HD] = fs[pl.ds(n, N * M, stride=KS), :].astype(BF16)

    def spread(mem, value, index):
        mem[j] = value.astype(BF16).reshape(N, M, HD)
        for r in (1, 3, 2):
            send(mem.at[j], mem.at[j], MEM + index, odev(r), 0)

    arrived(0)
    fs[...] = hv[...].astype(F32)
    unfold(vu)
    spread(mvg, dot_nn(vu[...], wv_ref[i]), 1)

    landed(Z1, zs.at[0 : nz - 1])
    gs[...] = gsp[...]
    for r in range(1, nz):
        gs[...] = gs[...] + zs[lax.rem(z + r, nz)]
    gain_q = gq_ref[i]
    gain_k = gk_ref[i]
    arrived(1)
    for a in range(N):
        rows = slice(a * T, (a + 1) * T)
        inverse = lax.rsqrt(gs[a] * (1.0 / hh) + EPS)
        icq[rows, :] = as_column(inverse[0:1])
        ick[rows, :] = as_column(inverse[1:2])
        normed = (hk[rows, :].astype(F32) * ick[rows, :] * gain_k).astype(BF16)
        kn[rows, :] = normed
        fs[rows, :] = normed.astype(F32)
    unfold(ku)
    spread(mkg, dot_nn(ku[...], wk_ref[i]), 0)

    arrived(2)
    arrived(3)
    key_at = lax.broadcasted_iota(jnp.int32, (T, T), 0)
    query_at = lax.broadcasted_iota(jnp.int32, (T, T), 1)
    rate = scale * LOG2E

    def score(a, block, mask, keys, values):
        at = pl.ds(pl.multiple_of(block * T, T), T)
        rows = slice(a * T, (a + 1) * T)
        scores = jnp.where(mask, dot_nt(keys, qn[rows, :]), NEG)
        grads = dot_nt(values, ho[rows, :])
        peak = jnp.max(jnp.max(fold8(scores), 0), 0, keepdims=True)
        lifted = jnp.exp2((scores - peak) * rate)
        p_all[a, at, :] = lifted
        g_all[a, at, :] = grads
        m_all[a, block] = peak
        mass = jnp.sum(jnp.sum(fold8(lifted), 0), 0, keepdims=True)
        weighted = jnp.sum(jnp.sum(fold8(lifted * grads), 0), 0, keepdims=True)
        return peak, mass, weighted

    state = []
    for a in range(N):
        rows = slice(a * T, (a + 1) * T)
        qn[rows, :] = (hq[rows, :].astype(F32) * icq[rows, :] * gain_q).astype(BF16)
        state.append(score(a, 0, key_at <= query_at, kn[rows, :], hv[rows, :]))
        knt[a] = jnp.transpose(kn[rows, :])

    landed(MEM, mkg.at[0:3])
    landed(MEM + 1, mvg.at[0:3])
    for b in range(N):
        for t in range(N):
            at = slice(t * M, (t + 1) * M)
            mkc[b, at, :] = mkg[t, b]
            mvc[b, at, :] = mvg[t, b]
        mkt[b] = jnp.transpose(mkc[b])

    past = jnp.where(j > 0, 0, 1)

    for a in range(N):

        def absorb(b, current, a=a):
            old_peak, old_mass, old_weighted = current
            limit = jnp.where(b == a, j * M, T)
            peak, mass, weighted = score(a, b + 1, key_at < limit, mkc[b], mvc[b])
            top = jnp.maximum(old_peak, peak)
            old_factor = jnp.exp2((old_peak - top) * rate)
            factor = jnp.exp2((peak - top) * rate)
            return (
                top,
                old_mass * old_factor + mass * factor,
                old_weighted * old_factor + weighted * factor,
            )

        peak, mass, weighted = lax.fori_loop(0, a + 1 - past, absorb, state[a])
        inverse_mass = 1.0 / mass
        fin[a, 0] = peak
        fin[a, 1] = inverse_mass
        fin[a, 2] = weighted * inverse_mass

    def settle(a, block):
        at = pl.ds(pl.multiple_of(block * T, T), T)
        factor = jnp.exp2((m_all[a, block] - fin[a, 0]) * rate) * fin[a, 1]
        attend = p_all[a, at, :] * factor
        d_scores = attend * (g_all[a, at, :] - fin[a, 2])
        return attend.astype(BF16), d_scores.astype(BF16)

    def homeward(src, dst, index, group=1):
        dst[i] = src[i]
        for r in (1, 3, 2):
            send(src.at[lax.rem(i + r, N)], dst.at[i], index, gdev(r), group)

    def norm_side(grad, raw, inv, gain):
        raw_full = raw.astype(F32)
        gained = grad * gain
        total = jnp.sum(fold8(grad * raw_full * inv), 0)
        return total, (gained * inv).astype(BF16), row_sum(gained * raw_full)

    gain_k_sum = jnp.zeros((8, HD), F32)
    for a in range(N):
        rows = slice(a * T, (a + 1) * T)
        attend, d_scores = settle(a, 0)
        dqt[a] = dot_nn(knt[a], d_scores)
        grad_k = dot_nn(d_scores, qn[rows, :]) * scale
        av[a] = dot_nn(attend, ho[rows, :]).astype(BF16)
        total, ak[a], pd[a, 1:2, :] = norm_side(grad_k, hk[rows, :], ick[rows, :], gain_k)
        gain_k_sum = gain_k_sum + total
    homeward(av, avh, DV)
    homeward(ak, akh, DK)

    last_parts = []
    for b in range(N):
        acc_k[...] = jnp.zeros((T, HD), F32)
        acc_v[...] = jnp.zeros((T, HD), F32)

        def add_up(a, nothing, b=b):
            rows = pl.ds(pl.multiple_of(a * T, T), T)
            attend, d_scores = settle(a, b + 1)
            acc_k[...] = acc_k[...] + dot_nn(d_scores, qn[rows, :])
            acc_v[...] = acc_v[...] + dot_nn(attend, ho[rows, :])
            dqt[a] = dqt[a] + dot_nn(mkt[b], d_scores)
            return nothing

        lax.fori_loop(b + past, N, add_up, 0)

        sbk[b] = (acc_k[...] * scale).astype(BF16).reshape(N, M, HD)
        sbv[b] = acc_v[...].astype(BF16).reshape(N, M, HD)
        for n, (sb, rb) in enumerate(((sbk, rbk), (sbv, rbv))):
            for r in (2, 1, 3):
                to = lax.rem(j + r, N)
                if b < N - 1:
                    send(sb.at[b, to], rb.at[j, b], DMEM + n, odev(r), 1)
                else:
                    index = 3 * n + r - 1
                    copy = remote(sb.at[b, to], rb.at[j, b], DMEM3 + index, odev(r), 4 + index)
                    pl.when(to < j)(copy.start)
                    last_parts.append((to < j, copy))

    gain_q_sum = jnp.zeros((8, HD), F32)
    for a in range(N):
        rows = slice(a * T, (a + 1) * T)
        grad_q = jnp.transpose(dqt[a]) * scale
        total, aq[a], pd[a, 0:1, :] = norm_side(grad_q, hq[rows, :], icq[rows, :], gain_q)
        gain_q_sum = gain_q_sum + total

    homeward(pd, pdh, PD, 3)
    homeward(aq, aqh, DQ)

    for m in range(N):
        at = slice(m * M, (m + 1) * M)
        acc_k[at, :] = sbk[m, j].astype(F32)
        acc_v[at, :] = sbv[m, j].astype(F32)
    for n in range(2):
        landed(DMEM + n, hv.at[0 : 9 * M, :])
    for r in (1, 3, 2):
        source = lax.rem(j + N - r, N)
        for n, (rb, acc) in enumerate(((rbk, acc_k), (rbv, acc_v))):
            at = slice(0, (N - 1) * M)
            acc[at, :] = acc[at, :] + rb[source, 0 : N - 1].reshape((N - 1) * M, HD).astype(F32)

            @pl.when(source > j)
            def _(source=source, n=n, r=r, rb=rb, acc=acc):
                landed(DMEM3 + 3 * n + r - 1, rb.at[source, N - 1])
                at = slice((N - 1) * M, N * M)
                acc[at, :] = acc[at, :] + rb[source, N - 1].astype(F32)

    grad_mem_k = acc_k[...].astype(BF16)
    grad_mem_v = acc_v[...].astype(BF16)

    square_k = dot_tn(ku[...], grad_mem_k)
    square_v = dot_tn(vu[...], grad_mem_v)
    for p in range(N):
        pay[0, p] = square_k[p * HD : (p + 1) * HD].astype(BF16)
        pay[1, p] = square_v[p * HD : (p + 1) * HD].astype(BF16)
    gmk[...] = grad_mem_k.reshape(N, M, HD)
    gmv[...] = grad_mem_v.reshape(N, M, HD)

    for p in range(N):
        send(pay.at[1 - c, p], rsi.at[1, j], RSX, cross(p), 2)
    for r in (1, 3, 2):
        send(pay.at[c, lax.rem(j + r, N)], rsi.at[0, j], RS, odev(r), 2)
    homeward(gmk, gmkh, GM)
    homeward(gmv, gmvh, GM + 1)

    crossed = square_k[0:HD] * wk_ref[i, 0:HD, :].astype(F32)
    for p in range(1, N):
        at = slice(p * HD, (p + 1) * HD)
        crossed = crossed + square_k[at] * wk_ref[i, at, :].astype(F32)
    gmine[0:1, :] = jnp.sum(gain_q_sum, 0, keepdims=True)
    gmine[1:2, :] = jnp.sum(gain_k_sum, 0, keepdims=True) + row_sum(crossed) / gain_k
    for r in (1, 3, 2):
        send(gmine, gsame.at[j], GR, odev(r), 3)
    for p in range(N):
        send(gmine, gother.at[j], GRX, cross(p), 3)

    landed(GM, gmkh.at[0:3])
    landed(GM + 1, gmvh.at[0:3])
    product = jnp.zeros((T, HD), F32)
    for h in range(N):
        spread_k = dot_nt(gmkh[h], wk_ref[h])
        spread_v = dot_nt(gmvh[h], wv_ref[h])
        for n in range(KS):
            at = pl.ds(n, M, stride=KS)
            cols = slice(n * HD, (n + 1) * HD)
            bkf[h, at, :] = spread_k[:, cols]
            bvf[h, at, :] = spread_v[:, cols]
        gained = bkf[h] * gk_ref[h]
        bkf[h] = gained
        product = product + gained * k_ref[:, h * HD : (h + 1) * HD].astype(F32)

    landed(PD, pdh.at[0:3])
    total = pdh[0]
    for h in range(1, N):
        total = total + pdh[h]
    zs2[z, 0:1, :] = total[0:1]
    zs2[z, 1:2, :] = total[1:2] + row_sum(product)
    for r in range(1, nz):
        send(zs2.at[z], zs2.at[z], Z2, zdev(r), 3)

    landed(RSX, rsi.at[1])
    landed(RS, rsi.at[0, 0:3])
    total = pay[c, j].astype(F32)
    for r in (1, 2, 3):
        total = total + rsi[0, lax.rem(j + r, N)].astype(F32)
    for p in range(N):
        total = total + rsi[1, p].astype(F32)
    full[c, far, near] = total.astype(BF16)
    mine = full.at[c, far, near]
    for n, r in enumerate((1, 3, 2)):
        send(mine, mine, AGG + n, ndev(r), 2)

    def pass_on(slot, member):
        piece = full.at[c, far, member]
        for r in (1, 3, 2):
            send(piece, piece, AGO + slot, fdev(r), 2)
        send(piece, piece, C2 + slot, cdev, 2)
        emit(c, far, member)

    pass_on(0, near)

    landed(GR, gsame.at[0:3])
    landed(GRX, gother)
    total = gmine[...]
    for r in (1, 2, 3):
        total = total + gsame[lax.rem(j + r, N)]
    for p in range(N):
        total = total + gother[p]
    gall[i] = total
    for r in (1, 3, 2):
        send(gall.at[i], gall.at[i], GG, gdev(r), 3)

    for n, r in enumerate((1, 3, 2)):
        landed(AGG + n, mine)
        pass_on(n + 1, lax.rem(near + N - r, N))

    landed(Z2, zs2.at[0 : nz - 1])
    total = zs2[0]
    for r in range(1, nz):
        total = total + zs2[r]
    inverse = lax.rsqrt(gs[i] * (1.0 / hh) + EPS)
    shift = inverse * inverse * inverse * total * (1.0 / hh)
    shift_q = as_column(shift[0:1])
    shift_k = as_column(shift[1:2])
    for index in (DQ, DK, DV):
        landed(index, aqh.at[0:3])
    inverse_k = as_column(inverse[1:2])
    for h in range(N):
        cols = slice(h * HD, (h + 1) * HD)
        dq_buf[:, cols] = (aqh[h].astype(F32) - q_ref[:, cols].astype(F32) * shift_q).astype(BF16)
        grad_k = akh[h].astype(F32) + bkf[h] * inverse_k
        dk_buf[:, cols] = (grad_k - k_ref[:, cols].astype(F32) * shift_k).astype(BF16)
        dv_buf[:, cols] = (avh[h].astype(F32) + bvf[h]).astype(BF16)
    for n, (buf, out) in enumerate(((dq_buf, dq_out), (dk_buf, dk_out), (dv_buf, dv_out))):
        write(buf, out, 1 + n)
    landed(GG, gall.at[0:3])
    for h in range(N):
        gain_buf[0, h] = gall[h, 0:1, :]
        gain_buf[1, h] = gall[h, 1:2, :]
    write(gain_buf, gain_out, 4)

    for slot, back in enumerate((0, 1, 3, 2)):
        landed(AGO + slot, full.at[c, 0:3, 0])
        member = lax.rem(near + N - back, N)
        for r in (1, 3, 2):
            at = full.at[c, lax.rem(far + N - r, N), member]
            send(at, at, C2 + 4 + slot, cdev, 2)
        for r in (1, 3, 2):
            emit(c, lax.rem(far + N - r, N), member)

    for slot, back in enumerate((0, 1, 3, 2)):
        landed(C2 + slot, mine)
        emit(1 - c, near, lax.rem(far + N - back, N))
    for slot, back in enumerate((0, 1, 3, 2)):
        landed(C2 + 4 + slot, full.at[c, 0:3, 0])
        for r in (1, 3, 2):
            emit(1 - c, lax.rem(near + N - r, N), lax.rem(far + N - back, N))

    for group, size in enumerate(sent):
        if group < 3:
            rows = size // (4 * T)
            assert rows * 4 * T == size and rows % 8 == 0
            space = p_all.at[0, 0:rows, :]
        else:
            assert size == tally.shape[0] * 8 * T
            space = tally
        remote(space, space, 0, cdev, group).wait_send()
    for needed, copy in last_parts:
        pl.when(needed)(copy.wait_send)
    pltpu.make_async_copy(kern, kern_out, out_sem.at[0]).wait()
    for copy in written:
        copy.wait()


def finish(
    dq_ref, dk_ref, dv_ref, kern_ref, gain_ref,
    dq_out, dk_out, dv_out, qg_out, kg_out, sk_out, sv_out,
    sems,
):
    pairs = [(kern_ref.at[0, h], sk_out.at[h]) for h in range(N)]
    pairs += [(kern_ref.at[1, h], sv_out.at[h]) for h in range(N)]
    pairs += [(dq_ref, dq_out), (dk_ref, dk_out), (dv_ref, dv_out)]
    pairs += [(gain_ref.at[0], qg_out), (gain_ref.at[1], kg_out)]
    copies = [pltpu.make_async_copy(src, dst, sems.at[n]) for n, (src, dst) in enumerate(pairs)]
    for copy in copies:
        copy.start()
    for copy in copies:
        copy.wait()


def on_device(nz, q, k, v, query_gain, key_gain, key_squeeze, value_squeeze, o):
    width = N * HD
    bf = functools.partial(pltpu.VMEM, dtype=BF16)
    ff = functools.partial(pltpu.VMEM, dtype=F32)
    rows = N * T
    deep = (N + 1) * T
    scratch = [ff((N, 1, HD))] * 2 + [bf((T, width))] * 3
    scratch += [ff((2, N, KS * HD, HD)), ff((2, N, 1, HD))]
    scratch += [bf((T, width))] * 4 + [bf((N, KS * HD, HD))] * 2
    scratch += [bf((rows, HD))] * 4 + [bf((rows, HD))] * 2 + [ff((rows, HD))] * 2
    scratch += [ff((rows, HD)), bf((N * M, KS * HD)), bf((N * M, KS * HD))]
    scratch += [ff((N, 2, T)), ff((nz, N, 2, T)), ff((N, 2, T))]
    scratch += [bf((N, N, M, HD))] * 2 + [bf((N, N * M, HD))] * 2
    scratch += [ff((N, deep, T))] * 2 + [ff((N, N + 1, 1, T)), ff((N, 3, 1, T))]
    scratch += [bf((N, HD, T))] * 2 + [ff((N, HD, T))]
    scratch += [ff((N * M, HD))] * 2 + [bf((N, N, M, HD))] * 4
    scratch += [bf((N, T, HD))] * 3 + [ff((N, 2, T))]
    scratch += [bf((N, T, HD))] * 3 + [ff((N, 2, T)), ff((nz, 2, T))]
    scratch += [bf((N, M, HD))] * 4 + [ff((N, T, HD))] * 2
    scratch += [ff((2, HD))] + [ff((N, 2, HD))] * 3
    scratch += [bf((2, N, HD, HD))] * 2 + [bf((2, N, N, HD, HD))]
    scratch += [ff((18, 2, T))]
    scratch += [
        pltpu.SemaphoreType.DMA((N_SEND,)),
        pltpu.SemaphoreType.DMA((N_RECV,)),
        pltpu.SemaphoreType.DMA((12,)),
        pltpu.SemaphoreType.DMA((5,)),
    ]
    anywhere = pl.BlockSpec(memory_space=pl.ANY)
    hbm = pl.BlockSpec(memory_space=pltpu.MemorySpace.HBM)
    stay = functools.partial(
        pltpu.with_memory_space_constraint, memory_space=pltpu.MemorySpace.HBM
    )
    grads = [jax.ShapeDtypeStruct((T, width), BF16)] * 3
    outs = pl.pallas_call(
        functools.partial(kernel, nz),
        out_shape=grads
        + [
            jax.ShapeDtypeStruct((2, N, KS * HD, HD), F32),
            jax.ShapeDtypeStruct((2, N, 1, HD), F32),
        ],
        in_specs=[hbm] * 8,
        out_specs=[anywhere] * 5,
        scratch_shapes=scratch,
        compiler_params=pltpu.CompilerParams(
            collective_id=0, has_side_effects=True, vmem_limit_bytes=40 * 2**20
        ),
    )(
        stay(q[0]), stay(k[0]), stay(v[0]), stay(o[0]),
        stay(query_gain.reshape(N, 1, HD)), stay(key_gain.reshape(N, 1, HD)),
        stay(key_squeeze), stay(value_squeeze),
    )
    kernels = jax.ShapeDtypeStruct((N, KS * HD, HD), F32)
    gains = jax.ShapeDtypeStruct((N, 1, HD), F32)
    dq, dk, dv, qg, kg, sk, sv = pl.pallas_call(
        finish,
        out_shape=grads + [gains] * 2 + [kernels] * 2,
        in_specs=[anywhere] * 5,
        out_specs=[hbm] * 7,
        scratch_shapes=[pltpu.SemaphoreType.DMA((13,))],
        compiler_params=pltpu.CompilerParams(vmem_limit_bytes=16 * 2**20),
    )(*outs)
    return dq[None], dk[None], dv[None], qg.reshape(width), kg.reshape(width), sk, sv


def solution(mesh):
    by_token = P("dp", "seq", "head")
    by_head = P("head", None, None)
    return jax.shard_map(
        functools.partial(on_device, mesh.shape["head"]),
        mesh=mesh,
        in_specs=(by_token,) * 3 + (P("head"), P("head"), by_head, by_head, by_token),
        out_specs=(by_token,) * 3 + (P("head"), P("head"), by_head, by_head),
        check_vma=False,
    )
```

```python
import functools

import jax
import jax.numpy as jnp
from jax import lax
from jax.experimental import pallas as pl
from jax.experimental.pallas import tpu as pltpu
from jax.sharding import PartitionSpec as P

HD = 128
KS = 4
N = 4
T = 256
M = 64
EPS = 1e-06
NEG = -1e30
LOG2E = 1.4426950408889634
MESH = pl.DeviceIdType.MESH
F32 = jnp.float32
BF16 = jnp.bfloat16

A2A = 0
Z1 = A2A + 4
G1 = Z1 + 1
MEM = G1 + 1
DMEM = MEM + 2
DMEM3 = DMEM + 2
DQ = DMEM3 + 6
DK = DQ + 1
DV = DK + 1
PD = DV + 1
Z2 = PD + 1
RS = Z2 + 1
RSX = RS + 1
AGG = RSX + 1
AGO = AGG + 3
C2 = AGO + 4
GM = C2 + 8
GR = GM + 2
GRX = GR + 1
GG = GRX + 1
N_RECV = GG + 1
N_SEND = 4 + 6


def dot_nt(a, b):
    return lax.dot_general(a, b, (((1,), (1,)), ((), ())), preferred_element_type=F32)


def dot_tn(a, b):
    return lax.dot_general(a, b, (((0,), (0,)), ((), ())), preferred_element_type=F32)


def dot_nn(a, b):
    return lax.dot_general(a, b, (((1,), (0,)), ((), ())), preferred_element_type=F32)


def as_column(row):
    return jnp.transpose(jnp.broadcast_to(row, (HD, row.shape[1])))


def row_sum(block):
    return jnp.sum(jnp.transpose(block), 0, keepdims=True)


def fold8(block):
    return block.reshape(block.shape[0] // 8, 8, block.shape[1])


def kernel(
    nz,
    q_hbm, k_hbm, v_hbm, o_hbm, gq_hbm, gk_hbm, wk_hbm, wv_hbm,
    dq_out, dk_out, dv_out, kern_out, gain_out,
    gq_ref, gk_ref, q_ref, k_ref, v_ref, o_ref, wk_ref, wv_ref,
    hq, hk, hv, ho, qn, kn, icq, ick, fs, ku, vu, gsp, zs, gs, mkg, mvg, mkc, mvc,
    p_all, g_all, m_all, fin, mkt, knt, dqt, acc_k, acc_v, sbk, sbv, rbk, rbv,
    aq, ak, av, pd, aqh, akh, avh, pdh, zs2,
    gmk, gmv, gmkh, gmvh, bkf, bvf, gmine, gsame, gother, gall,
    pay, rsi, full, tally,
    ss, rs, loc,
):
    seq = lax.axis_index("seq")
    x = lax.rem(seq, N)
    y = lax.div(seq, N)
    z = lax.axis_index("head")
    c = lax.axis_index("dp")
    i = y
    j = x
    near = i + c * (j - i)
    far = j + c * (i - j)
    hh = nz * N * HD
    scale = HD ** (-0.5)

    def gdev(r):
        return {"seq": lax.rem(i + r, N) * N + j}

    def odev(r):
        return {"seq": i * N + lax.rem(j + r, N)}

    def ndev(r):
        to = lax.rem(near + r, N)
        return {"seq": to * (N - (N - 1) * c) + far * (1 + (N - 1) * c)}

    def fdev(r):
        to = lax.rem(far + r, N)
        return {"seq": near * (N - (N - 1) * c) + to * (1 + (N - 1) * c)}

    def cross(p):
        return {"seq": i * N + p, "dp": 1 - c}

    def zdev(r):
        return {"head": lax.rem(z + r, nz)}

    cdev = {"dp": 1 - c}

    def remote(src, dst, index, device, group):
        return pltpu.make_async_remote_copy(
            src_ref=src,
            dst_ref=dst,
            send_sem=ss.at[group],
            recv_sem=rs.at[index],
            device_id=device,
            device_id_type=MESH,
        )

    sent = [0, 0, 0, 0]

    def send(src, dst, index, device, group):
        remote(src, dst, index, device, group).start()
        size = 1
        for length in src.shape:
            size = size * length
        sent[group] += size * src.dtype.itemsize

    def landed(index, space):
        remote(space, space, index, cdev, 0).wait_recv()

    def emit(core, across, along):
        head = along + core * (across - along)
        rows = pl.ds(pl.multiple_of((across + core * (along - across)) * HD, HD), HD)
        kern_out[core, head, rows, :] = full[core, across, along].astype(F32)

    barrier = pltpu.get_barrier_semaphore()
    peers = [gdev(r) for r in (1, 2, 3)] + [odev(r) for r in (1, 2, 3)]
    peers += [zdev(r) for r in range(1, nz)] + [cross(p) for p in range(N)] + [cdev]
    for peer in peers:
        pl.semaphore_signal(barrier, inc=1, device_id=peer, device_id_type=MESH)

    loads = [
        pltpu.make_async_copy(src, dst, loc.at[4 + n])
        for n, (src, dst) in enumerate(
            (
                (q_hbm, q_ref), (k_hbm, k_ref), (v_hbm, v_ref), (o_hbm, o_ref),
                (wv_hbm, wv_ref), (wk_hbm, wk_ref),
                (gq_hbm, gq_ref), (gk_hbm, gk_ref),
            )
        )
    ]
    for copy in loads:
        copy.start()

    for row, ref in ((0, q_ref), (1, k_ref)):
        loads[row].wait()
        full_rows = ref[...].astype(F32)
        squares = full_rows * full_rows
        folded = squares[:, :HD]
        for h in range(1, N):
            folded = folded + squares[:, h * HD : (h + 1) * HD]
        gsp[i, row : row + 1, :] = row_sum(folded)
    for copy in loads[2:4]:
        copy.wait()

    pl.semaphore_wait(barrier, len(peers))

    for r in (2, 1, 3):
        send(gsp.at[i], gsp.at[i], G1, gdev(r), 3)
    rows_mine = pl.ds(pl.multiple_of(i * T, T), T)
    own = {}

    def exchange(n, src, dst):
        for r in (2, 1, 3):
            cols = pl.ds(pl.multiple_of(lax.rem(i + r, N) * HD, HD), HD)
            send(src.at[:, cols], dst.at[rows_mine, :], A2A + n, gdev(r), 0)
        cols = pl.ds(pl.multiple_of(i * HD, HD), HD)
        own[n] = pltpu.make_async_copy(src.at[:, cols], dst.at[rows_mine, :], loc.at[n])
        own[n].start()

    def arrived(n):
        landed(A2A + n, hv.at[0 : 3 * T, :])
        own[n].wait()

    exchange(0, v_ref, hv)
    exchange(1, k_ref, hk)

    exchange(2, q_ref, hq)
    exchange(3, o_ref, ho)

    landed(G1, gsp.at[0:3])
    for r in range(1, nz):
        send(gsp, zs.at[z], Z1, zdev(r), 0)
    for copy in loads[4:]:
        copy.wait()

    def unfold(dst):
        for n in range(KS):
            dst[:, n * HD : (n + 1) * HD] = fs[pl.ds(n, N * M, stride=KS), :].astype(BF16)

    def spread(mem, value, index):
        mem[j] = value.astype(BF16).reshape(N, M, HD)
        for r in (2, 1, 3):
            send(mem.at[j], mem.at[j], MEM + index, odev(r), 0)

    arrived(0)
    fs[...] = hv[...].astype(F32)
    unfold(vu)
    spread(mvg, dot_nn(vu[...], wv_ref[i]), 1)

    landed(Z1, zs.at[0 : nz - 1])
    gs[...] = gsp[...]
    for r in range(1, nz):
        gs[...] = gs[...] + zs[lax.rem(z + r, nz)]
    gain_q = gq_ref[i]
    gain_k = gk_ref[i]
    arrived(1)
    for a in range(N):
        rows = slice(a * T, (a + 1) * T)
        inverse = lax.rsqrt(gs[a] * (1.0 / hh) + EPS)
        icq[rows, :] = as_column(inverse[0:1])
        ick[rows, :] = as_column(inverse[1:2])
        normed = (hk[rows, :].astype(F32) * ick[rows, :] * gain_k).astype(BF16)
        kn[rows, :] = normed
        fs[rows, :] = normed.astype(F32)
    unfold(ku)
    spread(mkg, dot_nn(ku[...], wk_ref[i]), 0)

    arrived(2)
    arrived(3)
    key_at = lax.broadcasted_iota(jnp.int32, (T, T), 0)
    query_at = lax.broadcasted_iota(jnp.int32, (T, T), 1)
    rate = scale * LOG2E

    def score(a, block, mask, keys, values):
        at = pl.ds(pl.multiple_of(block * T, T), T)
        rows = slice(a * T, (a + 1) * T)
        scores = dot_nt(keys, qn[rows, :])
        if mask is not None:
            scores = jnp.where(mask, scores, NEG)
        grads = dot_nt(values, ho[rows, :])
        peak = jnp.max(jnp.max(fold8(scores), 0), 0, keepdims=True)
        lifted = jnp.exp2((scores - peak) * rate)
        p_all[a, at, :] = lifted
        g_all[a, at, :] = grads
        m_all[a, block] = peak
        mass = jnp.sum(jnp.sum(fold8(lifted), 0), 0, keepdims=True)
        weighted = jnp.sum(jnp.sum(fold8(lifted * grads), 0), 0, keepdims=True)
        return peak, mass, weighted

    state = []
    for a in range(N):
        rows = slice(a * T, (a + 1) * T)
        qn[rows, :] = (hq[rows, :].astype(F32) * icq[rows, :] * gain_q).astype(BF16)
        state.append(score(a, 0, key_at <= query_at, kn[rows, :], hv[rows, :]))
        knt[a] = jnp.transpose(kn[rows, :])

    landed(MEM, mkg.at[0:3])
    landed(MEM + 1, mvg.at[0:3])
    for b in range(N):
        for t in range(N):
            at = slice(t * M, (t + 1) * M)
            mkc[b, at, :] = mkg[t, b]
            mvc[b, at, :] = mvg[t, b]
        mkt[b] = jnp.transpose(mkc[b])

    past = jnp.where(j > 0, 0, 1)

    for a in range(N):

        def absorb(b, current, a=a):
            old_peak, old_mass, old_weighted = current
            mask = None if isinstance(b, int) else key_at < j * M
            peak, mass, weighted = score(a, b + 1, mask, mkc[b], mvc[b])
            top = jnp.maximum(old_peak, peak)
            old_factor = jnp.exp2((old_peak - top) * rate)
            factor = jnp.exp2((peak - top) * rate)
            return (
                top,
                old_mass * old_factor + mass * factor,
                old_weighted * old_factor + weighted * factor,
            )

        current = state[a]
        for b in range(a):
            current = absorb(b, current)
        peak, mass, weighted = lax.fori_loop(a + past, a + 1, absorb, current)
        inverse_mass = 1.0 / mass
        fin[a, 0] = peak
        fin[a, 1] = inverse_mass
        fin[a, 2] = weighted * inverse_mass

    def settle(a, block):
        at = pl.ds(pl.multiple_of(block * T, T), T)
        factor = jnp.exp2((m_all[a, block] - fin[a, 0]) * rate) * fin[a, 1]
        attend = p_all[a, at, :] * factor
        d_scores = attend * (g_all[a, at, :] - fin[a, 2])
        return attend.astype(BF16), d_scores.astype(BF16)

    def homeward(src, dst, index, group=1):
        dst[i] = src[i]
        for r in (1, 3, 2):
            send(src.at[lax.rem(i + r, N)], dst.at[i], index, gdev(r), group)

    def norm_side(grad, raw, inv, gain):
        raw_full = raw.astype(F32)
        gained = grad * gain
        total = jnp.sum(fold8(grad * raw_full * inv), 0)
        return total, (gained * inv).astype(BF16), row_sum(gained * raw_full)

    last_parts = []
    for b in range(N):
        after = range(b + 1, N)
        settled = [settle(a, b + 1) for a in after]
        for a, (_, d_scores) in zip(after, settled):
            part = dot_nn(mkt[b], d_scores)
            dqt[a] = part if b == 0 else dqt[a] + part
        if settled:
            rows = slice((b + 1) * T, N * T)
            acc_k[...] = dot_nn(jnp.concatenate([d for _, d in settled], 1), qn[rows, :])
            acc_v[...] = dot_nn(jnp.concatenate([p for p, _ in settled], 1), ho[rows, :])
        else:
            acc_k[...] = jnp.zeros((T, HD), F32)
            acc_v[...] = jnp.zeros((T, HD), F32)
        if b == 0:
            dqt[0] = jnp.zeros((HD, T), F32)

        @pl.when(j > 0)
        def _(b=b):
            rows = slice(b * T, (b + 1) * T)
            attend, d_scores = settle(b, b + 1)
            acc_k[...] = acc_k[...] + dot_nn(d_scores, qn[rows, :])
            acc_v[...] = acc_v[...] + dot_nn(attend, ho[rows, :])
            dqt[b] = dqt[b] + dot_nn(mkt[b], d_scores)

        sbk[b] = (acc_k[...] * scale).astype(BF16).reshape(N, M, HD)
        sbv[b] = acc_v[...].astype(BF16).reshape(N, M, HD)
        for n, (sb, rb) in enumerate(((sbk, rbk), (sbv, rbv))):
            for r in (2, 1, 3):
                to = lax.rem(j + r, N)
                if b < N - 1:
                    send(sb.at[b, to], rb.at[j, b], DMEM + n, odev(r), 1)
                else:
                    index = 3 * n + r - 1
                    copy = remote(sb.at[b, to], rb.at[j, b], DMEM3 + index, odev(r), 4 + index)
                    pl.when(to < j)(copy.start)
                    last_parts.append((to < j, copy))

    gain_k_sum = jnp.zeros((8, HD), F32)
    for a in range(N):
        rows = slice(a * T, (a + 1) * T)
        attend, d_scores = settle(a, 0)
        dqt[a] = dqt[a] + dot_nn(knt[a], d_scores)
        grad_k = dot_nn(d_scores, qn[rows, :]) * scale
        av[a] = dot_nn(attend, ho[rows, :]).astype(BF16)
        total, ak[a], pd[a, 1:2, :] = norm_side(grad_k, hk[rows, :], ick[rows, :], gain_k)
        gain_k_sum = gain_k_sum + total
    homeward(av, avh, DV)
    homeward(ak, akh, DK)

    gain_q_sum = jnp.zeros((8, HD), F32)
    for a in range(N):
        rows = slice(a * T, (a + 1) * T)
        grad_q = jnp.transpose(dqt[a]) * scale
        total, aq[a], pd[a, 0:1, :] = norm_side(grad_q, hq[rows, :], icq[rows, :], gain_q)
        gain_q_sum = gain_q_sum + total

    homeward(pd, pdh, PD, 3)
    homeward(aq, aqh, DQ)

    for m in range(N):
        at = slice(m * M, (m + 1) * M)
        acc_k[at, :] = sbk[m, j].astype(F32)
        acc_v[at, :] = sbv[m, j].astype(F32)
    for n in range(2):
        landed(DMEM + n, hv.at[0 : 9 * M, :])
    for r in (1, 3, 2):
        source = lax.rem(j + N - r, N)
        for n, (rb, acc) in enumerate(((rbk, acc_k), (rbv, acc_v))):
            at = slice(0, (N - 1) * M)
            acc[at, :] = acc[at, :] + rb[source, 0 : N - 1].reshape((N - 1) * M, HD).astype(F32)

            @pl.when(source > j)
            def _(source=source, n=n, r=r, rb=rb, acc=acc):
                landed(DMEM3 + 3 * n + r - 1, rb.at[source, N - 1])
                at = slice((N - 1) * M, N * M)
                acc[at, :] = acc[at, :] + rb[source, N - 1].astype(F32)

    grad_mem_k = acc_k[...].astype(BF16)
    grad_mem_v = acc_v[...].astype(BF16)

    square_k = dot_tn(ku[...], grad_mem_k)
    square_v = dot_tn(vu[...], grad_mem_v)
    for p in range(N):
        pay[0, p] = square_k[p * HD : (p + 1) * HD].astype(BF16)
        pay[1, p] = square_v[p * HD : (p + 1) * HD].astype(BF16)
    gmk[...] = grad_mem_k.reshape(N, M, HD)
    gmv[...] = grad_mem_v.reshape(N, M, HD)

    for r in (2, 1, 3):
        to = lax.rem(j + r, N)
        send(pay.at[1 - c, to], rsi.at[1, j], RSX, cross(to), 2)
        send(pay.at[c, to], rsi.at[0, j], RS, odev(r), 2)
    send(pay.at[1 - c, j], rsi.at[1, j], RSX, cross(j), 2)
    homeward(gmk, gmkh, GM)
    homeward(gmv, gmvh, GM + 1)

    crossed = square_k[0:HD] * wk_ref[i, 0:HD, :].astype(F32)
    for p in range(1, N):
        at = slice(p * HD, (p + 1) * HD)
        crossed = crossed + square_k[at] * wk_ref[i, at, :].astype(F32)
    gmine[0:1, :] = jnp.sum(gain_q_sum, 0, keepdims=True)
    gmine[1:2, :] = jnp.sum(gain_k_sum, 0, keepdims=True) + row_sum(crossed) / gain_k
    for r in (1, 3, 2):
        send(gmine, gsame.at[j], GR, odev(r), 3)
    for p in range(N):
        send(gmine, gother.at[j], GRX, cross(p), 3)

    landed(RSX, rsi.at[1])
    landed(RS, rsi.at[0, 0:3])
    total = pay[c, j].astype(F32)
    for r in (1, 2, 3):
        total = total + rsi[0, lax.rem(j + r, N)].astype(F32)
    for p in range(N):
        total = total + rsi[1, p].astype(F32)
    full[c, far, near] = total.astype(BF16)
    mine = full.at[c, far, near]
    for n, r in enumerate((1, 3, 2)):
        send(mine, mine, AGG + n, ndev(r), 2)

    def pass_on(slot, member):
        piece = full.at[c, far, member]
        for r in (2, 1, 3):
            send(piece, piece, AGO + slot, fdev(r), 2)
        send(piece, piece, C2 + slot, cdev, 2)
        emit(c, far, member)

    pass_on(0, near)

    landed(GR, gsame.at[0:3])
    landed(GRX, gother)
    total = gmine[...]
    for r in (1, 2, 3):
        total = total + gsame[lax.rem(j + r, N)]
    for p in range(N):
        total = total + gother[p]
    gall[i] = total
    for r in (1, 3, 2):
        send(gall.at[i], gall.at[i], GG, gdev(r), 3)

    landed(GM, gmkh.at[0:3])
    landed(GM + 1, gmvh.at[0:3])
    product = jnp.zeros((T, HD), F32)
    for h in range(N):
        spread_k = dot_nt(gmkh[h], wk_ref[h])
        spread_v = dot_nt(gmvh[h], wv_ref[h])
        for n in range(KS):
            at = pl.ds(n, M, stride=KS)
            cols = slice(n * HD, (n + 1) * HD)
            bkf[h, at, :] = spread_k[:, cols]
            bvf[h, at, :] = spread_v[:, cols]
        gained = bkf[h] * gk_ref[h]
        bkf[h] = gained
        product = product + gained * k_ref[:, h * HD : (h + 1) * HD].astype(F32)

    landed(PD, pdh.at[0:3])
    total = pdh[0]
    for h in range(1, N):
        total = total + pdh[h]
    zs2[z, 0:1, :] = total[0:1]
    zs2[z, 1:2, :] = total[1:2] + row_sum(product)
    for r in range(1, nz):
        send(zs2.at[z], zs2.at[z], Z2, zdev(r), 3)

    for n, r in enumerate((1, 3, 2)):
        landed(AGG + n, mine)
        pass_on(n + 1, lax.rem(near + N - r, N))

    for slot, back in enumerate((0, 1, 3, 2)):
        landed(AGO + slot, full.at[c, 0:3, 0])
        member = lax.rem(near + N - back, N)
        for r in (1, 3, 2):
            at = full.at[c, lax.rem(far + N - r, N), member]
            send(at, at, C2 + 4 + slot, cdev, 2)
        for r in (1, 3, 2):
            emit(c, lax.rem(far + N - r, N), member)
        landed(C2 + slot, mine)
        emit(1 - c, near, lax.rem(far + N - back, N))

    landed(Z2, zs2.at[0 : nz - 1])
    total = zs2[0]
    for r in range(1, nz):
        total = total + zs2[r]
    inverse = lax.rsqrt(gs[i] * (1.0 / hh) + EPS)
    shift = inverse * inverse * inverse * total * (1.0 / hh)
    shift_q = as_column(shift[0:1])
    shift_k = as_column(shift[1:2])
    for index in (DQ, DK, DV):
        landed(index, aqh.at[0:3])
    inverse_k = as_column(inverse[1:2])
    for h in range(N):
        cols = slice(h * HD, (h + 1) * HD)
        dq_out[:, cols] = (aqh[h].astype(F32) - q_ref[:, cols].astype(F32) * shift_q).astype(BF16)
        grad_k = akh[h].astype(F32) + bkf[h] * inverse_k
        dk_out[:, cols] = (grad_k - k_ref[:, cols].astype(F32) * shift_k).astype(BF16)
        dv_out[:, cols] = (avh[h].astype(F32) + bvf[h]).astype(BF16)
    landed(GG, gall.at[0:3])
    for h in range(N):
        gain_out[0, h] = gall[h, 0:1, :]
        gain_out[1, h] = gall[h, 1:2, :]

    for slot, back in enumerate((0, 1, 3, 2)):
        landed(C2 + 4 + slot, full.at[c, 0:3, 0])
        for r in (1, 3, 2):
            emit(1 - c, lax.rem(near + N - r, N), lax.rem(far + N - back, N))

    for group, size in enumerate(sent):
        if group < 3:
            rows = size // (4 * T)
            assert rows * 4 * T == size and rows % 8 == 0
            space = p_all.at[0, 0:rows, :]
        else:
            assert size == tally.shape[0] * 8 * T
            space = tally
        remote(space, space, 0, cdev, group).wait_send()
    for needed, copy in last_parts:
        pl.when(needed)(copy.wait_send)


def finish(
    dq_ref, dk_ref, dv_ref, kern_ref, gain_ref,
    dq_out, dk_out, dv_out, qg_out, kg_out, sk_out, sv_out,
    sems,
):
    pairs = [(kern_ref.at[0, h], sk_out.at[h]) for h in range(N)]
    pairs += [(kern_ref.at[1, h], sv_out.at[h]) for h in range(N)]
    pairs += [(dq_ref, dq_out), (dk_ref, dk_out), (dv_ref, dv_out)]
    pairs += [(gain_ref.at[0], qg_out), (gain_ref.at[1], kg_out)]
    copies = [pltpu.make_async_copy(src, dst, sems.at[n]) for n, (src, dst) in enumerate(pairs)]
    for copy in copies:
        copy.start()
    for copy in copies:
        copy.wait()


def on_device(nz, q, k, v, query_gain, key_gain, key_squeeze, value_squeeze, o):
    width = N * HD
    bf = functools.partial(pltpu.VMEM, dtype=BF16)
    ff = functools.partial(pltpu.VMEM, dtype=F32)
    rows = N * T
    deep = (N + 1) * T
    scratch = [ff((N, 1, HD))] * 2
    scratch += [bf((T, width))] * 4 + [bf((N, KS * HD, HD))] * 2
    scratch += [bf((rows, HD))] * 4 + [bf((rows, HD))] * 2 + [ff((rows, HD))] * 2
    scratch += [ff((rows, HD)), bf((N * M, KS * HD)), bf((N * M, KS * HD))]
    scratch += [ff((N, 2, T)), ff((nz, N, 2, T)), ff((N, 2, T))]
    scratch += [bf((N, N, M, HD))] * 2 + [bf((N, N * M, HD))] * 2
    scratch += [ff((N, deep, T))] * 2 + [ff((N, N + 1, 1, T)), ff((N, 3, 1, T))]
    scratch += [bf((N, HD, T))] * 2 + [ff((N, HD, T))]
    scratch += [ff((N * M, HD))] * 2 + [bf((N, N, M, HD))] * 4
    scratch += [bf((N, T, HD))] * 3 + [ff((N, 2, T))]
    scratch += [bf((N, T, HD))] * 3 + [ff((N, 2, T)), ff((nz, 2, T))]
    scratch += [bf((N, M, HD))] * 4 + [ff((N, T, HD))] * 2
    scratch += [ff((2, HD))] + [ff((N, 2, HD))] * 3
    scratch += [bf((2, N, HD, HD))] * 2 + [bf((2, N, N, HD, HD))]
    scratch += [ff((18, 2, T))]
    scratch += [
        pltpu.SemaphoreType.DMA((N_SEND,)),
        pltpu.SemaphoreType.DMA((N_RECV,)),
        pltpu.SemaphoreType.DMA((12,)),
    ]
    vmem = pl.BlockSpec(memory_space=pltpu.VMEM)
    anywhere = pl.BlockSpec(memory_space=pl.ANY)
    hbm = pl.BlockSpec(memory_space=pltpu.MemorySpace.HBM)
    stay = functools.partial(
        pltpu.with_memory_space_constraint, memory_space=pltpu.MemorySpace.HBM
    )
    grads = [jax.ShapeDtypeStruct((T, width), BF16)] * 3
    outs = pl.pallas_call(
        functools.partial(kernel, nz),
        out_shape=grads
        + [
            jax.ShapeDtypeStruct((2, N, KS * HD, HD), F32),
            jax.ShapeDtypeStruct((2, N, 1, HD), F32),
        ],
        in_specs=[hbm] * 8,
        out_specs=[vmem] * 5,
        scratch_shapes=scratch,
        compiler_params=pltpu.CompilerParams(
            collective_id=0, has_side_effects=True, vmem_limit_bytes=40 * 2**20
        ),
    )(
        stay(q[0]), stay(k[0]), stay(v[0]), stay(o[0]),
        stay(query_gain.reshape(N, 1, HD)), stay(key_gain.reshape(N, 1, HD)),
        stay(key_squeeze), stay(value_squeeze),
    )
    kernels = jax.ShapeDtypeStruct((N, KS * HD, HD), F32)
    gains = jax.ShapeDtypeStruct((N, 1, HD), F32)
    dq, dk, dv, qg, kg, sk, sv = pl.pallas_call(
        finish,
        out_shape=grads + [gains] * 2 + [kernels] * 2,
        in_specs=[anywhere] * 5,
        out_specs=[hbm] * 7,
        scratch_shapes=[pltpu.SemaphoreType.DMA((13,))],
        compiler_params=pltpu.CompilerParams(vmem_limit_bytes=16 * 2**20),
    )(*outs)
    return dq[None], dk[None], dv[None], qg.reshape(width), kg.reshape(width), sk, sv


def solution(mesh):
    by_token = P("dp", "seq", "head")
    by_head = P("head", None, None)
    return jax.shard_map(
        functools.partial(on_device, mesh.shape["head"]),
        mesh=mesh,
        in_specs=(by_token,) * 3 + (P("head"), P("head"), by_head, by_head, by_token),
        out_specs=(by_token,) * 3 + (P("head"), P("head"), by_head, by_head),
        check_vma=False,
    )
```

```python
import functools

import jax
import jax.numpy as jnp
from jax import lax
from jax.experimental import pallas as pl
from jax.experimental.pallas import tpu as pltpu
from jax.sharding import PartitionSpec as P

HD = 128
KS = 4
N = 4
T = 256
M = 64
EPS = 1e-06
NEG = -1e30
LOG2E = 1.4426950408889634
MESH = pl.DeviceIdType.MESH
F32 = jnp.float32
BF16 = jnp.bfloat16

A2A = 0
Z1 = A2A + 4
G1 = Z1 + 1
MEM = G1 + 1
DMEM = MEM + 2
DMEM3 = DMEM + 2
DQ = DMEM3 + 6
DK = DQ + 1
DV = DK + 1
PD = DV + 1
Z2 = PD + 1
RS = Z2 + 1
RSX = RS + 1
AGG = RSX + 1
AGO = AGG + 3
C2 = AGO + 4
GM = C2 + 8
GR = GM + 2
GRX = GR + 1
GG = GRX + 1
N_RECV = GG + 1
N_SEND = 4 + 6


def dot_nt(a, b):
    return lax.dot_general(a, b, (((1,), (1,)), ((), ())), preferred_element_type=F32)


def dot_tn(a, b):
    return lax.dot_general(a, b, (((0,), (0,)), ((), ())), preferred_element_type=F32)


def dot_nn(a, b):
    return lax.dot_general(a, b, (((1,), (0,)), ((), ())), preferred_element_type=F32)


def as_column(row):
    return jnp.transpose(jnp.broadcast_to(row, (HD, row.shape[1])))


def row_sum(block):
    return jnp.sum(jnp.transpose(block), 0, keepdims=True)


def fold8(block):
    return block.reshape(block.shape[0] // 8, 8, block.shape[1])


def kernel(
    nz,
    q_hbm, k_hbm, v_hbm, o_hbm, gq_hbm, gk_hbm, wk_hbm, wv_hbm,
    dq_out, dk_out, dv_out, kern_out, gain_out,
    gq_ref, gk_ref, q_ref, k_ref, v_ref, o_ref, wk_ref, wv_ref,
    hq, hk, hv, ho, qn, kn, icq, ick, fs, ku, vu, gsp, zs, gs, mkg, mvg, mkc, mvc,
    p_all, g_all, m_all, fin, mkt, knt, dqt, acc_k, acc_v, sbk, sbv, rbk, rbv,
    aq, ak, av, pd, aqh, akh, avh, pdh, zs2,
    gmk, gmv, gmkh, gmvh, bkf, bvf, gmine, gsame, gother, gall,
    pay, rsi, full, tally,
    ss, rs, loc,
):
    seq = lax.axis_index("seq")
    x = lax.rem(seq, N)
    y = lax.div(seq, N)
    z = lax.axis_index("head")
    c = lax.axis_index("dp")
    i = y
    j = x
    near = i + c * (j - i)
    far = j + c * (i - j)
    hh = nz * N * HD
    scale = HD ** (-0.5)

    def gdev(r):
        return {"seq": lax.rem(i + r, N) * N + j}

    def odev(r):
        return {"seq": i * N + lax.rem(j + r, N)}

    def ndev(r):
        to = lax.rem(near + r, N)
        return {"seq": to * (N - (N - 1) * c) + far * (1 + (N - 1) * c)}

    def fdev(r):
        to = lax.rem(far + r, N)
        return {"seq": near * (N - (N - 1) * c) + to * (1 + (N - 1) * c)}

    def cross(p):
        return {"seq": i * N + p, "dp": 1 - c}

    def zdev(r):
        return {"head": lax.rem(z + r, nz)}

    cdev = {"dp": 1 - c}

    def remote(src, dst, index, device, group):
        return pltpu.make_async_remote_copy(
            src_ref=src,
            dst_ref=dst,
            send_sem=ss.at[group],
            recv_sem=rs.at[index],
            device_id=device,
            device_id_type=MESH,
        )

    sent = [0, 0, 0, 0]

    def send(src, dst, index, device, group):
        remote(src, dst, index, device, group).start()
        size = 1
        for length in src.shape:
            size = size * length
        sent[group] += size * src.dtype.itemsize

    def landed(index, space):
        remote(space, space, index, cdev, 0).wait_recv()

    def emit(core, across, along):
        head = along + core * (across - along)
        rows = pl.ds(pl.multiple_of((across + core * (along - across)) * HD, HD), HD)
        kern_out[core, head, rows, :] = full[core, across, along].astype(F32)

    barrier = pltpu.get_barrier_semaphore()
    peers = [gdev(r) for r in (1, 2, 3)] + [odev(r) for r in (1, 2, 3)]
    peers += [zdev(r) for r in range(1, nz)] + [cross(p) for p in range(N)] + [cdev]
    for peer in peers:
        pl.semaphore_signal(barrier, inc=1, device_id=peer, device_id_type=MESH)

    loads = [
        pltpu.make_async_copy(src, dst, loc.at[4 + n])
        for n, (src, dst) in enumerate(
            (
                (q_hbm, q_ref), (k_hbm, k_ref), (v_hbm, v_ref), (o_hbm, o_ref),
                (wv_hbm, wv_ref), (wk_hbm, wk_ref),
                (gq_hbm, gq_ref), (gk_hbm, gk_ref),
            )
        )
    ]
    for copy in loads:
        copy.start()

    for row, ref in ((0, q_ref), (1, k_ref)):
        loads[row].wait()
        full_rows = ref[...].astype(F32)
        squares = full_rows * full_rows
        folded = squares[:, :HD]
        for h in range(1, N):
            folded = folded + squares[:, h * HD : (h + 1) * HD]
        gsp[i, row : row + 1, :] = row_sum(folded)
    for copy in loads[2:4]:
        copy.wait()

    pl.semaphore_wait(barrier, len(peers))

    for r in (2, 1, 3):
        send(gsp.at[i], gsp.at[i], G1, gdev(r), 3)
    rows_mine = pl.ds(pl.multiple_of(i * T, T), T)
    own = {}

    def exchange(n, src, dst):
        for r in (2, 1, 3):
            cols = pl.ds(pl.multiple_of(lax.rem(i + r, N) * HD, HD), HD)
            send(src.at[:, cols], dst.at[rows_mine, :], A2A + n, gdev(r), 0)
        cols = pl.ds(pl.multiple_of(i * HD, HD), HD)
        own[n] = pltpu.make_async_copy(src.at[:, cols], dst.at[rows_mine, :], loc.at[n])
        own[n].start()

    def arrived(n):
        landed(A2A + n, hv.at[0 : 3 * T, :])
        own[n].wait()

    exchange(0, v_ref, hv)
    exchange(1, k_ref, hk)

    exchange(2, q_ref, hq)
    exchange(3, o_ref, ho)

    landed(G1, gsp.at[0:3])
    for r in range(1, nz):
        send(gsp, zs.at[z], Z1, zdev(r), 0)
    for copy in loads[4:]:
        copy.wait()

    def unfold(dst):
        for n in range(KS):
            dst[:, n * HD : (n + 1) * HD] = fs[pl.ds(n, N * M, stride=KS), :].astype(BF16)

    def spread(mem, value, index):
        mem[j] = value.astype(BF16).reshape(N, M, HD)
        for r in (2, 1, 3):
            send(mem.at[j], mem.at[j], MEM + index, odev(r), 0)

    arrived(0)
    fs[...] = hv[...].astype(F32)
    unfold(vu)
    spread(mvg, dot_nn(vu[...], wv_ref[i]), 1)

    landed(Z1, zs.at[0 : nz - 1])
    gs[...] = gsp[...]
    for r in range(1, nz):
        gs[...] = gs[...] + zs[lax.rem(z + r, nz)]
    gain_q = gq_ref[i]
    gain_k = gk_ref[i]
    arrived(1)
    for a in range(N):
        rows = slice(a * T, (a + 1) * T)
        inverse = lax.rsqrt(gs[a] * (1.0 / hh) + EPS)
        icq[rows, :] = as_column(inverse[0:1])
        ick[rows, :] = as_column(inverse[1:2])
        normed = (hk[rows, :].astype(F32) * ick[rows, :] * gain_k).astype(BF16)
        kn[rows, :] = normed
        fs[rows, :] = normed.astype(F32)
    unfold(ku)
    spread(mkg, dot_nn(ku[...], wk_ref[i]), 0)

    arrived(2)
    arrived(3)
    key_at = lax.broadcasted_iota(jnp.int32, (T, T), 0)
    query_at = lax.broadcasted_iota(jnp.int32, (T, T), 1)
    rate = scale * LOG2E

    def score(a, block, mask, keys, values):
        at = pl.ds(pl.multiple_of(block * T, T), T)
        rows = slice(a * T, (a + 1) * T)
        scores = dot_nt(keys, qn[rows, :])
        if mask is not None:
            scores = jnp.where(mask, scores, NEG)
        grads = dot_nt(values, ho[rows, :])
        peak = jnp.max(jnp.max(fold8(scores), 0), 0, keepdims=True)
        lifted = jnp.exp2((scores - peak) * rate)
        p_all[a, at, :] = lifted
        g_all[a, at, :] = grads
        m_all[a, block] = peak
        mass = jnp.sum(jnp.sum(fold8(lifted), 0), 0, keepdims=True)
        weighted = jnp.sum(jnp.sum(fold8(lifted * grads), 0), 0, keepdims=True)
        return peak, mass, weighted

    state = []
    for a in range(N):
        rows = slice(a * T, (a + 1) * T)
        qn[rows, :] = (hq[rows, :].astype(F32) * icq[rows, :] * gain_q).astype(BF16)
        state.append(score(a, 0, key_at <= query_at, kn[rows, :], hv[rows, :]))
        knt[a] = jnp.transpose(kn[rows, :])

    landed(MEM, mkg.at[0:3])
    landed(MEM + 1, mvg.at[0:3])
    for b in range(N):
        for t in range(N):
            at = slice(t * M, (t + 1) * M)
            mkc[b, at, :] = mkg[t, b]
            mvc[b, at, :] = mvg[t, b]
        mkt[b] = jnp.transpose(mkc[b])

    past = jnp.where(j > 0, 0, 1)

    for a in range(N):

        def absorb(b, current, a=a):
            old_peak, old_mass, old_weighted = current
            mask = None if isinstance(b, int) else key_at < j * M
            peak, mass, weighted = score(a, b + 1, mask, mkc[b], mvc[b])
            top = jnp.maximum(old_peak, peak)
            old_factor = jnp.exp2((old_peak - top) * rate)
            factor = jnp.exp2((peak - top) * rate)
            return (
                top,
                old_mass * old_factor + mass * factor,
                old_weighted * old_factor + weighted * factor,
            )

        current = state[a]
        for b in range(a):
            current = absorb(b, current)
        peak, mass, weighted = lax.fori_loop(a + past, a + 1, absorb, current)
        inverse_mass = 1.0 / mass
        fin[a, 0] = peak
        fin[a, 1] = inverse_mass
        fin[a, 2] = weighted * inverse_mass

    def settle(a, block):
        at = pl.ds(pl.multiple_of(block * T, T), T)
        factor = jnp.exp2((m_all[a, block] - fin[a, 0]) * rate) * fin[a, 1]
        attend = p_all[a, at, :] * factor
        d_scores = attend * (g_all[a, at, :] - fin[a, 2])
        return attend.astype(BF16), d_scores.astype(BF16)

    def homeward(src, dst, index, group=1):
        dst[i] = src[i]
        for r in (1, 3, 2):
            send(src.at[lax.rem(i + r, N)], dst.at[i], index, gdev(r), group)

    def norm_side(grad, raw, inv, gain):
        raw_full = raw.astype(F32)
        gained = grad * gain
        total = jnp.sum(fold8(grad * raw_full * inv), 0)
        return total, (gained * inv).astype(BF16), row_sum(gained * raw_full)

    last_parts = []
    for a in range(N):
        dqt[a] = jnp.zeros((HD, T), F32)
    for b in range(N - 1, -1, -1):
        after = range(b + 1, N)
        settled = [settle(a, b + 1) for a in after]
        for a, (_, d_scores) in zip(after, settled):
            part = dot_nn(mkt[b], d_scores)
            dqt[a] = dqt[a] + part
        if settled:
            rows = slice((b + 1) * T, N * T)
            acc_k[...] = dot_nn(jnp.concatenate([d for _, d in settled], 1), qn[rows, :])
            acc_v[...] = dot_nn(jnp.concatenate([p for p, _ in settled], 1), ho[rows, :])
        else:
            acc_k[...] = jnp.zeros((T, HD), F32)
            acc_v[...] = jnp.zeros((T, HD), F32)

        @pl.when(j > 0)
        def _(b=b):
            rows = slice(b * T, (b + 1) * T)
            attend, d_scores = settle(b, b + 1)
            acc_k[...] = acc_k[...] + dot_nn(d_scores, qn[rows, :])
            acc_v[...] = acc_v[...] + dot_nn(attend, ho[rows, :])
            dqt[b] = dqt[b] + dot_nn(mkt[b], d_scores)

        sbk[b] = (acc_k[...] * scale).astype(BF16).reshape(N, M, HD)
        sbv[b] = acc_v[...].astype(BF16).reshape(N, M, HD)
        for n, (sb, rb) in enumerate(((sbk, rbk), (sbv, rbv))):
            for r in (2, 1, 3):
                to = lax.rem(j + r, N)
                if b < N - 1:
                    send(sb.at[b, to], rb.at[j, b], DMEM + n, odev(r), 1)
                else:
                    index = 3 * n + r - 1
                    copy = remote(sb.at[b, to], rb.at[j, b], DMEM3 + index, odev(r), 4 + index)
                    pl.when(to < j)(copy.start)
                    last_parts.append((to < j, copy))

    gain_k_sum = jnp.zeros((8, HD), F32)
    for a in range(N):
        rows = slice(a * T, (a + 1) * T)
        attend, d_scores = settle(a, 0)
        dqt[a] = dqt[a] + dot_nn(knt[a], d_scores)
        grad_k = dot_nn(d_scores, qn[rows, :]) * scale
        av[a] = dot_nn(attend, ho[rows, :]).astype(BF16)
        total, ak[a], pd[a, 1:2, :] = norm_side(grad_k, hk[rows, :], ick[rows, :], gain_k)
        gain_k_sum = gain_k_sum + total
    homeward(av, avh, DV)
    homeward(ak, akh, DK)

    gain_q_sum = jnp.zeros((8, HD), F32)
    for a in range(N):
        rows = slice(a * T, (a + 1) * T)
        grad_q = jnp.transpose(dqt[a]) * scale
        total, aq[a], pd[a, 0:1, :] = norm_side(grad_q, hq[rows, :], icq[rows, :], gain_q)
        gain_q_sum = gain_q_sum + total

    homeward(pd, pdh, PD, 3)
    homeward(aq, aqh, DQ)

    for m in range(N):
        at = slice(m * M, (m + 1) * M)
        acc_k[at, :] = sbk[m, j].astype(F32)
        acc_v[at, :] = sbv[m, j].astype(F32)
    for n in range(2):
        landed(DMEM + n, hv.at[0 : 9 * M, :])
    for r in (1, 3, 2):
        source = lax.rem(j + N - r, N)
        for n, (rb, acc) in enumerate(((rbk, acc_k), (rbv, acc_v))):
            at = slice(0, (N - 1) * M)
            acc[at, :] = acc[at, :] + rb[source, 0 : N - 1].reshape((N - 1) * M, HD).astype(F32)

            @pl.when(source > j)
            def _(source=source, n=n, r=r, rb=rb, acc=acc):
                landed(DMEM3 + 3 * n + r - 1, rb.at[source, N - 1])
                at = slice((N - 1) * M, N * M)
                acc[at, :] = acc[at, :] + rb[source, N - 1].astype(F32)

    grad_mem_k = acc_k[...].astype(BF16)
    grad_mem_v = acc_v[...].astype(BF16)

    square_k = dot_tn(ku[...], grad_mem_k)
    square_v = dot_tn(vu[...], grad_mem_v)
    for p in range(N):
        pay[0, p] = square_k[p * HD : (p + 1) * HD].astype(BF16)
        pay[1, p] = square_v[p * HD : (p + 1) * HD].astype(BF16)
    gmk[...] = grad_mem_k.reshape(N, M, HD)
    gmv[...] = grad_mem_v.reshape(N, M, HD)

    for r in (2, 1, 3):
        to = lax.rem(j + r, N)
        send(pay.at[1 - c, to], rsi.at[1, j], RSX, cross(to), 2)
        send(pay.at[c, to], rsi.at[0, j], RS, odev(r), 2)
    send(pay.at[1 - c, j], rsi.at[1, j], RSX, cross(j), 2)
    homeward(gmk, gmkh, GM)
    homeward(gmv, gmvh, GM + 1)

    crossed = square_k[0:HD] * wk_ref[i, 0:HD, :].astype(F32)
    for p in range(1, N):
        at = slice(p * HD, (p + 1) * HD)
        crossed = crossed + square_k[at] * wk_ref[i, at, :].astype(F32)
    gmine[0:1, :] = jnp.sum(gain_q_sum, 0, keepdims=True)
    gmine[1:2, :] = jnp.sum(gain_k_sum, 0, keepdims=True) + row_sum(crossed) / gain_k
    for r in (1, 3, 2):
        send(gmine, gsame.at[j], GR, odev(r), 3)
    for p in range(N):
        send(gmine, gother.at[j], GRX, cross(p), 3)

    landed(RSX, rsi.at[1])
    landed(RS, rsi.at[0, 0:3])
    total = pay[c, j].astype(F32)
    for r in (1, 2, 3):
        total = total + rsi[0, lax.rem(j + r, N)].astype(F32)
    for p in range(N):
        total = total + rsi[1, p].astype(F32)
    full[c, far, near] = total.astype(BF16)
    mine = full.at[c, far, near]
    for n, r in enumerate((1, 3, 2)):
        send(mine, mine, AGG + n, ndev(r), 2)

    def pass_on(slot, member):
        piece = full.at[c, far, member]
        for r in (2, 1, 3):
            send(piece, piece, AGO + slot, fdev(r), 2)
        send(piece, piece, C2 + slot, cdev, 2)
        emit(c, far, member)

    pass_on(0, near)

    landed(GR, gsame.at[0:3])
    landed(GRX, gother)
    total = gmine[...]
    for r in (1, 2, 3):
        total = total + gsame[lax.rem(j + r, N)]
    for p in range(N):
        total = total + gother[p]
    gall[i] = total
    for r in (1, 3, 2):
        send(gall.at[i], gall.at[i], GG, gdev(r), 3)

    def forward(n, r):
        landed(AGG + n, mine)
        pass_on(n + 1, lax.rem(near + N - r, N))

    forward(0, 1)
    forward(1, 3)

    landed(GM, gmkh.at[0:3])
    landed(GM + 1, gmvh.at[0:3])
    product = jnp.zeros((T, HD), F32)
    for h in range(N):
        spread_k = dot_nt(gmkh[h], wk_ref[h])
        spread_v = dot_nt(gmvh[h], wv_ref[h])
        for n in range(KS):
            at = pl.ds(n, M, stride=KS)
            cols = slice(n * HD, (n + 1) * HD)
            bkf[h, at, :] = spread_k[:, cols]
            bvf[h, at, :] = spread_v[:, cols]
        gained = bkf[h] * gk_ref[h]
        bkf[h] = gained
        product = product + gained * k_ref[:, h * HD : (h + 1) * HD].astype(F32)

    landed(PD, pdh.at[0:3])
    total = pdh[0]
    for h in range(1, N):
        total = total + pdh[h]
    zs2[z, 0:1, :] = total[0:1]
    zs2[z, 1:2, :] = total[1:2] + row_sum(product)
    for r in range(1, nz):
        send(zs2.at[z], zs2.at[z], Z2, zdev(r), 3)

    forward(2, 2)

    for slot, back in enumerate((0, 1, 3, 2)):
        landed(AGO + slot, full.at[c, 0:3, 0])
        member = lax.rem(near + N - back, N)
        for r in (1, 3, 2):
            at = full.at[c, lax.rem(far + N - r, N), member]
            send(at, at, C2 + 4 + slot, cdev, 2)
        for r in (1, 3, 2):
            emit(c, lax.rem(far + N - r, N), member)
        landed(C2 + slot, mine)
        emit(1 - c, near, lax.rem(far + N - back, N))

    landed(Z2, zs2.at[0 : nz - 1])
    total = zs2[0]
    for r in range(1, nz):
        total = total + zs2[r]
    inverse = lax.rsqrt(gs[i] * (1.0 / hh) + EPS)
    shift = inverse * inverse * inverse * total * (1.0 / hh)
    shift_q = as_column(shift[0:1])
    shift_k = as_column(shift[1:2])
    for index in (DQ, DK, DV):
        landed(index, aqh.at[0:3])
    inverse_k = as_column(inverse[1:2])
    for h in range(N):
        cols = slice(h * HD, (h + 1) * HD)
        dq_out[:, cols] = (aqh[h].astype(F32) - q_ref[:, cols].astype(F32) * shift_q).astype(BF16)
        grad_k = akh[h].astype(F32) + bkf[h] * inverse_k
        dk_out[:, cols] = (grad_k - k_ref[:, cols].astype(F32) * shift_k).astype(BF16)
        dv_out[:, cols] = (avh[h].astype(F32) + bvf[h]).astype(BF16)
    landed(GG, gall.at[0:3])
    for h in range(N):
        gain_out[0, h] = gall[h, 0:1, :]
        gain_out[1, h] = gall[h, 1:2, :]

    for slot, back in enumerate((0, 1, 3, 2)):
        landed(C2 + 4 + slot, full.at[c, 0:3, 0])
        for r in (1, 3, 2):
            emit(1 - c, lax.rem(near + N - r, N), lax.rem(far + N - back, N))

    for group, size in enumerate(sent):
        if group < 3:
            rows = size // (4 * T)
            assert rows * 4 * T == size and rows % 8 == 0
            space = p_all.at[0, 0:rows, :]
        else:
            assert size == tally.shape[0] * 8 * T
            space = tally
        remote(space, space, 0, cdev, group).wait_send()
    for needed, copy in last_parts:
        pl.when(needed)(copy.wait_send)


def finish(
    dq_ref, dk_ref, dv_ref, kern_ref, gain_ref,
    dq_out, dk_out, dv_out, qg_out, kg_out, sk_out, sv_out,
    sems,
):
    pairs = [(kern_ref.at[0, h], sk_out.at[h]) for h in range(N)]
    pairs += [(kern_ref.at[1, h], sv_out.at[h]) for h in range(N)]
    pairs += [(dq_ref, dq_out), (dk_ref, dk_out), (dv_ref, dv_out)]
    pairs += [(gain_ref.at[0], qg_out), (gain_ref.at[1], kg_out)]
    copies = [pltpu.make_async_copy(src, dst, sems.at[n]) for n, (src, dst) in enumerate(pairs)]
    for copy in copies:
        copy.start()
    for copy in copies:
        copy.wait()


def on_device(nz, q, k, v, query_gain, key_gain, key_squeeze, value_squeeze, o):
    width = N * HD
    bf = functools.partial(pltpu.VMEM, dtype=BF16)
    ff = functools.partial(pltpu.VMEM, dtype=F32)
    rows = N * T
    deep = (N + 1) * T
    scratch = [ff((N, 1, HD))] * 2
    scratch += [bf((T, width))] * 4 + [bf((N, KS * HD, HD))] * 2
    scratch += [bf((rows, HD))] * 4 + [bf((rows, HD))] * 2 + [ff((rows, HD))] * 2
    scratch += [ff((rows, HD)), bf((N * M, KS * HD)), bf((N * M, KS * HD))]
    scratch += [ff((N, 2, T)), ff((nz, N, 2, T)), ff((N, 2, T))]
    scratch += [bf((N, N, M, HD))] * 2 + [bf((N, N * M, HD))] * 2
    scratch += [ff((N, deep, T))] * 2 + [ff((N, N + 1, 1, T)), ff((N, 3, 1, T))]
    scratch += [bf((N, HD, T))] * 2 + [ff((N, HD, T))]
    scratch += [ff((N * M, HD))] * 2 + [bf((N, N, M, HD))] * 4
    scratch += [bf((N, T, HD))] * 3 + [ff((N, 2, T))]
    scratch += [bf((N, T, HD))] * 3 + [ff((N, 2, T)), ff((nz, 2, T))]
    scratch += [bf((N, M, HD))] * 4 + [ff((N, T, HD))] * 2
    scratch += [ff((2, HD))] + [ff((N, 2, HD))] * 3
    scratch += [bf((2, N, HD, HD))] * 2 + [bf((2, N, N, HD, HD))]
    scratch += [ff((18, 2, T))]
    scratch += [
        pltpu.SemaphoreType.DMA((N_SEND,)),
        pltpu.SemaphoreType.DMA((N_RECV,)),
        pltpu.SemaphoreType.DMA((12,)),
    ]
    vmem = pl.BlockSpec(memory_space=pltpu.VMEM)
    anywhere = pl.BlockSpec(memory_space=pl.ANY)
    hbm = pl.BlockSpec(memory_space=pltpu.MemorySpace.HBM)
    stay = functools.partial(
        pltpu.with_memory_space_constraint, memory_space=pltpu.MemorySpace.HBM
    )
    grads = [jax.ShapeDtypeStruct((T, width), BF16)] * 3
    outs = pl.pallas_call(
        functools.partial(kernel, nz),
        out_shape=grads
        + [
            jax.ShapeDtypeStruct((2, N, KS * HD, HD), F32),
            jax.ShapeDtypeStruct((2, N, 1, HD), F32),
        ],
        in_specs=[hbm] * 8,
        out_specs=[vmem] * 5,
        scratch_shapes=scratch,
        compiler_params=pltpu.CompilerParams(
            collective_id=0, has_side_effects=True, vmem_limit_bytes=40 * 2**20
        ),
    )(
        stay(q[0]), stay(k[0]), stay(v[0]), stay(o[0]),
        stay(query_gain.reshape(N, 1, HD)), stay(key_gain.reshape(N, 1, HD)),
        stay(key_squeeze), stay(value_squeeze),
    )
    kernels = jax.ShapeDtypeStruct((N, KS * HD, HD), F32)
    gains = jax.ShapeDtypeStruct((N, 1, HD), F32)
    dq, dk, dv, qg, kg, sk, sv = pl.pallas_call(
        finish,
        out_shape=grads + [gains] * 2 + [kernels] * 2,
        in_specs=[anywhere] * 5,
        out_specs=[hbm] * 7,
        scratch_shapes=[pltpu.SemaphoreType.DMA((13,))],
        compiler_params=pltpu.CompilerParams(vmem_limit_bytes=16 * 2**20),
    )(*outs)
    return dq[None], dk[None], dv[None], qg.reshape(width), kg.reshape(width), sk, sv


def solution(mesh):
    by_token = P("dp", "seq", "head")
    by_head = P("head", None, None)
    return jax.shard_map(
        functools.partial(on_device, mesh.shape["head"]),
        mesh=mesh,
        in_specs=(by_token,) * 3 + (P("head"), P("head"), by_head, by_head, by_token),
        out_specs=(by_token,) * 3 + (P("head"), P("head"), by_head, by_head),
        check_vma=False,
    )
```

```python
import functools

import jax
import jax.numpy as jnp
from jax import lax
from jax.experimental import pallas as pl
from jax.experimental.pallas import tpu as pltpu
from jax.sharding import PartitionSpec as P

HD = 128
KS = 4
N = 4
T = 256
M = 64
EPS = 1e-06
NEG = -1e30
LOG2E = 1.4426950408889634
MESH = pl.DeviceIdType.MESH
F32 = jnp.float32
BF16 = jnp.bfloat16

A2A = 0
Z1 = A2A + 4
G1 = Z1 + 1
MEM = G1 + 1
DMEM = MEM + 2
DMEM3 = DMEM + 2
DQ = DMEM3 + 6
DK = DQ + 1
DV = DK + 1
PD = DV + 1
Z2 = PD + 1
RS = Z2 + 1
RSX = RS + 1
AGG = RSX + 1
AGO = AGG + 3
C2 = AGO + 4
GM = C2 + 8
GR = GM + 2
GRX = GR + 1
GG = GRX + 1
N_RECV = GG + 1
N_SEND = 4 + 6


def dot_nt(a, b):
    return lax.dot_general(a, b, (((1,), (1,)), ((), ())), preferred_element_type=F32)


def dot_tn(a, b):
    return lax.dot_general(a, b, (((0,), (0,)), ((), ())), preferred_element_type=F32)


def dot_nn(a, b):
    return lax.dot_general(a, b, (((1,), (0,)), ((), ())), preferred_element_type=F32)


def as_column(row):
    return jnp.transpose(jnp.broadcast_to(row, (HD, row.shape[1])))


def row_sum(block):
    return jnp.sum(jnp.transpose(block), 0, keepdims=True)


def fold8(block):
    return block.reshape(block.shape[0] // 8, 8, block.shape[1])


def kernel(
    nz,
    q_hbm, k_hbm, v_hbm, o_hbm, gq_hbm, gk_hbm, wk_hbm, wv_hbm,
    dq_out, dk_out, dv_out, kern_out, gain_out,
    gq_ref, gk_ref, q_ref, k_ref, v_ref, o_ref, wk_ref, wv_ref,
    hq, hk, hv, ho, qn, kn, icq, ick, fs, ku, vu, gsp, zs, gs, mkg, mvg, mkc, mvc,
    p_all, g_all, m_all, fin, mkt, knt, dqt, acc_k, acc_v, sbk, sbv, rbk, rbv,
    aq, ak, av, pd, aqh, akh, avh, pdh, zs2,
    gmk, gmv, gmkh, gmvh, bkf, bvf, gmine, gsame, gother, gall,
    pay, rsi, full, tally,
    ss, rs, loc,
):
    seq = lax.axis_index("seq")
    x = lax.rem(seq, N)
    y = lax.div(seq, N)
    z = lax.axis_index("head")
    c = lax.axis_index("dp")
    i = y
    j = x
    near = i + c * (j - i)
    far = j + c * (i - j)
    hh = nz * N * HD
    scale = HD ** (-0.5)

    def gdev(r):
        return {"seq": lax.rem(i + r, N) * N + j}

    def odev(r):
        return {"seq": i * N + lax.rem(j + r, N)}

    def ndev(r):
        to = lax.rem(near + r, N)
        return {"seq": to * (N - (N - 1) * c) + far * (1 + (N - 1) * c)}

    def fdev(r):
        to = lax.rem(far + r, N)
        return {"seq": near * (N - (N - 1) * c) + to * (1 + (N - 1) * c)}

    def cross(p):
        return {"seq": i * N + p, "dp": 1 - c}

    def zdev(r):
        return {"head": lax.rem(z + r, nz)}

    cdev = {"dp": 1 - c}

    def remote(src, dst, index, device, group):
        return pltpu.make_async_remote_copy(
            src_ref=src,
            dst_ref=dst,
            send_sem=ss.at[group],
            recv_sem=rs.at[index],
            device_id=device,
            device_id_type=MESH,
        )

    sent = [0, 0, 0, 0]

    def send(src, dst, index, device, group):
        remote(src, dst, index, device, group).start()
        size = 1
        for length in src.shape:
            size = size * length
        sent[group] += size * src.dtype.itemsize

    def landed(index, space):
        remote(space, space, index, cdev, 0).wait_recv()

    def emit(core, across, along):
        head = along + core * (across - along)
        rows = pl.ds(pl.multiple_of((across + core * (along - across)) * HD, HD), HD)
        kern_out[core, head, rows, :] = full[core, across, along].astype(F32)

    barrier = pltpu.get_barrier_semaphore()
    peers = [gdev(r) for r in (1, 2, 3)] + [odev(r) for r in (1, 2, 3)]
    peers += [zdev(r) for r in range(1, nz)] + [cross(p) for p in range(N)] + [cdev]
    for peer in peers:
        pl.semaphore_signal(barrier, inc=1, device_id=peer, device_id_type=MESH)

    loads = [
        pltpu.make_async_copy(src, dst, loc.at[4 + n])
        for n, (src, dst) in enumerate(
            (
                (q_hbm, q_ref), (k_hbm, k_ref), (v_hbm, v_ref), (o_hbm, o_ref),
                (wv_hbm, wv_ref), (wk_hbm, wk_ref),
                (gq_hbm, gq_ref), (gk_hbm, gk_ref),
            )
        )
    ]
    for copy in loads:
        copy.start()

    for row, ref in ((0, q_ref), (1, k_ref)):
        loads[row].wait()
        full_rows = ref[...].astype(F32)
        squares = full_rows * full_rows
        folded = squares[:, :HD]
        for h in range(1, N):
            folded = folded + squares[:, h * HD : (h + 1) * HD]
        gsp[i, row : row + 1, :] = row_sum(folded)
    for copy in loads[2:4]:
        copy.wait()

    pl.semaphore_wait(barrier, len(peers))

    for r in (2, 1, 3):
        send(gsp.at[i], gsp.at[i], G1, gdev(r), 3)
    rows_mine = pl.ds(pl.multiple_of(i * T, T), T)
    own = {}

    def exchange(n, src, dst):
        for r in (2, 1, 3):
            cols = pl.ds(pl.multiple_of(lax.rem(i + r, N) * HD, HD), HD)
            send(src.at[:, cols], dst.at[rows_mine, :], A2A + n, gdev(r), 0)
        cols = pl.ds(pl.multiple_of(i * HD, HD), HD)
        own[n] = pltpu.make_async_copy(src.at[:, cols], dst.at[rows_mine, :], loc.at[n])
        own[n].start()

    def arrived(n):
        landed(A2A + n, hv.at[0 : 3 * T, :])
        own[n].wait()

    exchange(0, v_ref, hv)
    exchange(1, k_ref, hk)

    exchange(2, q_ref, hq)
    exchange(3, o_ref, ho)

    landed(G1, gsp.at[0:3])
    for r in sorted(range(1, nz), key=lambda r: -min(r, nz - r)):
        send(gsp, zs.at[z], Z1, zdev(r), 0)
    for copy in loads[4:]:
        copy.wait()

    def unfold(dst):
        for n in range(KS):
            dst[:, n * HD : (n + 1) * HD] = fs[pl.ds(n, N * M, stride=KS), :].astype(BF16)

    def spread(mem, value, index):
        mem[j] = value.astype(BF16).reshape(N, M, HD)
        for r in (2, 1, 3):
            send(mem.at[j], mem.at[j], MEM + index, odev(r), 0)

    arrived(0)
    fs[...] = hv[...].astype(F32)
    unfold(vu)
    spread(mvg, dot_nn(vu[...], wv_ref[i]), 1)

    landed(Z1, zs.at[0 : nz - 1])
    gs[...] = gsp[...]
    for r in range(1, nz):
        gs[...] = gs[...] + zs[lax.rem(z + r, nz)]
    gain_q = gq_ref[i]
    gain_k = gk_ref[i]
    arrived(1)
    for a in range(N):
        rows = slice(a * T, (a + 1) * T)
        inverse = lax.rsqrt(gs[a] * (1.0 / hh) + EPS)
        icq[rows, :] = as_column(inverse[0:1])
        ick[rows, :] = as_column(inverse[1:2])
        normed = (hk[rows, :].astype(F32) * ick[rows, :] * gain_k).astype(BF16)
        kn[rows, :] = normed
        fs[rows, :] = normed.astype(F32)
    unfold(ku)
    spread(mkg, dot_nn(ku[...], wk_ref[i]), 0)

    arrived(2)
    arrived(3)
    key_at = lax.broadcasted_iota(jnp.int32, (T, T), 0)
    query_at = lax.broadcasted_iota(jnp.int32, (T, T), 1)
    rate = scale * LOG2E

    def score(a, block, mask, keys, values):
        at = pl.ds(pl.multiple_of(block * T, T), T)
        rows = slice(a * T, (a + 1) * T)
        scores = dot_nt(keys, qn[rows, :])
        if mask is not None:
            scores = jnp.where(mask, scores, NEG)
        grads = dot_nt(values, ho[rows, :])
        peak = jnp.max(jnp.max(fold8(scores), 0), 0, keepdims=True)
        lifted = jnp.exp2((scores - peak) * rate)
        p_all[a, at, :] = lifted
        g_all[a, at, :] = grads
        m_all[a, block] = peak
        mass = jnp.sum(jnp.sum(fold8(lifted), 0), 0, keepdims=True)
        weighted = jnp.sum(jnp.sum(fold8(lifted * grads), 0), 0, keepdims=True)
        return peak, mass, weighted

    state = []
    for a in range(N):
        rows = slice(a * T, (a + 1) * T)
        qn[rows, :] = (hq[rows, :].astype(F32) * icq[rows, :] * gain_q).astype(BF16)
        state.append(score(a, 0, key_at <= query_at, kn[rows, :], hv[rows, :]))
        knt[a] = jnp.transpose(kn[rows, :])

    landed(MEM, mkg.at[0:3])
    landed(MEM + 1, mvg.at[0:3])
    for b in range(N):
        for t in range(N):
            at = slice(t * M, (t + 1) * M)
            mkc[b, at, :] = mkg[t, b]
            mvc[b, at, :] = mvg[t, b]
        mkt[b] = jnp.transpose(mkc[b])

    past = jnp.where(j > 0, 0, 1)

    for a in range(N):

        def absorb(b, current, a=a):
            old_peak, old_mass, old_weighted = current
            mask = None if isinstance(b, int) else key_at < j * M
            peak, mass, weighted = score(a, b + 1, mask, mkc[b], mvc[b])
            top = jnp.maximum(old_peak, peak)
            old_factor = jnp.exp2((old_peak - top) * rate)
            factor = jnp.exp2((peak - top) * rate)
            return (
                top,
                old_mass * old_factor + mass * factor,
                old_weighted * old_factor + weighted * factor,
            )

        current = state[a]
        for b in range(a):
            current = absorb(b, current)
        peak, mass, weighted = lax.fori_loop(a + past, a + 1, absorb, current)
        inverse_mass = 1.0 / mass
        fin[a, 0] = peak
        fin[a, 1] = inverse_mass
        fin[a, 2] = weighted * inverse_mass

    def settle(a, block):
        at = pl.ds(pl.multiple_of(block * T, T), T)
        factor = jnp.exp2((m_all[a, block] - fin[a, 0]) * rate) * fin[a, 1]
        attend = p_all[a, at, :] * factor
        d_scores = attend * (g_all[a, at, :] - fin[a, 2])
        return attend.astype(BF16), d_scores.astype(BF16)

    def homeward(src, dst, index, group=1):
        dst[i] = src[i]
        for r in (2, 1, 3):
            send(src.at[lax.rem(i + r, N)], dst.at[i], index, gdev(r), group)

    def norm_side(grad, raw, inv, gain):
        raw_full = raw.astype(F32)
        gained = grad * gain
        total = jnp.sum(fold8(grad * raw_full * inv), 0)
        return total, (gained * inv).astype(BF16), row_sum(gained * raw_full)

    last_parts = []
    for a in range(N):
        dqt[a] = jnp.zeros((HD, T), F32)
    for b in range(N - 1, -1, -1):
        after = range(b + 1, N)
        settled = [settle(a, b + 1) for a in after]
        for a, (_, d_scores) in zip(after, settled):
            part = dot_nn(mkt[b], d_scores)
            dqt[a] = dqt[a] + part
        if settled:
            rows = slice((b + 1) * T, N * T)
            acc_k[...] = dot_nn(jnp.concatenate([d for _, d in settled], 1), qn[rows, :])
            acc_v[...] = dot_nn(jnp.concatenate([p for p, _ in settled], 1), ho[rows, :])
        else:
            acc_k[...] = jnp.zeros((T, HD), F32)
            acc_v[...] = jnp.zeros((T, HD), F32)

        @pl.when(j > 0)
        def _(b=b):
            rows = slice(b * T, (b + 1) * T)
            attend, d_scores = settle(b, b + 1)
            acc_k[...] = acc_k[...] + dot_nn(d_scores, qn[rows, :])
            acc_v[...] = acc_v[...] + dot_nn(attend, ho[rows, :])
            dqt[b] = dqt[b] + dot_nn(mkt[b], d_scores)

        sbk[b] = (acc_k[...] * scale).astype(BF16).reshape(N, M, HD)
        sbv[b] = acc_v[...].astype(BF16).reshape(N, M, HD)
        for n, (sb, rb) in enumerate(((sbk, rbk), (sbv, rbv))):
            for r in (2, 1, 3):
                to = lax.rem(j + r, N)
                if b < N - 1:
                    send(sb.at[b, to], rb.at[j, b], DMEM + n, odev(r), 1)
                else:
                    index = 3 * n + r - 1
                    copy = remote(sb.at[b, to], rb.at[j, b], DMEM3 + index, odev(r), 4 + index)
                    pl.when(to < j)(copy.start)
                    last_parts.append((to < j, copy))

    gain_k_sum = jnp.zeros((8, HD), F32)
    for a in range(N):
        rows = slice(a * T, (a + 1) * T)
        attend, d_scores = settle(a, 0)
        dqt[a] = dqt[a] + dot_nn(knt[a], d_scores)
        grad_k = dot_nn(d_scores, qn[rows, :]) * scale
        av[a] = dot_nn(attend, ho[rows, :]).astype(BF16)
        total, ak[a], pd[a, 1:2, :] = norm_side(grad_k, hk[rows, :], ick[rows, :], gain_k)
        gain_k_sum = gain_k_sum + total
    homeward(av, avh, DV)
    homeward(ak, akh, DK)

    gain_q_sum = jnp.zeros((8, HD), F32)
    for a in range(N):
        rows = slice(a * T, (a + 1) * T)
        grad_q = jnp.transpose(dqt[a]) * scale
        total, aq[a], pd[a, 0:1, :] = norm_side(grad_q, hq[rows, :], icq[rows, :], gain_q)
        gain_q_sum = gain_q_sum + total

    homeward(pd, pdh, PD, 3)
    homeward(aq, aqh, DQ)

    for m in range(N):
        at = slice(m * M, (m + 1) * M)
        acc_k[at, :] = sbk[m, j].astype(F32)
        acc_v[at, :] = sbv[m, j].astype(F32)
    for n in range(2):
        landed(DMEM + n, hv.at[0 : 9 * M, :])
    for r in (1, 3, 2):
        source = lax.rem(j + N - r, N)
        for n, (rb, acc) in enumerate(((rbk, acc_k), (rbv, acc_v))):
            at = slice(0, (N - 1) * M)
            acc[at, :] = acc[at, :] + rb[source, 0 : N - 1].reshape((N - 1) * M, HD).astype(F32)

            @pl.when(source > j)
            def _(source=source, n=n, r=r, rb=rb, acc=acc):
                landed(DMEM3 + 3 * n + r - 1, rb.at[source, N - 1])
                at = slice((N - 1) * M, N * M)
                acc[at, :] = acc[at, :] + rb[source, N - 1].astype(F32)

    grad_mem_k = acc_k[...].astype(BF16)
    grad_mem_v = acc_v[...].astype(BF16)

    square_k = dot_tn(ku[...], grad_mem_k)
    square_v = dot_tn(vu[...], grad_mem_v)
    for p in range(N):
        pay[0, p] = square_k[p * HD : (p + 1) * HD].astype(BF16)
        pay[1, p] = square_v[p * HD : (p + 1) * HD].astype(BF16)
    gmk[...] = grad_mem_k.reshape(N, M, HD)
    gmv[...] = grad_mem_v.reshape(N, M, HD)

    for r in (2, 1, 3):
        to = lax.rem(j + r, N)
        send(pay.at[1 - c, to], rsi.at[1, j], RSX, cross(to), 2)
        send(pay.at[c, to], rsi.at[0, j], RS, odev(r), 2)
    send(pay.at[1 - c, j], rsi.at[1, j], RSX, cross(j), 2)
    homeward(gmk, gmkh, GM)
    homeward(gmv, gmvh, GM + 1)

    crossed = square_k[0:HD] * wk_ref[i, 0:HD, :].astype(F32)
    for p in range(1, N):
        at = slice(p * HD, (p + 1) * HD)
        crossed = crossed + square_k[at] * wk_ref[i, at, :].astype(F32)
    gmine[0:1, :] = jnp.sum(gain_q_sum, 0, keepdims=True)
    gmine[1:2, :] = jnp.sum(gain_k_sum, 0, keepdims=True) + row_sum(crossed) / gain_k
    for r in (1, 3, 2):
        send(gmine, gsame.at[j], GR, odev(r), 3)
    for p in range(N):
        send(gmine, gother.at[j], GRX, cross(p), 3)

    landed(RSX, rsi.at[1])
    landed(RS, rsi.at[0, 0:3])
    total = pay[c, j].astype(F32)
    for r in (1, 2, 3):
        total = total + rsi[0, lax.rem(j + r, N)].astype(F32)
    for p in range(N):
        total = total + rsi[1, p].astype(F32)
    full[c, far, near] = total.astype(BF16)
    mine = full.at[c, far, near]
    for n, r in ((2, 2), (0, 1), (1, 3)):
        send(mine, mine, AGG + n, ndev(r), 2)

    def pass_on(slot, member):
        piece = full.at[c, far, member]
        for r in (2, 1, 3):
            send(piece, piece, AGO + slot, fdev(r), 2)
        send(piece, piece, C2 + slot, cdev, 2)
        emit(c, far, member)

    pass_on(0, near)

    landed(GR, gsame.at[0:3])
    landed(GRX, gother)
    total = gmine[...]
    for r in (1, 2, 3):
        total = total + gsame[lax.rem(j + r, N)]
    for p in range(N):
        total = total + gother[p]
    gall[i] = total
    for r in (1, 3, 2):
        send(gall.at[i], gall.at[i], GG, gdev(r), 3)

    def forward(n, r):
        landed(AGG + n, mine)
        pass_on(n + 1, lax.rem(near + N - r, N))

    forward(0, 1)
    forward(1, 3)

    landed(GM, gmkh.at[0:3])
    landed(GM + 1, gmvh.at[0:3])
    product = jnp.zeros((T, HD), F32)
    for h in range(N):
        spread_k = dot_nt(gmkh[h], wk_ref[h])
        spread_v = dot_nt(gmvh[h], wv_ref[h])
        for n in range(KS):
            at = pl.ds(n, M, stride=KS)
            cols = slice(n * HD, (n + 1) * HD)
            bkf[h, at, :] = spread_k[:, cols]
            bvf[h, at, :] = spread_v[:, cols]
        gained = bkf[h] * gk_ref[h]
        bkf[h] = gained
        product = product + gained * k_ref[:, h * HD : (h + 1) * HD].astype(F32)

    landed(PD, pdh.at[0:3])
    total = pdh[0]
    for h in range(1, N):
        total = total + pdh[h]
    zs2[z, 0:1, :] = total[0:1]
    zs2[z, 1:2, :] = total[1:2] + row_sum(product)
    for r in sorted(range(1, nz), key=lambda r: -min(r, nz - r)):
        send(zs2.at[z], zs2.at[z], Z2, zdev(r), 3)

    forward(2, 2)

    for slot, back in enumerate((0, 1, 3, 2)):
        landed(AGO + slot, full.at[c, 0:3, 0])
        member = lax.rem(near + N - back, N)
        for r in (1, 3, 2):
            at = full.at[c, lax.rem(far + N - r, N), member]
            send(at, at, C2 + 4 + slot, cdev, 2)
        for r in (1, 3, 2):
            emit(c, lax.rem(far + N - r, N), member)
        landed(C2 + slot, mine)
        emit(1 - c, near, lax.rem(far + N - back, N))

    landed(Z2, zs2.at[0 : nz - 1])
    total = zs2[0]
    for r in range(1, nz):
        total = total + zs2[r]
    inverse = lax.rsqrt(gs[i] * (1.0 / hh) + EPS)
    shift = inverse * inverse * inverse * total * (1.0 / hh)
    shift_q = as_column(shift[0:1])
    shift_k = as_column(shift[1:2])
    for index in (DQ, DK, DV):
        landed(index, aqh.at[0:3])
    inverse_k = as_column(inverse[1:2])
    for h in range(N):
        cols = slice(h * HD, (h + 1) * HD)
        dq_out[:, cols] = (aqh[h].astype(F32) - q_ref[:, cols].astype(F32) * shift_q).astype(BF16)
        grad_k = akh[h].astype(F32) + bkf[h] * inverse_k
        dk_out[:, cols] = (grad_k - k_ref[:, cols].astype(F32) * shift_k).astype(BF16)
        dv_out[:, cols] = (avh[h].astype(F32) + bvf[h]).astype(BF16)
    landed(GG, gall.at[0:3])
    for h in range(N):
        gain_out[0, h] = gall[h, 0:1, :]
        gain_out[1, h] = gall[h, 1:2, :]

    for slot, back in enumerate((0, 1, 3, 2)):
        landed(C2 + 4 + slot, full.at[c, 0:3, 0])
        for r in (1, 3, 2):
            emit(1 - c, lax.rem(near + N - r, N), lax.rem(far + N - back, N))

    for group, size in enumerate(sent):
        if group < 3:
            rows = size // (4 * T)
            assert rows * 4 * T == size and rows % 8 == 0
            space = p_all.at[0, 0:rows, :]
        else:
            assert size == tally.shape[0] * 8 * T
            space = tally
        remote(space, space, 0, cdev, group).wait_send()
    for needed, copy in last_parts:
        pl.when(needed)(copy.wait_send)


def finish(
    dq_ref, dk_ref, dv_ref, kern_ref, gain_ref,
    dq_out, dk_out, dv_out, qg_out, kg_out, sk_out, sv_out,
    sems,
):
    pairs = [(kern_ref.at[0, h], sk_out.at[h]) for h in range(N)]
    pairs += [(kern_ref.at[1, h], sv_out.at[h]) for h in range(N)]
    pairs += [(dq_ref, dq_out), (dk_ref, dk_out), (dv_ref, dv_out)]
    pairs += [(gain_ref.at[0], qg_out), (gain_ref.at[1], kg_out)]
    copies = [pltpu.make_async_copy(src, dst, sems.at[n]) for n, (src, dst) in enumerate(pairs)]
    for copy in copies:
        copy.start()
    for copy in copies:
        copy.wait()


def on_device(nz, q, k, v, query_gain, key_gain, key_squeeze, value_squeeze, o):
    width = N * HD
    bf = functools.partial(pltpu.VMEM, dtype=BF16)
    ff = functools.partial(pltpu.VMEM, dtype=F32)
    rows = N * T
    deep = (N + 1) * T
    scratch = [ff((N, 1, HD))] * 2
    scratch += [bf((T, width))] * 4 + [bf((N, KS * HD, HD))] * 2
    scratch += [bf((rows, HD))] * 4 + [bf((rows, HD))] * 2 + [ff((rows, HD))] * 2
    scratch += [ff((rows, HD)), bf((N * M, KS * HD)), bf((N * M, KS * HD))]
    scratch += [ff((N, 2, T)), ff((nz, N, 2, T)), ff((N, 2, T))]
    scratch += [bf((N, N, M, HD))] * 2 + [bf((N, N * M, HD))] * 2
    scratch += [ff((N, deep, T))] * 2 + [ff((N, N + 1, 1, T)), ff((N, 3, 1, T))]
    scratch += [bf((N, HD, T))] * 2 + [ff((N, HD, T))]
    scratch += [ff((N * M, HD))] * 2 + [bf((N, N, M, HD))] * 4
    scratch += [bf((N, T, HD))] * 3 + [ff((N, 2, T))]
    scratch += [bf((N, T, HD))] * 3 + [ff((N, 2, T)), ff((nz, 2, T))]
    scratch += [bf((N, M, HD))] * 4 + [ff((N, T, HD))] * 2
    scratch += [ff((2, HD))] + [ff((N, 2, HD))] * 3
    scratch += [bf((2, N, HD, HD))] * 2 + [bf((2, N, N, HD, HD))]
    scratch += [ff((18, 2, T))]
    scratch += [
        pltpu.SemaphoreType.DMA((N_SEND,)),
        pltpu.SemaphoreType.DMA((N_RECV,)),
        pltpu.SemaphoreType.DMA((12,)),
    ]
    vmem = pl.BlockSpec(memory_space=pltpu.VMEM)
    anywhere = pl.BlockSpec(memory_space=pl.ANY)
    hbm = pl.BlockSpec(memory_space=pltpu.MemorySpace.HBM)
    stay = functools.partial(
        pltpu.with_memory_space_constraint, memory_space=pltpu.MemorySpace.HBM
    )
    grads = [jax.ShapeDtypeStruct((T, width), BF16)] * 3
    outs = pl.pallas_call(
        functools.partial(kernel, nz),
        out_shape=grads
        + [
            jax.ShapeDtypeStruct((2, N, KS * HD, HD), F32),
            jax.ShapeDtypeStruct((2, N, 1, HD), F32),
        ],
        in_specs=[hbm] * 8,
        out_specs=[vmem] * 5,
        scratch_shapes=scratch,
        compiler_params=pltpu.CompilerParams(
            collective_id=0, has_side_effects=True, vmem_limit_bytes=40 * 2**20
        ),
    )(
        stay(q[0]), stay(k[0]), stay(v[0]), stay(o[0]),
        stay(query_gain.reshape(N, 1, HD)), stay(key_gain.reshape(N, 1, HD)),
        stay(key_squeeze), stay(value_squeeze),
    )
    kernels = jax.ShapeDtypeStruct((N, KS * HD, HD), F32)
    gains = jax.ShapeDtypeStruct((N, 1, HD), F32)
    dq, dk, dv, qg, kg, sk, sv = pl.pallas_call(
        finish,
        out_shape=grads + [gains] * 2 + [kernels] * 2,
        in_specs=[anywhere] * 5,
        out_specs=[hbm] * 7,
        scratch_shapes=[pltpu.SemaphoreType.DMA((13,))],
        compiler_params=pltpu.CompilerParams(vmem_limit_bytes=16 * 2**20),
    )(*outs)
    return dq[None], dk[None], dv[None], qg.reshape(width), kg.reshape(width), sk, sv


def solution(mesh):
    by_token = P("dp", "seq", "head")
    by_head = P("head", None, None)
    return jax.shard_map(
        functools.partial(on_device, mesh.shape["head"]),
        mesh=mesh,
        in_specs=(by_token,) * 3 + (P("head"), P("head"), by_head, by_head, by_token),
        out_specs=(by_token,) * 3 + (P("head"), P("head"), by_head, by_head),
        check_vma=False,
    )
```

```python
import functools

import jax
import jax.numpy as jnp
from jax import lax
from jax.experimental import pallas as pl
from jax.experimental.pallas import tpu as pltpu
from jax.sharding import PartitionSpec as P

HD = 128
KS = 4
N = 4
T = 256
M = 64
EPS = 1e-06
NEG = -1e30
LOG2E = 1.4426950408889634
MESH = pl.DeviceIdType.MESH
F32 = jnp.float32
BF16 = jnp.bfloat16

A2A = 0
Z1 = A2A + 4
G1 = Z1 + 1
MEM = G1 + 1
DMEM = MEM + 2
DMEM3 = DMEM + 2
DQ = DMEM3 + 6
DK = DQ + 1
DV = DK + 1
PD = DV + 1
Z2 = PD + 1
RS = Z2 + 1
RSX = RS + 1
AGG = RSX + 1
AGO = AGG + 3
C2 = AGO + 4
GM = C2 + 8
GR = GM + 2
GRX = GR + 1
GG = GRX + 1
N_RECV = GG + 1
N_SEND = 4 + 6


def dot_nt(a, b):
    return lax.dot_general(a, b, (((1,), (1,)), ((), ())), preferred_element_type=F32)


def dot_tn(a, b):
    return lax.dot_general(a, b, (((0,), (0,)), ((), ())), preferred_element_type=F32)


def dot_nn(a, b):
    return lax.dot_general(a, b, (((1,), (0,)), ((), ())), preferred_element_type=F32)


def as_column(row):
    return jnp.transpose(jnp.broadcast_to(row, (HD, row.shape[1])))


def row_sum(block):
    return jnp.sum(jnp.transpose(block), 0, keepdims=True)


def fold8(block):
    return block.reshape(block.shape[0] // 8, 8, block.shape[1])


def kernel(
    nz,
    q_hbm, k_hbm, v_hbm, o_hbm, gq_hbm, gk_hbm, wk_hbm, wv_hbm,
    dq_out, dk_out, dv_out, kern_out, gain_out,
    gq_ref, gk_ref, q_ref, k_ref, v_ref, o_ref, wk_ref, wv_ref,
    hq, hk, hv, ho, qn, kn, icq, ick, fs, ku, vu, gsp, zs, gs, mkg, mvg, mkc, mvc,
    p_all, g_all, m_all, fin, mkt, knt, dqt, acc_k, acc_v, sbk, sbv, rbk, rbv,
    aq, ak, av, pd, aqh, akh, avh, pdh, zs2,
    gmk, gmv, gmkh, gmvh, bkf, bvf, gmine, gsame, gother, gall,
    pay, rsi, full, tally,
    ss, rs, loc,
):
    seq = lax.axis_index("seq")
    x = lax.rem(seq, N)
    y = lax.div(seq, N)
    z = lax.axis_index("head")
    c = lax.axis_index("dp")
    i = y
    j = x
    near = i + c * (j - i)
    far = j + c * (i - j)
    hh = nz * N * HD
    scale = HD ** (-0.5)

    def gdev(r):
        return {"seq": lax.rem(i + r, N) * N + j}

    def odev(r):
        return {"seq": i * N + lax.rem(j + r, N)}

    def ndev(r):
        to = lax.rem(near + r, N)
        return {"seq": to * (N - (N - 1) * c) + far * (1 + (N - 1) * c)}

    def fdev(r):
        to = lax.rem(far + r, N)
        return {"seq": near * (N - (N - 1) * c) + to * (1 + (N - 1) * c)}

    def cross(p):
        return {"seq": i * N + p, "dp": 1 - c}

    def zdev(r):
        return {"head": lax.rem(z + r, nz)}

    cdev = {"dp": 1 - c}

    def remote(src, dst, index, device, group):
        return pltpu.make_async_remote_copy(
            src_ref=src,
            dst_ref=dst,
            send_sem=ss.at[group],
            recv_sem=rs.at[index],
            device_id=device,
            device_id_type=MESH,
        )

    sent = [0, 0, 0, 0]

    def send(src, dst, index, device, group):
        remote(src, dst, index, device, group).start()
        size = 1
        for length in src.shape:
            size = size * length
        sent[group] += size * src.dtype.itemsize

    def landed(index, space):
        remote(space, space, index, cdev, 0).wait_recv()

    def emit(core, across, along):
        head = along + core * (across - along)
        rows = pl.ds(pl.multiple_of((across + core * (along - across)) * HD, HD), HD)
        kern_out[core, head, rows, :] = full[core, across, along].astype(F32)

    barrier = pltpu.get_barrier_semaphore()
    peers = [gdev(r) for r in (1, 2, 3)] + [odev(r) for r in (1, 2, 3)]
    peers += [zdev(r) for r in range(1, nz)] + [cross(p) for p in range(N)]
    for peer in peers:
        pl.semaphore_signal(barrier, inc=1, device_id=peer, device_id_type=MESH)

    loads = [
        pltpu.make_async_copy(src, dst, loc.at[4 + n])
        for n, (src, dst) in enumerate(
            (
                (q_hbm, q_ref), (k_hbm, k_ref), (v_hbm, v_ref), (o_hbm, o_ref),
                (wv_hbm, wv_ref), (wk_hbm, wk_ref),
                (gq_hbm, gq_ref), (gk_hbm, gk_ref),
            )
        )
    ]
    for copy in loads:
        copy.start()

    for row, ref in ((0, q_ref), (1, k_ref)):
        loads[row].wait()
        full_rows = ref[...].astype(F32)
        squares = full_rows * full_rows
        folded = squares[:, :HD]
        for h in range(1, N):
            folded = folded + squares[:, h * HD : (h + 1) * HD]
        gsp[i, row : row + 1, :] = row_sum(folded)
    for copy in loads[2:4]:
        copy.wait()

    pl.semaphore_wait(barrier, len(peers))

    for r in (2, 1, 3):
        send(gsp.at[i], gsp.at[i], G1, gdev(r), 3)
    rows_mine = pl.ds(pl.multiple_of(i * T, T), T)
    own = {}

    def exchange(n, src, dst):
        for r in (2, 1, 3):
            cols = pl.ds(pl.multiple_of(lax.rem(i + r, N) * HD, HD), HD)
            send(src.at[:, cols], dst.at[rows_mine, :], A2A + n, gdev(r), 0)
        cols = pl.ds(pl.multiple_of(i * HD, HD), HD)
        own[n] = pltpu.make_async_copy(src.at[:, cols], dst.at[rows_mine, :], loc.at[n])
        own[n].start()

    def arrived(n):
        landed(A2A + n, hv.at[0 : 3 * T, :])
        own[n].wait()

    exchange(0, v_ref, hv)
    exchange(1, k_ref, hk)

    exchange(2, q_ref, hq)
    exchange(3, o_ref, ho)

    landed(G1, gsp.at[0:3])
    for r in sorted(range(1, nz), key=lambda r: -min(r, nz - r)):
        send(gsp, zs.at[z], Z1, zdev(r), 0)
    for copy in loads[4:]:
        copy.wait()

    def unfold(dst):
        for n in range(KS):
            dst[:, n * HD : (n + 1) * HD] = fs[pl.ds(n, N * M, stride=KS), :].astype(BF16)

    def spread(mem, value, index):
        mem[j] = value.astype(BF16).reshape(N, M, HD)
        for r in (2, 1, 3):
            send(mem.at[j], mem.at[j], MEM + index, odev(r), 0)

    arrived(0)
    fs[...] = hv[...].astype(F32)
    unfold(vu)
    spread(mvg, dot_nn(vu[...], wv_ref[i]), 1)

    landed(Z1, zs.at[0 : nz - 1])
    gs[...] = gsp[...]
    for r in range(1, nz):
        gs[...] = gs[...] + zs[lax.rem(z + r, nz)]
    gain_q = gq_ref[i]
    gain_k = gk_ref[i]
    arrived(1)
    for a in range(N):
        rows = slice(a * T, (a + 1) * T)
        ick[rows, :] = as_column(lax.rsqrt(gs[a, 1:2, :] * (1.0 / hh) + EPS))
        normed = (hk[rows, :].astype(F32) * ick[rows, :] * gain_k).astype(BF16)
        kn[rows, :] = normed
        fs[rows, :] = normed.astype(F32)
    unfold(ku)
    spread(mkg, dot_nn(ku[...], wk_ref[i]), 0)

    for a in range(N):
        rows = slice(a * T, (a + 1) * T)
        icq[rows, :] = as_column(lax.rsqrt(gs[a, 0:1, :] * (1.0 / hh) + EPS))
        knt[a] = jnp.transpose(kn[rows, :])

    arrived(2)
    for a in range(N):
        rows = slice(a * T, (a + 1) * T)
        qn[rows, :] = (hq[rows, :].astype(F32) * icq[rows, :] * gain_q).astype(BF16)
    arrived(3)
    key_at = lax.broadcasted_iota(jnp.int32, (T, T), 0)
    query_at = lax.broadcasted_iota(jnp.int32, (T, T), 1)
    rate = scale * LOG2E

    def score(a, block, mask, keys, values):
        at = pl.ds(pl.multiple_of(block * T, T), T)
        rows = slice(a * T, (a + 1) * T)
        scores = dot_nt(keys, qn[rows, :])
        if mask is not None:
            scores = jnp.where(mask, scores, NEG)
        grads = dot_nt(values, ho[rows, :])
        peak = jnp.max(jnp.max(fold8(scores), 0), 0, keepdims=True)
        lifted = jnp.exp2((scores - peak) * rate)
        p_all[a, at, :] = lifted
        g_all[a, at, :] = grads
        m_all[a, block] = peak
        mass = jnp.sum(jnp.sum(fold8(lifted), 0), 0, keepdims=True)
        weighted = jnp.sum(jnp.sum(fold8(lifted * grads), 0), 0, keepdims=True)
        return peak, mass, weighted

    state = []
    for a in range(N):
        rows = slice(a * T, (a + 1) * T)
        state.append(score(a, 0, key_at <= query_at, kn[rows, :], hv[rows, :]))

    landed(MEM, mkg.at[0:3])
    landed(MEM + 1, mvg.at[0:3])
    for b in range(N):
        for t in range(N):
            at = slice(t * M, (t + 1) * M)
            mkc[b, at, :] = mkg[t, b]
            mvc[b, at, :] = mvg[t, b]
        mkt[b] = jnp.transpose(mkc[b])

    past = jnp.where(j > 0, 0, 1)

    for a in range(N):

        def absorb(b, current, a=a):
            old_peak, old_mass, old_weighted = current
            mask = None if isinstance(b, int) else key_at < j * M
            peak, mass, weighted = score(a, b + 1, mask, mkc[b], mvc[b])
            top = jnp.maximum(old_peak, peak)
            old_factor = jnp.exp2((old_peak - top) * rate)
            factor = jnp.exp2((peak - top) * rate)
            return (
                top,
                old_mass * old_factor + mass * factor,
                old_weighted * old_factor + weighted * factor,
            )

        current = state[a]
        for b in range(a):
            current = absorb(b, current)
        peak, mass, weighted = lax.fori_loop(a + past, a + 1, absorb, current)
        inverse_mass = 1.0 / mass
        fin[a, 0] = peak
        fin[a, 1] = inverse_mass
        fin[a, 2] = weighted * inverse_mass

    def settle(a, block):
        at = pl.ds(pl.multiple_of(block * T, T), T)
        factor = jnp.exp2((m_all[a, block] - fin[a, 0]) * rate) * fin[a, 1]
        attend = p_all[a, at, :] * factor
        d_scores = attend * (g_all[a, at, :] - fin[a, 2])
        return attend.astype(BF16), d_scores.astype(BF16)

    def homeward(src, dst, index, group=1):
        dst[i] = src[i]
        for r in (2, 1, 3):
            send(src.at[lax.rem(i + r, N)], dst.at[i], index, gdev(r), group)

    def norm_side(grad, raw, inv, gain):
        raw_full = raw.astype(F32)
        gained = grad * gain
        total = jnp.sum(fold8(grad * raw_full * inv), 0)
        return total, (gained * inv).astype(BF16), row_sum(gained * raw_full)

    last_parts = []
    for a in range(N):
        dqt[a] = jnp.zeros((HD, T), F32)
    for b in range(N - 1, -1, -1):
        after = range(b + 1, N)
        settled = [settle(a, b + 1) for a in after]
        for a, (_, d_scores) in zip(after, settled):
            part = dot_nn(mkt[b], d_scores)
            dqt[a] = dqt[a] + part
        if settled:
            rows = slice((b + 1) * T, N * T)
            acc_k[...] = dot_nn(jnp.concatenate([d for _, d in settled], 1), qn[rows, :])
            acc_v[...] = dot_nn(jnp.concatenate([p for p, _ in settled], 1), ho[rows, :])
        else:
            acc_k[...] = jnp.zeros((T, HD), F32)
            acc_v[...] = jnp.zeros((T, HD), F32)

        @pl.when(j > 0)
        def _(b=b):
            rows = slice(b * T, (b + 1) * T)
            attend, d_scores = settle(b, b + 1)
            acc_k[...] = acc_k[...] + dot_nn(d_scores, qn[rows, :])
            acc_v[...] = acc_v[...] + dot_nn(attend, ho[rows, :])
            dqt[b] = dqt[b] + dot_nn(mkt[b], d_scores)

        sbk[b] = (acc_k[...] * scale).astype(BF16).reshape(N, M, HD)
        sbv[b] = acc_v[...].astype(BF16).reshape(N, M, HD)
        for n, (sb, rb) in enumerate(((sbk, rbk), (sbv, rbv))):
            for r in (2, 1, 3):
                to = lax.rem(j + r, N)
                if b < N - 1:
                    send(sb.at[b, to], rb.at[j, b], DMEM + n, odev(r), 1)
                else:
                    index = 3 * n + r - 1
                    copy = remote(sb.at[b, to], rb.at[j, b], DMEM3 + index, odev(r), 4 + index)
                    pl.when(to < j)(copy.start)
                    last_parts.append((to < j, copy))

    gain_k_sum = jnp.zeros((8, HD), F32)
    for a in range(N):
        rows = slice(a * T, (a + 1) * T)
        attend, d_scores = settle(a, 0)
        dqt[a] = dqt[a] + dot_nn(knt[a], d_scores)
        grad_k = dot_nn(d_scores, qn[rows, :]) * scale
        av[a] = dot_nn(attend, ho[rows, :]).astype(BF16)
        total, ak[a], pd[a, 1:2, :] = norm_side(grad_k, hk[rows, :], ick[rows, :], gain_k)
        gain_k_sum = gain_k_sum + total
    homeward(av, avh, DV)
    homeward(ak, akh, DK)

    gain_q_sum = jnp.zeros((8, HD), F32)
    for a in range(N):
        rows = slice(a * T, (a + 1) * T)
        grad_q = jnp.transpose(dqt[a]) * scale
        total, aq[a], pd[a, 0:1, :] = norm_side(grad_q, hq[rows, :], icq[rows, :], gain_q)
        gain_q_sum = gain_q_sum + total

    homeward(pd, pdh, PD, 3)
    homeward(aq, aqh, DQ)

    for m in range(N):
        at = slice(m * M, (m + 1) * M)
        acc_k[at, :] = sbk[m, j].astype(F32)
        acc_v[at, :] = sbv[m, j].astype(F32)
    for n in range(2):
        landed(DMEM + n, hv.at[0 : 9 * M, :])
    for r in (1, 3, 2):
        source = lax.rem(j + N - r, N)
        for n, (rb, acc) in enumerate(((rbk, acc_k), (rbv, acc_v))):
            at = slice(0, (N - 1) * M)
            acc[at, :] = acc[at, :] + rb[source, 0 : N - 1].reshape((N - 1) * M, HD).astype(F32)

            @pl.when(source > j)
            def _(source=source, n=n, r=r, rb=rb, acc=acc):
                landed(DMEM3 + 3 * n + r - 1, rb.at[source, N - 1])
                at = slice((N - 1) * M, N * M)
                acc[at, :] = acc[at, :] + rb[source, N - 1].astype(F32)

    grad_mem_k = acc_k[...].astype(BF16)
    grad_mem_v = acc_v[...].astype(BF16)

    square_k = dot_tn(ku[...], grad_mem_k)
    square_v = dot_tn(vu[...], grad_mem_v)
    for p in range(N):
        pay[0, p] = square_k[p * HD : (p + 1) * HD].astype(BF16)
        pay[1, p] = square_v[p * HD : (p + 1) * HD].astype(BF16)
    gmk[...] = grad_mem_k.reshape(N, M, HD)
    gmv[...] = grad_mem_v.reshape(N, M, HD)

    for r in (2, 1, 3):
        to = lax.rem(j + r, N)
        send(pay.at[1 - c, to], rsi.at[1, j], RSX, cross(to), 2)
        send(pay.at[c, to], rsi.at[0, j], RS, odev(r), 2)
    send(pay.at[1 - c, j], rsi.at[1, j], RSX, cross(j), 2)
    homeward(gmk, gmkh, GM)
    homeward(gmv, gmvh, GM + 1)

    crossed = square_k[0:HD] * wk_ref[i, 0:HD, :].astype(F32)
    for p in range(1, N):
        at = slice(p * HD, (p + 1) * HD)
        crossed = crossed + square_k[at] * wk_ref[i, at, :].astype(F32)
    gmine[0:1, :] = jnp.sum(gain_q_sum, 0, keepdims=True)
    gmine[1:2, :] = jnp.sum(gain_k_sum, 0, keepdims=True) + row_sum(crossed) / gain_k
    for r in (1, 3, 2):
        send(gmine, gsame.at[j], GR, odev(r), 3)
    for p in range(N):
        send(gmine, gother.at[j], GRX, cross(p), 3)

    landed(RSX, rsi.at[1])
    landed(RS, rsi.at[0, 0:3])
    total = pay[c, j].astype(F32)
    for r in (1, 2, 3):
        total = total + rsi[0, lax.rem(j + r, N)].astype(F32)
    for p in range(N):
        total = total + rsi[1, p].astype(F32)
    full[c, far, near] = total.astype(BF16)
    mine = full.at[c, far, near]
    for n, r in ((2, 2), (0, 1), (1, 3)):
        send(mine, mine, AGG + n, ndev(r), 2)

    def pass_on(slot, member):
        piece = full.at[c, far, member]
        for r in (2, 1, 3):
            send(piece, piece, AGO + slot, fdev(r), 2)
        send(piece, piece, C2 + slot, cdev, 2)
        emit(c, far, member)

    pass_on(0, near)

    landed(GR, gsame.at[0:3])
    landed(GRX, gother)
    total = gmine[...]
    for r in (1, 2, 3):
        total = total + gsame[lax.rem(j + r, N)]
    for p in range(N):
        total = total + gother[p]
    gall[i] = total
    for r in (1, 3, 2):
        send(gall.at[i], gall.at[i], GG, gdev(r), 3)

    def forward(n, r):
        landed(AGG + n, mine)
        pass_on(n + 1, lax.rem(near + N - r, N))

    forward(0, 1)
    forward(1, 3)

    landed(GM, gmkh.at[0:3])
    landed(GM + 1, gmvh.at[0:3])
    product = jnp.zeros((T, HD), F32)
    for h in range(N):
        spread_k = dot_nt(gmkh[h], wk_ref[h])
        spread_v = dot_nt(gmvh[h], wv_ref[h])
        for n in range(KS):
            at = pl.ds(n, M, stride=KS)
            cols = slice(n * HD, (n + 1) * HD)
            bkf[h, at, :] = spread_k[:, cols]
            bvf[h, at, :] = spread_v[:, cols]
        gained = bkf[h] * gk_ref[h]
        bkf[h] = gained
        product = product + gained * k_ref[:, h * HD : (h + 1) * HD].astype(F32)

    landed(PD, pdh.at[0:3])
    total = pdh[0]
    for h in range(1, N):
        total = total + pdh[h]
    zs2[z, 0:1, :] = total[0:1]
    zs2[z, 1:2, :] = total[1:2] + row_sum(product)
    for r in sorted(range(1, nz), key=lambda r: -min(r, nz - r)):
        send(zs2.at[z], zs2.at[z], Z2, zdev(r), 3)

    forward(2, 2)

    for slot, back in enumerate((0, 1, 3, 2)):
        landed(AGO + slot, full.at[c, 0:3, 0])
        member = lax.rem(near + N - back, N)
        for r in (1, 3, 2):
            at = full.at[c, lax.rem(far + N - r, N), member]
            send(at, at, C2 + 4 + slot, cdev, 2)
        for r in (1, 3, 2):
            emit(c, lax.rem(far + N - r, N), member)
        landed(C2 + slot, mine)
        emit(1 - c, near, lax.rem(far + N - back, N))

    landed(Z2, zs2.at[0 : nz - 1])
    total = zs2[0]
    for r in range(1, nz):
        total = total + zs2[r]
    inverse = lax.rsqrt(gs[i] * (1.0 / hh) + EPS)
    shift = inverse * inverse * inverse * total * (1.0 / hh)
    shift_q = as_column(shift[0:1])
    shift_k = as_column(shift[1:2])
    for index in (DQ, DK, DV):
        landed(index, aqh.at[0:3])
    inverse_k = as_column(inverse[1:2])
    for h in range(N):
        cols = slice(h * HD, (h + 1) * HD)
        dq_out[:, cols] = (aqh[h].astype(F32) - q_ref[:, cols].astype(F32) * shift_q).astype(BF16)
        grad_k = akh[h].astype(F32) + bkf[h] * inverse_k
        dk_out[:, cols] = (grad_k - k_ref[:, cols].astype(F32) * shift_k).astype(BF16)
        dv_out[:, cols] = (avh[h].astype(F32) + bvf[h]).astype(BF16)
    landed(GG, gall.at[0:3])
    for h in range(N):
        gain_out[0, h] = gall[h, 0:1, :]
        gain_out[1, h] = gall[h, 1:2, :]

    for slot, back in enumerate((0, 1, 3, 2)):
        landed(C2 + 4 + slot, full.at[c, 0:3, 0])
        for r in (1, 3, 2):
            emit(1 - c, lax.rem(near + N - r, N), lax.rem(far + N - back, N))

    for group, size in enumerate(sent):
        if group < 3:
            rows = size // (4 * T)
            assert rows * 4 * T == size and rows % 8 == 0
            space = p_all.at[0, 0:rows, :]
        else:
            assert size == tally.shape[0] * 8 * T
            space = tally
        remote(space, space, 0, cdev, group).wait_send()
    for needed, copy in last_parts:
        pl.when(needed)(copy.wait_send)


def finish(
    dq_ref, dk_ref, dv_ref, kern_ref, gain_ref,
    dq_out, dk_out, dv_out, qg_out, kg_out, sk_out, sv_out,
    sems,
):
    pairs = [(kern_ref.at[0, h], sk_out.at[h]) for h in range(N)]
    pairs += [(kern_ref.at[1, h], sv_out.at[h]) for h in range(N)]
    pairs += [(dq_ref, dq_out), (dk_ref, dk_out), (dv_ref, dv_out)]
    pairs += [(gain_ref.at[0], qg_out), (gain_ref.at[1], kg_out)]
    copies = [pltpu.make_async_copy(src, dst, sems.at[n]) for n, (src, dst) in enumerate(pairs)]
    for copy in copies:
        copy.start()
    for copy in copies:
        copy.wait()


def on_device(nz, q, k, v, query_gain, key_gain, key_squeeze, value_squeeze, o):
    width = N * HD
    bf = functools.partial(pltpu.VMEM, dtype=BF16)
    ff = functools.partial(pltpu.VMEM, dtype=F32)
    rows = N * T
    deep = (N + 1) * T
    scratch = [ff((N, 1, HD))] * 2
    scratch += [bf((T, width))] * 4 + [bf((N, KS * HD, HD))] * 2
    scratch += [bf((rows, HD))] * 4 + [bf((rows, HD))] * 2 + [ff((rows, HD))] * 2
    scratch += [ff((rows, HD)), bf((N * M, KS * HD)), bf((N * M, KS * HD))]
    scratch += [ff((N, 2, T)), ff((nz, N, 2, T)), ff((N, 2, T))]
    scratch += [bf((N, N, M, HD))] * 2 + [bf((N, N * M, HD))] * 2
    scratch += [ff((N, deep, T))] * 2 + [ff((N, N + 1, 1, T)), ff((N, 3, 1, T))]
    scratch += [bf((N, HD, T))] * 2 + [ff((N, HD, T))]
    scratch += [ff((N * M, HD))] * 2 + [bf((N, N, M, HD))] * 4
    scratch += [bf((N, T, HD))] * 3 + [ff((N, 2, T))]
    scratch += [bf((N, T, HD))] * 3 + [ff((N, 2, T)), ff((nz, 2, T))]
    scratch += [bf((N, M, HD))] * 4 + [ff((N, T, HD))] * 2
    scratch += [ff((2, HD))] + [ff((N, 2, HD))] * 3
    scratch += [bf((2, N, HD, HD))] * 2 + [bf((2, N, N, HD, HD))]
    scratch += [ff((18, 2, T))]
    scratch += [
        pltpu.SemaphoreType.DMA((N_SEND,)),
        pltpu.SemaphoreType.DMA((N_RECV,)),
        pltpu.SemaphoreType.DMA((12,)),
    ]
    vmem = pl.BlockSpec(memory_space=pltpu.VMEM)
    anywhere = pl.BlockSpec(memory_space=pl.ANY)
    hbm = pl.BlockSpec(memory_space=pltpu.MemorySpace.HBM)
    stay = functools.partial(
        pltpu.with_memory_space_constraint, memory_space=pltpu.MemorySpace.HBM
    )
    grads = [jax.ShapeDtypeStruct((T, width), BF16)] * 3
    outs = pl.pallas_call(
        functools.partial(kernel, nz),
        out_shape=grads
        + [
            jax.ShapeDtypeStruct((2, N, KS * HD, HD), F32),
            jax.ShapeDtypeStruct((2, N, 1, HD), F32),
        ],
        in_specs=[hbm] * 8,
        out_specs=[vmem] * 5,
        scratch_shapes=scratch,
        compiler_params=pltpu.CompilerParams(
            collective_id=0, has_side_effects=True, vmem_limit_bytes=40 * 2**20
        ),
    )(
        stay(q[0]), stay(k[0]), stay(v[0]), stay(o[0]),
        stay(query_gain.reshape(N, 1, HD)), stay(key_gain.reshape(N, 1, HD)),
        stay(key_squeeze), stay(value_squeeze),
    )
    kernels = jax.ShapeDtypeStruct((N, KS * HD, HD), F32)
    gains = jax.ShapeDtypeStruct((N, 1, HD), F32)
    dq, dk, dv, qg, kg, sk, sv = pl.pallas_call(
        finish,
        out_shape=grads + [gains] * 2 + [kernels] * 2,
        in_specs=[anywhere] * 5,
        out_specs=[hbm] * 7,
        scratch_shapes=[pltpu.SemaphoreType.DMA((13,))],
        compiler_params=pltpu.CompilerParams(vmem_limit_bytes=16 * 2**20),
    )(*outs)
    return dq[None], dk[None], dv[None], qg.reshape(width), kg.reshape(width), sk, sv


def solution(mesh):
    by_token = P("dp", "seq", "head")
    by_head = P("head", None, None)
    return jax.shard_map(
        functools.partial(on_device, mesh.shape["head"]),
        mesh=mesh,
        in_specs=(by_token,) * 3 + (P("head"), P("head"), by_head, by_head, by_token),
        out_specs=(by_token,) * 3 + (P("head"), P("head"), by_head, by_head),
        check_vma=False,
    )
```
